256 devices in a mesh: head: 8 (over y, core), seq: 32 (over z, x).
Axes of the slice: x: 4, y: 4, z: 8, core: 2. Of those that a mesh axis runs over, the one named last changes fastest.
Arguments:
- queries: bfloat16 [2, 8, 256, 128], P(None, None, ('head', 'seq')), may hold values from -16 to 16
- keys: bfloat16 [2, 8, 65536, 128], P(None, 'head', 'seq'), may hold values from -6 to 6
- values: bfloat16 [2, 8, 65536, 128], P(None, 'head', 'seq'), may hold values from -6 to 6
- indices: int32 [8, 8, 1024], P('head'), may hold values from 0 to 65535, as said below
- sizes: int32 [8, 8], P('head'), may hold values from 128 to 1024, as said below
- owners: int32 [8, 8], P('head'), may hold values from 0 to 31, as said below
Outputs:
- compact_values: bfloat16 [8, 96, 1024, 128], P('head', 'seq')
The draws below stay inside these ranges and needn't reach their ends.
Inputs may be any that keep to these rules, and one draw needn't show every extreme that they name: `indices`: in each row of a head and fit, the 1024 positions are distinct and the first two are 0 and 1; only the first sizes[h,f] are used. `sizes`: multiples of 128; in each head one fit has 1024. `owners`: no index owns more than 3 fits of a head; in each head one index owns exactly 3.
All inputs are finite; a program needn't handle non-finite values.
Results may differ from the reference program's by a relative error of at most 0.008.
Values may be sent and summed in bfloat16 or wider, within the bound.
No kernel may reach another device: no remote copies, remote signals or barrier semaphores. Data moves between devices by JAX's collectives and lax.ppermute only.
A program may use at most 128 MiB of HBM per device.

```python
import jax
import jax.numpy as jnp
from jax import lax

HD = 128
LAYERS = 2
FITS_LAYER = 4
CMAX = 1024
SLOTS = 3
KVH = 8
SEQ_LEN = 65536
QUERIES = 256
FITS = 8
STEP = 128
N_SEQ = 32


def draw_keys(key, part):
    base = jax.random.normal(jax.random.fold_in(key, 1), (LAYERS, KVH, SEQ_LEN, HD), jnp.float32)
    return jnp.clip(base, -6.0, 6.0).astype(jnp.bfloat16)


def draw_queries(key, part):
    base = 2.5 * jax.random.normal(jax.random.fold_in(key, 3), (LAYERS, KVH, QUERIES, HD), jnp.float32)
    return jnp.clip(base, -16.0, 16.0).astype(jnp.bfloat16)


def draw_indices(key, part):
    streams = jax.random.split(jax.random.fold_in(key, 6), KVH * FITS)
    picked = jax.vmap(lambda one: jax.random.permutation(one, SEQ_LEN - 2)[:CMAX - 2] + 2)(streams)
    lead = jnp.broadcast_to(jnp.array([0, 1], jnp.int32), (KVH * FITS, 2))
    return jnp.concatenate([lead, picked.astype(jnp.int32)], axis=1).reshape(KVH, FITS, CMAX)


def draw_sizes(key, part):
    units = jax.random.randint(jax.random.fold_in(key, 7), (KVH, FITS), 1, 9)
    chosen = jax.random.randint(jax.random.fold_in(key, 8), (KVH, 1), 0, FITS)
    units = jnp.where(jnp.arange(FITS)[None, :] == chosen, 8, units)
    return (units * STEP).astype(jnp.int32)


def owner_row(one):
    busy = jax.random.randint(jax.random.fold_in(one, 1), (), 0, N_SEQ)
    rest = jax.random.permutation(jax.random.fold_in(one, 2), N_SEQ - 1)
    rest = jnp.where(rest >= busy, rest + 1, rest)[:FITS - SLOTS]
    listed = jnp.concatenate([jnp.full((SLOTS,), busy), rest])
    order = jax.random.permutation(jax.random.fold_in(one, 3), FITS)
    return listed[order].astype(jnp.int32)


def draw_owners(key, part):
    streams = jax.random.split(jax.random.fold_in(key, 9), KVH)
    return jax.vmap(owner_row)(streams)


def levels(own_key, extent, shards, low, top_value):
    level, own = 1.0, jax.random.fold_in(own_key, 6)
    for position, shards_of in shards:
        draws = jnp.exp(jax.random.uniform(jax.random.fold_in(own, position), (shards_of,), jnp.float32, low / len(shards), top_value / len(shards)))
        level = level * jnp.repeat(draws, extent[position] // shards_of).reshape([-1 if axis == position else 1 for axis in range(len(extent))])
    return level


def noise(own_key, shape, scale, limit, cuts=(), kind=jnp.bfloat16):
    entries = scale * jax.random.normal(own_key, shape, jnp.float32)
    if cuts:
        entries = entries * levels(own_key, shape, cuts, -0.22, 0.18)
    return jnp.clip(entries, -limit, limit).astype(kind)


def setup_inputs(seed: int = 0) -> dict:
    splits = jax.random.split(jax.random.key(seed), 7)
    queries = draw_queries(jax.random.fold_in(splits[6], 71), 0)
    keys = draw_keys(jax.random.fold_in(splits[6], 71), 0)
    values = noise(splits[2], (LAYERS, KVH, SEQ_LEN, HD), 1.0, 6.0, ((1, 8), (2, 32)))
    indices = draw_indices(jax.random.fold_in(splits[6], 71), 0)
    sizes = draw_sizes(jax.random.fold_in(splits[6], 71), 0)
    owners = draw_owners(jax.random.fold_in(splits[6], 71), 0)
    return {"queries": queries, "keys": keys, "values": values, "indices": indices, "sizes": sizes, "owners": owners}


RIDGE = 0.3

def solve_fit(query_rows, target_rows, compact, size):
    scale = query_rows.shape[-1] ** (-0.5)
    width = compact.shape[0]
    scores = lax.dot_general(query_rows.astype(jnp.float32), compact.astype(jnp.float32), (((1,), (1,)), ((), ())), preferred_element_type=jnp.float32) * scale
    live = jnp.arange(width, dtype=jnp.int32) < size
    scores = jnp.where(live[None, :], scores, -jnp.inf)
    peak = jnp.max(scores, axis=1)
    expo = jnp.exp(scores - peak[:, None])
    probs = (expo / jnp.sum(expo, axis=1)[:, None]).astype(jnp.bfloat16)
    gram = lax.dot_general(probs.astype(jnp.float32), probs.astype(jnp.float32), (((0,), (0,)), ((), ())), preferred_element_type=jnp.float32)
    rhs = lax.dot_general(probs.astype(jnp.float32), target_rows.astype(jnp.float32), (((0,), (0,)), ((), ())), preferred_element_type=jnp.float32)
    ridge = RIDGE * jnp.trace(gram) / size.astype(jnp.float32)
    system = gram + jnp.diag(jnp.where(live, ridge, jnp.float32(1.0)))
    factor = jnp.linalg.cholesky(system)
    solution = jax.scipy.linalg.cho_solve((factor, True), rhs)
    return solution.astype(jnp.bfloat16)

def attend(query_rows, key_rows, value_rows):
    scale = query_rows.shape[-1] ** (-0.5)
    scores = jnp.dot(query_rows.astype(jnp.float32), key_rows.astype(jnp.float32).T.astype(jnp.float32), preferred_element_type=jnp.float32) * scale
    peak = jnp.max(scores, axis=1)
    weights = jnp.exp(scores - peak[:, None])
    total = jnp.sum(weights, axis=1)
    rounded = lax.optimization_barrier(weights.astype(jnp.bfloat16))
    numer = jnp.dot(rounded.astype(jnp.float32), value_rows.astype(jnp.float32), preferred_element_type=jnp.float32)
    return (numer / total[:, None]).astype(jnp.bfloat16)

def reference(queries, keys, values, indices, sizes, owners):
    layers, heads = (keys.shape[0], keys.shape[1])
    width = keys.shape[3]
    flat_q = queries.reshape(layers * heads, QUERIES, width)
    flat_k = keys.reshape(layers * heads, SEQ_LEN, width)
    flat_v = values.reshape(layers * heads, SEQ_LEN, width)
    targets = lax.map(lambda group: attend(group[0], group[1], group[2]), (flat_q, flat_k, flat_v))
    targets = targets.reshape(layers, heads, QUERIES, width)
    head_ids = jnp.repeat(jnp.arange(heads, dtype=jnp.int32), FITS)
    fit_list = jnp.tile(jnp.arange(FITS, dtype=jnp.int32), heads)

    def one_fit(pair):
        head, fit = pair
        layer = fit // FITS_LAYER
        compact = jnp.take(keys[layer, head], indices[head, fit], axis=0)
        return solve_fit(queries[layer, head], targets[layer, head], compact, sizes[head, fit])
    solutions = lax.map(one_fit, (head_ids, fit_list)).reshape(heads, FITS, CMAX, width)
    fit_ids = jnp.arange(FITS, dtype=jnp.int32)
    same = owners[:, :, None] == owners[:, None, :]
    before = fit_ids[:, None] > fit_ids[None, :]
    earlier = jnp.sum((same & before[None]).astype(jnp.int32), axis=2)
    slot = (owners * SLOTS + earlier).astype(jnp.int32)
    result = jnp.zeros((heads, N_SEQ * SLOTS, CMAX, width), jnp.bfloat16)
    return result.at[jnp.arange(heads, dtype=jnp.int32)[:, None], slot].set(solutions)
```

```python
import jax
import jax.numpy as jnp
from jax import lax
from jax.experimental import pallas as pl
from jax.experimental.pallas import tpu as pltpu
from jax.sharding import Mesh
from jax.sharding import PartitionSpec as P

FITS = 8
FITS_LAYER = 4
SLOTS = 3
CMAX = 1024
HD = 128
LANES = 128
ROOM = 128
ROWS = ROOM + 16
STEPS = 8
RIDGE = 0.3
SCALE = HD ** (-0.5)
SEQ = ("seq_0", "seq_1")
HEAD_SEQ = ("head", "seq_0", "seq_1")
F32 = jnp.float32
BF16 = jnp.bfloat16
PARAMS = pltpu.CompilerParams(vmem_limit_bytes=56 << 20)
SMEM = pl.BlockSpec(memory_space=pltpu.SMEM)
VMEM = pl.BlockSpec(memory_space=pltpu.VMEM)


def cost(flops, moved, exps=0):
    return pl.CostEstimate(flops=flops, transcendentals=exps, bytes_accessed=moved)


def iota(shape, dim):
    return lax.broadcasted_iota(jnp.int32, shape, dim)


def fiota(shape, dim):
    return iota(shape, dim).astype(F32)


def dot(a, b, dims=((1,), (0,))):
    return lax.dot_general(a, b, (dims, ((), ())), preferred_element_type=F32)


def running(mask):
    rows, width = mask.shape
    blocks = width // LANES
    upper = (iota((LANES, LANES), 0) <= iota((LANES, LANES), 1)).astype(BF16)
    stacked = jnp.concatenate(
        [mask[:, b * LANES : (b + 1) * LANES] for b in range(blocks)], axis=0
    )
    inner = dot(stacked.astype(BF16), upper)
    carry = jnp.zeros((rows, 1), F32)
    parts = []
    for b in range(blocks):
        part = inner[b * rows : (b + 1) * rows]
        parts.append(part + carry)
        carry = carry + part[:, LANES - 1 : LANES]
    return jnp.concatenate(parts, axis=1), carry


def send_kernel(shards, me_ref, own_ref, size_ref, idx_ref, keys_ref, send_ref, flag_ref):
    me = me_ref[0]
    local = keys_ref.shape[1]
    shift = local.bit_length() - 1
    fits, width = idx_ref.shape
    idx = idx_ref[...]
    row = iota((fits, width), 0)
    lane = iota((fits, width), 1)
    size = jnp.zeros((fits, width), jnp.int32)
    own = jnp.zeros((fits, LANES), jnp.int32)
    row1 = iota((fits, LANES), 0)
    lane1 = iota((fits, LANES), 1)
    for f in range(fits):
        size = jnp.where(row == f, size_ref[0, f], size)
        own = jnp.where(row1 == f, own_ref[0, f], own)
    shard = jnp.where(lane < size, lax.shift_right_logical(idx, shift), -1)
    counts = jnp.zeros((fits, LANES), F32)
    for s in range(shards):
        count = jnp.sum(jnp.where(shard == s, 1.0, 0.0), axis=1, keepdims=True)
        counts = jnp.where(lane1 == s, count, counts)
    total = jnp.zeros((fits, LANES), F32)
    before = jnp.zeros((fits, LANES), F32)
    for f in range(fits):
        shared = jnp.where(own == own_ref[0, f], counts[f : f + 1, :], 0.0)
        total = total + shared
        before = before + jnp.where(row1 > f, shared, 0.0)
    flag_ref[0] = (jnp.max(total) > ROOM).astype(jnp.int32)
    first = jnp.sum(jnp.where(lane1 == me, before, 0.0), axis=1, keepdims=True)
    mine = shard == me
    held = jnp.where(mine, 1.0, 0.0)
    place, _ = running(held)
    place = jnp.where(mine, place - 1.0 + first, -1.0)
    spot = jnp.where(mine, idx - me * local + 1, 0).astype(F32)
    send_ref[...] = jnp.zeros(send_ref.shape, BF16)
    slot = fiota((ROOM, width), 0)
    at = fiota((ROOM, local), 1)
    for f in range(fits):
        here = place[f : f + 1, :] == slot
        pos = jnp.sum(jnp.where(here, spot[f : f + 1, :], 0.0), axis=1, keepdims=True) - 1.0
        pick = jnp.where(pos == at, 1.0, 0.0).astype(BF16)
        rows = dot(pick, keys_ref[f // FITS_LAYER])
        to = own_ref[0, f]
        send_ref[to, 0:ROOM, :] += rows.T.astype(BF16)


def pack_keys(me, owners, sizes, indices, keys, shards):
    return pl.pallas_call(
        lambda *refs: send_kernel(shards, *refs),
        out_shape=(
            jax.ShapeDtypeStruct((shards, ROWS, LANES), BF16),
            jax.ShapeDtypeStruct((1,), jnp.int32),
        ),
        in_specs=[SMEM, SMEM, SMEM, VMEM, VMEM],
        out_specs=(VMEM, SMEM),
        compiler_params=PARAMS,
        cost_estimate=cost(10**9, 3 * 10**6),
        name="pack_keys",
    )(me, owners, sizes, indices, keys)


def slots_of(me, own_ref):
    found = [jnp.int32(-1)] * SLOTS
    seen = jnp.int32(0)
    for f in range(FITS):
        match = own_ref[0, f] == me
        for j in range(SLOTS):
            found[j] = jnp.where(match & (seen == j), f, found[j])
        seen = seen + match.astype(jnp.int32)
    return found


def order_kernel(shift, me_ref, own_ref, size_ref, idx_ref, recv_ref, out_ref):
    shards = recv_ref.shape[0]
    width = idx_ref.shape[1]
    chunk = 4
    fits = slots_of(me_ref[0], own_ref)
    first = jnp.zeros((shards, 1), F32)
    lane = iota((1, width), 1)
    source = iota((shards, width), 0)
    depth = fiota((chunk * ROOM, width), 0)
    for j in range(SLOTS):
        fit = jnp.maximum(fits[j], 0)
        size = jnp.where(fits[j] >= 0, size_ref[0, fit], 0)
        idx = idx_ref[pl.ds(fit, 1), :]
        shard = jnp.where(lane < size, lax.shift_right_logical(idx, shift), -1)
        held = jnp.where(shard == source, 1.0, 0.0)
        place, count = running(held)
        rank = jnp.sum(held * (place - 1.0 + first), axis=0, keepdims=True)
        first = first + count
        dest = jnp.where(shard >= 0, shard.astype(F32) * ROOM + rank, -1.0)

        @pl.when(fits[j] >= 0)
        def _():
            total = jnp.zeros((HD, width), F32)
            for s in range(0, shards, chunk):
                pick = jnp.where(dest - float(s * ROOM) == depth, 1.0, 0.0).astype(BF16)
                block = jnp.concatenate(
                    [recv_ref[s + i, 0:ROOM, :] for i in range(chunk)], axis=1
                )
                total = total + dot(block, pick)
            out_ref[j] = total.astype(BF16)


def order_keys(me, owners, sizes, indices, received, shift):
    return pl.pallas_call(
        lambda *refs: order_kernel(shift, *refs),
        out_shape=jax.ShapeDtypeStruct((SLOTS, HD, CMAX), BF16),
        in_specs=[SMEM, SMEM, SMEM, VMEM, VMEM],
        out_specs=VMEM,
        compiler_params=PARAMS,
        cost_estimate=cost(3 * 10**9, 2 * 10**6),
        name="order_keys",
    )(me, owners, sizes, indices, received)


def layer_rows(rows, layer):
    wide = rows.astype(F32)[:, 8 * layer : 8 * layer + 8, :]
    return wide.reshape(-1, wide.shape[-1])


def attend_kernel(recv_ref, keys_ref, values_ref, out_ref):
    shards = recv_ref.shape[0]
    outs, stats = [], []
    for layer in range(2):
        query = layer_rows(recv_ref[...], layer).astype(BF16)
        scores = dot(query, keys_ref[layer], ((1,), (1,))) * SCALE
        peak = jnp.max(scores, axis=1, keepdims=True)
        weights = jnp.exp(scores - peak)
        total = jnp.sum(weights, axis=1, keepdims=True)
        numer = dot(weights.astype(BF16), values_ref[layer])
        outs.append((numer / total).reshape(shards, 8, HD))
        level = peak + jnp.log(total)
        high = level.astype(BF16).astype(F32)
        middle = (level - high).astype(BF16).astype(F32)
        low = level - high - middle
        lane = iota((level.shape[0], LANES), 1)
        row = jnp.where(lane == 0, high, 0.0)
        row = jnp.where(lane == 1, middle, row)
        row = jnp.where(lane == 2, low, row)
        stats.append(row.reshape(shards, 8, LANES))
    out_ref[...] = jnp.concatenate(outs + stats, axis=1).astype(BF16)


def attend(received, keys, values):
    shards = received.shape[0]
    return pl.pallas_call(
        attend_kernel,
        out_shape=jax.ShapeDtypeStruct((shards, 32, LANES), BF16),
        grid=(1,),
        in_specs=[
            pl.BlockSpec((shards, 16, LANES), lambda i: (0, ROOM // 16, 0)),
            pl.BlockSpec(keys.shape, lambda i: (0, 0, 0)),
            pl.BlockSpec(values.shape, lambda i: (0, 0, 0)),
        ],
        out_specs=pl.BlockSpec((shards, 32, LANES), lambda i: (0, 0, 0)),
        compiler_params=PARAMS,
        cost_estimate=cost(5 * 10**8, 3 * 10**6, 10**6),
        name="attend",
    )(received, keys, values)


def join_kernel(parts_ref, out_ref):
    parts = parts_ref[...].astype(F32)
    level = jnp.sum(parts[:, 16:32, :], axis=2, keepdims=True)
    weights = jnp.exp(level - jnp.max(level, axis=0, keepdims=True))
    numer = jnp.sum(weights * parts[:, 0:16, :], axis=0, keepdims=True)
    target = numer / jnp.sum(weights, axis=0, keepdims=True)
    out_ref[...] = jnp.broadcast_to(target, out_ref.shape).astype(BF16)


def join(parts):
    shards = parts.shape[0]
    return pl.pallas_call(
        join_kernel,
        out_shape=jax.ShapeDtypeStruct((shards, 16, LANES), BF16),
        in_specs=[VMEM],
        out_specs=VMEM,
        compiler_params=PARAMS,
        cost_estimate=cost(10**6, 4 * 10**5, 10**3),
        name="join_parts",
    )(parts)


def system_kernel(me_ref, own_ref, size_ref, recv_ref, keys_ref, probs_ref, sys_ref, ends_ref):
    fits = slots_of(me_ref[0], own_ref)
    for j in range(SLOTS):
        count = recv_ref.shape[0] * 8
        eye = iota((count, count), 0) == iota((count, count), 1)

        @pl.when(fits[j] >= 0)
        def _():
            fit = jnp.maximum(fits[j], 0)
            size = size_ref[0, fit]
            second = (fit >= FITS_LAYER).astype(F32)
            rows = recv_ref[...]
            first_rows, second_rows = layer_rows(rows, 0), layer_rows(rows, 1)
            query = jnp.where(second > 0.5, second_rows, first_rows).astype(BF16)
            scores = dot(query, keys_ref[j]) * SCALE
            live = iota((1, scores.shape[1]), 1) < size
            scores = jnp.where(live, scores, -jnp.inf)
            expo = jnp.exp(scores - jnp.max(scores, axis=1, keepdims=True))
            probs = (expo / jnp.sum(expo, axis=1, keepdims=True)).astype(BF16)
            gram = dot(probs, probs, ((1,), (1,)))
            trace = jnp.sum(jnp.where(eye, gram, 0.0))
            ridge = RIDGE * trace / size.astype(F32)
            top = jnp.max(jnp.sum(gram, axis=1, keepdims=True))
            sys_ref[j] = gram + jnp.where(eye, ridge, 0.0)
            ends_ref[2 * j] = ridge
            ends_ref[2 * j + 1] = jnp.minimum(top, trace) + ridge
            probs_ref[j] = probs.astype(F32).T.astype(BF16)

        @pl.when(fits[j] < 0)
        def _():
            sys_ref[j] = jnp.where(eye, 1.0, 0.0)
            ends_ref[2 * j] = jnp.float32(1.0)
            ends_ref[2 * j + 1] = jnp.float32(1.0)


def systems(me, owners, sizes, received, compact):
    shards = received.shape[0]
    count = shards * 8
    return pl.pallas_call(
        system_kernel,
        out_shape=(
            jax.ShapeDtypeStruct((SLOTS, CMAX, count), BF16),
            jax.ShapeDtypeStruct((SLOTS, count, count), F32),
            jax.ShapeDtypeStruct((2 * SLOTS,), F32),
        ),
        grid=(1,),
        in_specs=[
            SMEM,
            SMEM,
            SMEM,
            pl.BlockSpec((shards, 16, LANES), lambda i: (0, ROOM // 16, 0)),
            pl.BlockSpec(compact.shape, lambda i: (0, 0, 0)),
        ],
        out_specs=(
            pl.BlockSpec((SLOTS, CMAX, count), lambda i: (0, 0, 0)),
            pl.BlockSpec((SLOTS, count, count), lambda i: (0, 0, 0)),
            SMEM,
        ),
        compiler_params=PARAMS,
        cost_estimate=cost(10**9, 3 * 10**6, 10**6),
        name="systems",
    )(me, owners, sizes, received, compact)


def split(x):
    high = x.astype(BF16)
    return high, (x - high.astype(F32)).astype(BF16)


def split3(x):
    high, _ = split(x)
    rest = x - high.astype(F32)
    middle, low = split(rest)
    return high, middle, low


def product(a, b):
    (a_high, a_low), (b_high, b_low) = a, b
    return dot(
        jnp.concatenate([a_high, a_high, a_low], axis=1),
        jnp.concatenate([b_high, b_low, b_high], axis=0),
    )


def product_full(a, b):
    (a0, a1, a2), (b0, b1, b2) = split3(a), split3(b)
    return dot(
        jnp.concatenate([a0, a0, a1, a0, a1, a2], axis=1),
        jnp.concatenate([b0, b1, b0, b2, b1, b0], axis=0),
    )


def invert_kernel(sys_ref, ends_ref, out_ref):
    count = sys_ref.shape[1]
    eye = iota((count, count), 0) == iota((count, count), 1)
    held, lows, highs = [], [], []
    for j in range(SLOTS):
        low, high = ends_ref[2 * j], ends_ref[2 * j + 1]
        middle = 2.0 / (low + high)
        held.append(middle * (jnp.where(eye, 2.0, 0.0) - middle * sys_ref[j]))
        ratio = (high - low) / (high + low)
        lows.append(1.0 - ratio * ratio)
    for step in range(STEPS):
        nexts = []
        for j in range(SLOTS):
            middle = 2.0 / (lows[j] + 1.0)
            if step < STEPS - 1:
                parts = split(held[j])
                images = product(split(sys_ref[j]), parts)
                rest = jnp.where(eye, 1.0, 0.0) - middle * images
                moved = product(parts, split(rest))
            else:
                images = product_full(sys_ref[j], held[j])
                rest = jnp.where(eye, 1.0, 0.0) - middle * images
                moved = product(split(held[j]), split(rest))
            nexts.append(middle * (held[j] + moved))
            ratio = (1.0 - lows[j]) / (1.0 + lows[j])
            lows[j] = 1.0 - ratio * ratio
        held = nexts
    for j in range(SLOTS):
        out_ref[j] = held[j]


def invert(system, ends):
    return pl.pallas_call(
        invert_kernel,
        out_shape=jax.ShapeDtypeStruct(system.shape, F32),
        in_specs=[VMEM, SMEM],
        out_specs=VMEM,
        compiler_params=PARAMS,
        cost_estimate=cost(5 * 10**9, 2 * 10**6),
        name="invert",
    )(system, ends)


def values_kernel(me_ref, own_ref, inverse_ref, probs_ref, target_ref, out_ref):
    fits = slots_of(me_ref[0], own_ref)
    for j in range(SLOTS):

        @pl.when(fits[j] >= 0)
        def _():
            rows = target_ref[...]
            first_rows, second_rows = layer_rows(rows, 0), layer_rows(rows, 1)
            second = (fits[j] >= FITS_LAYER).astype(F32)
            target = jnp.where(second > 0.5, second_rows, first_rows).astype(BF16)
            weights = dot(
                jnp.concatenate(split3(inverse_ref[j]), axis=1),
                jnp.concatenate([target] * 3, axis=0),
            )
            high, low = split(weights)
            probs = probs_ref[j]
            result = dot(
                jnp.concatenate([probs, probs], axis=1), jnp.concatenate([high, low], axis=0)
            )
            out_ref[0, j] = result.astype(BF16)

        @pl.when(fits[j] < 0)
        def _():
            out_ref[0, j] = jnp.zeros(out_ref.shape[2:], BF16)


def fitted_values(me, owners, inverse, probs, target):
    return pl.pallas_call(
        values_kernel,
        out_shape=jax.ShapeDtypeStruct((1, SLOTS, CMAX, HD), BF16),
        in_specs=[SMEM, SMEM, VMEM, VMEM, VMEM],
        out_specs=VMEM,
        compiler_params=PARAMS,
        cost_estimate=cost(10**9, 4 * 10**6),
        name="fitted_values",
    )(me, owners, inverse, probs, target)


def exchange(blocks):
    return lax.all_to_all(blocks, SEQ, split_axis=0, concat_axis=0, tiled=True)


def gathered_keys(me, owners, indices, keys):
    layers, local, width = keys.shape
    shards = lax.axis_size(SEQ)
    fits, count = indices.shape
    fit_ids = jnp.arange(fits, dtype=jnp.int32)
    offset = indices - me[0] * local
    inside = (offset >= 0) & (offset < local)
    source = (fit_ids // FITS_LAYER)[:, None] * local + jnp.clip(offset, 0, local - 1)
    picked = jnp.take(keys.reshape(layers * local, width), source, axis=0)
    found = jnp.where(inside[..., None], picked, jnp.zeros((), picked.dtype))
    parts = exchange(found.reshape(shards, -1, width))
    own_part = jnp.sum(parts.astype(F32), axis=0).astype(BF16)
    everything = exchange(jnp.broadcast_to(own_part, (shards, *own_part.shape)))
    everything = everything.reshape(fits, count, width)
    owned = owners[0]
    mine = owned == me[0]
    earlier = jnp.sum(jnp.where(mine[None, :] & (fit_ids[:, None] > fit_ids[None, :]), 1, 0), axis=1)
    chosen = [
        everything[jnp.sum(jnp.where(mine & (earlier == slot), fit_ids, 0))]
        for slot in range(SLOTS)
    ]
    return jnp.swapaxes(jnp.stack(chosen), 1, 2)


def on_device(queries, keys, values, indices, sizes, owners):
    layers, _, local, width = keys.shape
    key_rows = keys.reshape(layers, local, width)
    value_rows = values.reshape(layers, local, width)
    positions = indices[0]
    shards = lax.axis_size(SEQ)
    me = lax.axis_index(SEQ).astype(jnp.int32).reshape(1)
    regrouped = lax.all_to_all(queries, "head", split_axis=1, concat_axis=2, tiled=True)
    own_rows = regrouped.reshape(1, 16, width)
    packed, over = pack_keys(me, owners, sizes, positions, key_rows, shards)
    packed = lax.dynamic_update_slice(
        packed, jnp.broadcast_to(own_rows, (shards, 16, width)), (0, ROOM, 0)
    )
    received = exchange(packed)

    def finish(compact):
        parts = exchange(attend(received, key_rows, value_rows))
        probs, system, ends = systems(me, owners, sizes, received, compact())
        target = exchange(join(parts))
        inverse = invert(system, ends)
        return fitted_values(me, owners, inverse, probs, target)

    shift = local.bit_length() - 1
    return lax.cond(
        over[0] > 0,
        lambda: finish(lambda: gathered_keys(me, owners, positions, key_rows)),
        lambda: finish(lambda: order_keys(me, owners, sizes, positions, received, shift)),
    )


def solution(mesh):
    apart = Mesh(mesh.devices.reshape(mesh.shape["head"], 8, 4), ("head", "seq_0", "seq_1"))
    placed = (
        P(None, None, HEAD_SEQ, None),
        P(None, "head", SEQ, None),
        P(None, "head", SEQ, None),
        P("head", None, None),
        P("head", None),
        P("head", None),
    )
    return jax.shard_map(
        on_device,
        mesh=apart,
        in_specs=placed,
        out_specs=P("head", SEQ, None, None),
        check_vma=False,
    )
```

```python
import functools

import jax
import jax.numpy as jnp
from jax import lax
from jax.experimental import pallas as pl
from jax.experimental.pallas import tpu as pltpu
from jax.sharding import Mesh
from jax.sharding import PartitionSpec as P

FITS = 8
FITS_LAYER = 4
SLOTS = 3
CMAX = 1024
HD = 128
LANES = 128
ROOM = 128
ROWS = ROOM + 16
CLOSE = 0.999
RIDGE = 0.3
SCALE = HD ** (-0.5)
SEQ = ("seq_0", "seq_1")
HEAD_SEQ = ("head", "seq_0", "seq_1")
F32 = jnp.float32
BF16 = jnp.bfloat16


def room(mib):
    return pltpu.CompilerParams(vmem_limit_bytes=mib << 20)


SMEM = pl.BlockSpec(memory_space=pltpu.SMEM)
VMEM = pl.BlockSpec(memory_space=pltpu.VMEM)


def cost(flops, moved, exps=0):
    return pl.CostEstimate(flops=flops, transcendentals=exps, bytes_accessed=moved)


def iota(shape, dim):
    return lax.broadcasted_iota(jnp.int32, shape, dim)


def fiota(shape, dim):
    return iota(shape, dim).astype(F32)


def dot(a, b, dims=((1,), (0,))):
    return lax.dot_general(a, b, (dims, ((), ())), preferred_element_type=F32)


def running(mask):
    rows, width = mask.shape
    blocks = width // LANES
    upper = (iota((LANES, LANES), 0) <= iota((LANES, LANES), 1)).astype(BF16)
    stacked = jnp.concatenate(
        [mask[:, b * LANES : (b + 1) * LANES] for b in range(blocks)], axis=0
    )
    inner = dot(stacked.astype(BF16), upper)
    carry = jnp.zeros((rows, 1), F32)
    parts = []
    for b in range(blocks):
        part = inner[b * rows : (b + 1) * rows]
        parts.append(part + carry)
        carry = carry + part[:, LANES - 1 : LANES]
    return jnp.concatenate(parts, axis=1), carry


def send_kernel(shards, me_ref, own_ref, size_ref, idx_ref, keys_ref, send_ref, flag_ref):
    me = me_ref[0]
    local = keys_ref.shape[1]
    shift = local.bit_length() - 1
    fits, width = idx_ref.shape
    idx = idx_ref[...]
    row = iota((fits, width), 0)
    lane = iota((fits, width), 1)
    size = jnp.zeros((fits, width), jnp.int32)
    own = jnp.zeros((fits, LANES), jnp.int32)
    row1 = iota((fits, LANES), 0)
    lane1 = iota((fits, LANES), 1)
    for f in range(fits):
        size = jnp.where(row == f, size_ref[0, f], size)
        own = jnp.where(row1 == f, own_ref[0, f], own)
    shard = jnp.where(lane < size, lax.shift_right_logical(idx, shift), -1)
    counts = jnp.zeros((fits, LANES), F32)
    for s in range(shards):
        count = jnp.sum(jnp.where(shard == s, 1.0, 0.0), axis=1, keepdims=True)
        counts = jnp.where(lane1 == s, count, counts)
    total = jnp.zeros((fits, LANES), F32)
    before = jnp.zeros((fits, LANES), F32)
    for f in range(fits):
        shared = jnp.where(own == own_ref[0, f], counts[f : f + 1, :], 0.0)
        total = total + shared
        before = before + jnp.where(row1 > f, shared, 0.0)
    flag_ref[0] = (jnp.max(total) > ROOM).astype(jnp.int32)
    first = jnp.sum(jnp.where(lane1 == me, before, 0.0), axis=1, keepdims=True)
    mine = shard == me
    held = jnp.where(mine, 1.0, 0.0)
    place, _ = running(held)
    place = jnp.where(mine, place - 1.0 + first, -1.0)
    spot = jnp.where(mine, idx - me * local + 1, 0).astype(F32)
    send_ref[...] = jnp.zeros(send_ref.shape, BF16)
    slot = fiota((ROOM, width), 0)
    at = fiota((ROOM, local), 1)
    for f in range(fits):
        here = place[f : f + 1, :] == slot
        pos = jnp.sum(jnp.where(here, spot[f : f + 1, :], 0.0), axis=1, keepdims=True) - 1.0
        pick = jnp.where(pos == at, 1.0, 0.0).astype(BF16)
        rows = dot(pick, keys_ref[f // FITS_LAYER])
        to = own_ref[0, f]
        send_ref[to, 0:ROOM, :] += rows.T.astype(BF16)


def pack_keys(me, owners, sizes, indices, keys, shards):
    return pl.pallas_call(
        lambda *refs: send_kernel(shards, *refs),
        out_shape=(
            jax.ShapeDtypeStruct((shards, ROWS, LANES), BF16),
            jax.ShapeDtypeStruct((1,), jnp.int32),
        ),
        in_specs=[SMEM, SMEM, SMEM, VMEM, VMEM],
        out_specs=(VMEM, SMEM),
        compiler_params=room(24),
        cost_estimate=cost(10**9, 3 * 10**6),
        name="pack_keys",
    )(me, owners, sizes, indices, keys)


def slots_of(me, own_ref):
    found = [jnp.int32(-1)] * SLOTS
    seen = jnp.int32(0)
    for f in range(FITS):
        match = own_ref[0, f] == me
        for j in range(SLOTS):
            found[j] = jnp.where(match & (seen == j), f, found[j])
        seen = seen + match.astype(jnp.int32)
    return found


def layer_rows(rows, layer):
    wide = rows.astype(F32)[:, 8 * layer : 8 * layer + 8, :]
    return wide.reshape(-1, wide.shape[-1])


def attend_kernel(recv_ref, keys_ref, values_ref, after_ref, out_ref):
    shards = recv_ref.shape[0]
    outs, stats = [], []
    for layer in range(2):
        query = layer_rows(recv_ref[...], layer).astype(BF16)
        scores = dot(query, keys_ref[layer], ((1,), (1,))) * SCALE
        peak = jnp.max(scores, axis=1, keepdims=True)
        weights = jnp.exp(scores - peak)
        total = jnp.sum(weights, axis=1, keepdims=True)
        numer = dot(weights.astype(BF16), values_ref[layer])
        outs.append((numer / total).reshape(shards, 8, HD))
        level = peak + jnp.log(total)
        high = level.astype(BF16).astype(F32)
        middle = (level - high).astype(BF16).astype(F32)
        low = level - high - middle
        lane = iota((level.shape[0], LANES), 1)
        row = jnp.where(lane == 0, high, 0.0)
        row = jnp.where(lane == 1, middle, row)
        row = jnp.where(lane == 2, low, row)
        stats.append(row.reshape(shards, 8, LANES))
    out_ref[...] = jnp.concatenate(outs + stats, axis=1).astype(BF16)


def attend(received, keys, values, after):
    shards = received.shape[0]
    return pl.pallas_call(
        attend_kernel,
        out_shape=jax.ShapeDtypeStruct((shards, 32, LANES), BF16),
        grid=(1,),
        in_specs=[
            pl.BlockSpec((shards, 16, LANES), lambda i: (0, ROOM // 16, 0)),
            pl.BlockSpec(keys.shape, lambda i: (0, 0, 0)),
            pl.BlockSpec(values.shape, lambda i: (0, 0, 0)),
            pl.BlockSpec(memory_space=pl.ANY),
        ],
        out_specs=pl.BlockSpec((shards, 32, LANES), lambda i: (0, 0, 0)),
        compiler_params=room(24),
        cost_estimate=cost(5 * 10**8, 3 * 10**6, 10**6),
        name="attend",
    )(received, keys, values, after)


def join_kernel(parts_ref, out_ref):
    parts = parts_ref[...].astype(F32)
    level = jnp.sum(parts[:, 16:32, :], axis=2, keepdims=True)
    weights = jnp.exp(level - jnp.max(level, axis=0, keepdims=True))
    numer = jnp.sum(weights * parts[:, 0:16, :], axis=0, keepdims=True)
    target = numer / jnp.sum(weights, axis=0, keepdims=True)
    out_ref[...] = jnp.broadcast_to(target, out_ref.shape).astype(BF16)


def join(parts):
    shards = parts.shape[0]
    return pl.pallas_call(
        join_kernel,
        out_shape=jax.ShapeDtypeStruct((shards, 16, LANES), BF16),
        in_specs=[VMEM],
        out_specs=VMEM,
        compiler_params=room(8),
        cost_estimate=cost(10**6, 4 * 10**5, 10**3),
        name="join_parts",
    )(parts)


def system_kernel(
    shift, me_ref, own_ref, size_ref, over_ref, idx_ref, recv_ref, spare_ref, probs_ref, sys_ref, ends_ref, keys_ref
):
    shards = recv_ref.shape[0]
    width = idx_ref.shape[1]
    chunk = 4
    count = shards * 8
    eye = iota((count, count), 0) == iota((count, count), 1)
    fits = slots_of(me_ref[0], own_ref)
    first = jnp.zeros((shards, 1), F32)
    lane = iota((1, width), 1)
    source = iota((shards, width), 0)
    depth = fiota((chunk * ROOM, width), 0)
    for j in range(SLOTS):
        fit = jnp.maximum(fits[j], 0)
        size = jnp.where(fits[j] >= 0, size_ref[0, fit], 0)
        idx = idx_ref[pl.ds(fit, 1), :]
        shard = jnp.where(lane < size, lax.shift_right_logical(idx, shift), -1)
        held = jnp.where(shard == source, 1.0, 0.0)
        place, number = running(held)
        rank = jnp.sum(held * (place - 1.0 + first), axis=0, keepdims=True)
        first = first + number
        dest = jnp.where(shard >= 0, shard.astype(F32) * ROOM + rank, -1.0)

        @pl.when(fits[j] >= 0)
        def _():
            @pl.when(over_ref[0] == 0)
            def _():
                total = jnp.zeros((HD, width), F32)
                for s in range(0, shards, chunk):
                    pick = jnp.where(dest - float(s * ROOM) == depth, 1.0, 0.0).astype(BF16)
                    block = jnp.concatenate(
                        [recv_ref[s + i, 0:ROOM, :] for i in range(chunk)], axis=1
                    )
                    total = total + dot(block, pick)
                keys_ref[...] = total.astype(BF16)

            @pl.when(over_ref[0] > 0)
            def _():
                pltpu.sync_copy(spare_ref.at[j], keys_ref)

            rows = recv_ref[:, ROOM:ROWS, :]
            second = (fit >= FITS_LAYER).astype(F32)
            query = jnp.where(second > 0.5, layer_rows(rows, 1), layer_rows(rows, 0)).astype(BF16)
            scores = dot(query, keys_ref[...]) * SCALE
            scores = jnp.where(lane < size, scores, -jnp.inf)
            expo = jnp.exp(scores - jnp.max(scores, axis=1, keepdims=True))
            probs = (expo / jnp.sum(expo, axis=1, keepdims=True)).astype(BF16)
            gram = dot(probs, probs, ((1,), (1,)))
            trace = jnp.sum(jnp.where(eye, gram, 0.0))
            ridge = RIDGE * trace / size.astype(F32)
            top = jnp.max(jnp.sum(gram, axis=1, keepdims=True))
            sys_ref[j] = gram + jnp.where(eye, ridge, 0.0)
            ends_ref[2 * j] = ridge
            ends_ref[2 * j + 1] = jnp.minimum(top, trace) + ridge
            probs_ref[j] = probs.astype(F32).T.astype(BF16)

        @pl.when(fits[j] < 0)
        def _():
            sys_ref[j] = jnp.where(eye, 1.0, 0.0)
            ends_ref[2 * j] = jnp.float32(1.0)
            ends_ref[2 * j + 1] = jnp.float32(1.0)


def systems(me, owners, sizes, over, indices, received, spare, shift):
    count = received.shape[0] * 8
    return pl.pallas_call(
        lambda *refs: system_kernel(shift, *refs),
        out_shape=(
            jax.ShapeDtypeStruct((SLOTS, CMAX, count), BF16),
            jax.ShapeDtypeStruct((SLOTS, count, count), F32),
            jax.ShapeDtypeStruct((2 * SLOTS,), F32),
        ),
        in_specs=[SMEM, SMEM, SMEM, SMEM, VMEM, VMEM, pl.BlockSpec(memory_space=pl.ANY)],
        out_specs=(VMEM, VMEM, SMEM),
        scratch_shapes=[pltpu.VMEM((HD, CMAX), BF16)],
        compiler_params=room(24),
        cost_estimate=cost(4 * 10**9, 5 * 10**6, 10**6),
        name="systems",
    )(me, owners, sizes, over, indices, received, spare)


def split(x):
    high = x.astype(BF16)
    return high, (x - high.astype(F32)).astype(BF16)


def split3(x):
    high, _ = split(x)
    rest = x - high.astype(F32)
    middle, low = split(rest)
    return high, middle, low


def product(a, b):
    (a_high, a_low), (b_high, b_low) = a, b
    return dot(
        jnp.concatenate([a_high, a_high, a_low], axis=1),
        jnp.concatenate([b_high, b_low, b_high], axis=0),
    )


def product_full(a, b):
    (a0, a1, a2), (b0, b1, b2) = split3(a), split3(b)
    return dot(
        jnp.concatenate([a0, a0, a1, a0, a1, a2], axis=1),
        jnp.concatenate([b0, b1, b0, b2, b1, b0], axis=0),
    )


def invert_kernel(sys_ref, ends_ref, out_ref, parts_ref):
    count = sys_ref.shape[1]
    eye = iota((count, count), 0) == iota((count, count), 1)
    lows = []
    for j in range(SLOTS):
        low, high = ends_ref[2 * j], ends_ref[2 * j + 1]
        middle = 2.0 / (low + high)
        out_ref[j] = middle * (jnp.where(eye, 2.0, 0.0) - middle * sys_ref[j])
        parts_ref[j, 0], parts_ref[j, 1] = split(sys_ref[j])
        ratio = (high - low) / (high + low)
        lows.append(1.0 - ratio * ratio)

    def step(lows, full):
        nexts = []
        for j in range(SLOTS):
            held = out_ref[j]
            middle = 2.0 / (lows[j] + 1.0)
            parts = split(held)
            if full:
                images = product_full(sys_ref[j], held)
            else:
                images = product((parts_ref[j, 0], parts_ref[j, 1]), parts)
            rest = jnp.where(eye, 1.0, 0.0) - middle * images
            out_ref[j] = middle * (held + product(parts, split(rest)))
            ratio = (1.0 - lows[j]) / (1.0 + lows[j])
            nexts.append(1.0 - ratio * ratio)
        return tuple(nexts)

    lows = lax.while_loop(
        lambda lows: functools.reduce(jnp.minimum, lows) < CLOSE,
        lambda lows: step(lows, False),
        tuple(lows),
    )
    step(lows, True)


def invert(system, ends):
    return pl.pallas_call(
        invert_kernel,
        out_shape=jax.ShapeDtypeStruct(system.shape, F32),
        in_specs=[VMEM, SMEM],
        out_specs=VMEM,
        scratch_shapes=[pltpu.VMEM((SLOTS, 2, *system.shape[1:]), BF16)],
        compiler_params=room(16),
        cost_estimate=cost(5 * 10**9, 2 * 10**6),
        name="invert",
    )(system, ends)


def values_kernel(me_ref, own_ref, inverse_ref, probs_ref, target_ref, out_ref):
    fits = slots_of(me_ref[0], own_ref)
    for j in range(SLOTS):

        @pl.when(fits[j] >= 0)
        def _():
            rows = target_ref[...]
            first_rows, second_rows = layer_rows(rows, 0), layer_rows(rows, 1)
            second = (fits[j] >= FITS_LAYER).astype(F32)
            target = jnp.where(second > 0.5, second_rows, first_rows).astype(BF16)
            weights = dot(
                jnp.concatenate(split3(inverse_ref[j]), axis=1),
                jnp.concatenate([target] * 3, axis=0),
            )
            high, low = split(weights)
            probs = probs_ref[j]
            result = dot(
                jnp.concatenate([probs, probs], axis=1), jnp.concatenate([high, low], axis=0)
            )
            out_ref[0, j] = result.astype(BF16)

        @pl.when(fits[j] < 0)
        def _():
            out_ref[0, j] = jnp.zeros(out_ref.shape[2:], BF16)


def fitted_values(me, owners, inverse, probs, target):
    return pl.pallas_call(
        values_kernel,
        out_shape=jax.ShapeDtypeStruct((1, SLOTS, CMAX, HD), BF16),
        in_specs=[SMEM, SMEM, VMEM, VMEM, VMEM],
        out_specs=VMEM,
        compiler_params=room(16),
        cost_estimate=cost(10**9, 4 * 10**6),
        name="fitted_values",
    )(me, owners, inverse, probs, target)


def exchange(blocks):
    return lax.all_to_all(blocks, SEQ, split_axis=0, concat_axis=0, tiled=True)


def gathered_keys(me, owners, indices, keys):
    layers, local, width = keys.shape
    shards = lax.axis_size(SEQ)
    fits = indices.shape[0]
    fit_ids = jnp.arange(fits, dtype=jnp.int32)
    offset = indices - me[0] * local
    inside = (offset >= 0) & (offset < local)
    source = (fit_ids // FITS_LAYER)[:, None] * local + jnp.clip(offset, 0, local - 1)
    picked = jnp.take(keys.reshape(layers * local, width), source, axis=0)
    found = jnp.where(inside[..., None], picked, jnp.zeros((), picked.dtype))
    ring = [(k, (k + 1) % shards) for k in range(shards)]

    def pass_on(_, carried):
        moving, whole = carried
        moving = lax.ppermute(moving, SEQ, ring)
        return moving, whole + moving

    _, everything = lax.fori_loop(0, shards - 1, pass_on, (found, found))
    mine = owners[0] == me[0]
    earlier = jnp.sum(
        jnp.where(mine[None, :] & (fit_ids[:, None] > fit_ids[None, :]), 1, 0), axis=1
    )
    chosen = [
        everything[jnp.sum(jnp.where(mine & (earlier == slot), fit_ids, 0))]
        for slot in range(SLOTS)
    ]
    return jnp.swapaxes(jnp.stack(chosen), 1, 2)


def on_device(queries, keys, values, indices, sizes, owners):
    layers, _, local, width = keys.shape
    key_rows = keys.reshape(layers, local, width)
    value_rows = values.reshape(layers, local, width)
    positions = indices[0]
    shards = lax.axis_size(SEQ)
    me = lax.axis_index(SEQ).astype(jnp.int32).reshape(1)
    regrouped = lax.all_to_all(queries, "head", split_axis=1, concat_axis=2, tiled=True)
    own_rows = regrouped.reshape(1, 16, width)
    packed, over = pack_keys(me, owners, sizes, positions, key_rows, shards)
    packed = lax.dynamic_update_slice(
        packed, jnp.broadcast_to(own_rows, (shards, 16, width)), (0, ROOM, 0)
    )
    received = exchange(packed)
    spare = lax.cond(
        over[0] > 0,
        lambda: gathered_keys(me, owners, positions, key_rows),
        lambda: jnp.zeros((SLOTS, width, CMAX), BF16),
    )
    parts = exchange(attend(received, key_rows, value_rows, spare))
    shift = local.bit_length() - 1
    probs, system, ends = systems(me, owners, sizes, over, positions, received, spare, shift)
    target = exchange(join(parts))
    inverse = invert(system, ends)
    return fitted_values(me, owners, inverse, probs, target)


def solution(mesh):
    apart = Mesh(mesh.devices.reshape(mesh.shape["head"], 8, 4), ("head", "seq_0", "seq_1"))
    placed = (
        P(None, None, HEAD_SEQ, None),
        P(None, "head", SEQ, None),
        P(None, "head", SEQ, None),
        P("head", None, None),
        P("head", None),
        P("head", None),
    )
    return jax.shard_map(
        on_device,
        mesh=apart,
        in_specs=placed,
        out_specs=P("head", SEQ, None, None),
        check_vma=False,
    )
```

```python
import functools

import jax
import jax.numpy as jnp
from jax import lax
from jax.experimental import pallas as pl
from jax.experimental.pallas import tpu as pltpu
from jax.sharding import Mesh
from jax.sharding import PartitionSpec as P

FITS = 8
FITS_LAYER = 4
SLOTS = 3
CMAX = 1024
HD = 128
LANES = 128
ROOM = 48
ROWS = ROOM + 16
PARTS = 4
CLOSE = 0.999
RIDGE = 0.3
SCALE = HD ** (-0.5)
SEQ = ("seq_0", "seq_1")
HEAD_SEQ = ("head", "seq_0", "seq_1")
F32 = jnp.float32
BF16 = jnp.bfloat16


def room(mib):
    return pltpu.CompilerParams(vmem_limit_bytes=mib << 20)


SMEM = pl.BlockSpec(memory_space=pltpu.SMEM)
VMEM = pl.BlockSpec(memory_space=pltpu.VMEM)


def cost(flops, moved, exps=0):
    return pl.CostEstimate(flops=flops, transcendentals=exps, bytes_accessed=moved)


def iota(shape, dim):
    return lax.broadcasted_iota(jnp.int32, shape, dim)


def fiota(shape, dim):
    return iota(shape, dim).astype(F32)


def dot(a, b, dims=((1,), (0,))):
    return lax.dot_general(a, b, (dims, ((), ())), preferred_element_type=F32)


def running(mask):
    rows, width = mask.shape
    blocks = width // LANES
    upper = (iota((LANES, LANES), 0) <= iota((LANES, LANES), 1)).astype(BF16)
    stacked = jnp.concatenate(
        [mask[:, b * LANES : (b + 1) * LANES] for b in range(blocks)], axis=0
    )
    inner = dot(stacked.astype(BF16), upper)
    carry = jnp.zeros((rows, 1), F32)
    parts = []
    for b in range(blocks):
        part = inner[b * rows : (b + 1) * rows]
        parts.append(part + carry)
        carry = carry + part[:, LANES - 1 : LANES]
    return jnp.concatenate(parts, axis=1), carry


def send_kernel(shards, me_ref, own_ref, size_ref, idx_ref, keys_ref, send_ref, flag_ref):
    me = me_ref[0]
    local = keys_ref.shape[1]
    shift = local.bit_length() - 1
    fits, width = idx_ref.shape
    idx = idx_ref[...]
    row = iota((fits, width), 0)
    lane = iota((fits, width), 1)
    size = jnp.zeros((fits, width), jnp.int32)
    own = jnp.zeros((fits, LANES), jnp.int32)
    row1 = iota((fits, LANES), 0)
    lane1 = iota((fits, LANES), 1)
    for f in range(fits):
        size = jnp.where(row == f, size_ref[0, f], size)
        own = jnp.where(row1 == f, own_ref[0, f] // PARTS, own)
    shard = jnp.where(lane < size, lax.shift_right_logical(idx, shift), -1)
    counts = jnp.zeros((fits, LANES), F32)
    for s in range(shards):
        count = jnp.sum(jnp.where(shard == s, 1.0, 0.0), axis=1, keepdims=True)
        counts = jnp.where(lane1 == s, count, counts)
    total = jnp.zeros((fits, LANES), F32)
    before = jnp.zeros((fits, LANES), F32)
    for f in range(fits):
        shared = jnp.where(own == own_ref[0, f] // PARTS, counts[f : f + 1, :], 0.0)
        total = total + shared
        before = before + jnp.where(row1 > f, shared, 0.0)
    flag_ref[0] = (jnp.max(total) > PARTS * ROOM).astype(jnp.int32)
    first = jnp.sum(jnp.where(lane1 == me, before, 0.0), axis=1, keepdims=True)
    mine = shard == me
    held = jnp.where(mine, 1.0, 0.0)
    place, _ = running(held)
    place = jnp.where(mine, place - 1.0 + first, -1.0)
    spot = jnp.where(mine, idx - me * local + 1, 0).astype(F32)
    send_ref[...] = jnp.zeros(send_ref.shape, BF16)
    slot = fiota((PARTS * ROOM, width), 0)
    at = fiota((PARTS * ROOM, local), 1)
    for f in range(fits):
        here = place[f : f + 1, :] == slot
        pos = jnp.sum(jnp.where(here, spot[f : f + 1, :], 0.0), axis=1, keepdims=True) - 1.0
        pick = jnp.where(pos == at, 1.0, 0.0).astype(BF16)
        rows = dot(pick, keys_ref[f // FITS_LAYER])
        rows = rows.astype(BF16)
        to = own_ref[0, f] // PARTS * PARTS
        for part in range(PARTS):
            send_ref[to + part, 0:ROOM, :] += rows[part * ROOM : (part + 1) * ROOM]


def pack_keys(me, owners, sizes, indices, keys, shards):
    return pl.pallas_call(
        lambda *refs: send_kernel(shards, *refs),
        out_shape=(
            jax.ShapeDtypeStruct((shards, ROWS, LANES), BF16),
            jax.ShapeDtypeStruct((1,), jnp.int32),
        ),
        in_specs=[SMEM, SMEM, SMEM, VMEM, VMEM],
        out_specs=(VMEM, SMEM),
        compiler_params=room(24),
        cost_estimate=cost(10**9, 3 * 10**6),
        name="pack_keys",
    )(me, owners, sizes, indices, keys)


def slots_of(me, own_ref):
    found = [jnp.int32(-1)] * SLOTS
    seen = jnp.int32(0)
    for f in range(FITS):
        match = own_ref[0, f] == me
        for j in range(SLOTS):
            found[j] = jnp.where(match & (seen == j), f, found[j])
        seen = seen + match.astype(jnp.int32)
    return found


def layer_rows(rows, layer):
    wide = rows.astype(F32)[:, 8 * layer : 8 * layer + 8, :]
    return wide.reshape(-1, wide.shape[-1])


def attend_kernel(recv_ref, keys_ref, values_ref, after_ref, out_ref):
    shards = recv_ref.shape[0]
    outs = []
    stat = jnp.zeros((shards * 8, LANES), F32)
    lane = iota(stat.shape, 1)
    for layer in range(2):
        query = layer_rows(recv_ref[...], layer).astype(BF16)
        scores = dot(query, keys_ref[layer], ((1,), (1,))) * SCALE
        peak = jnp.max(scores, axis=1, keepdims=True)
        weights = jnp.exp(scores - peak)
        total = jnp.sum(weights, axis=1, keepdims=True)
        numer = dot(weights.astype(BF16), values_ref[layer])
        outs.append((numer / total).reshape(shards, 8, HD))
        level = peak + jnp.log(total)
        high = level.astype(BF16).astype(F32)
        middle = (level - high).astype(BF16).astype(F32)
        for k, piece in enumerate((high, middle, level - high - middle)):
            stat = jnp.where(lane == 64 * layer + k, piece, stat)
    out_ref[...] = jnp.concatenate(outs + [stat.reshape(shards, 8, LANES)], axis=1).astype(BF16)


def attend(received, keys, values, after):
    shards = received.shape[0]
    return pl.pallas_call(
        attend_kernel,
        out_shape=jax.ShapeDtypeStruct((shards, 24, LANES), BF16),
        grid=(1,),
        in_specs=[
            pl.BlockSpec((shards, 16, LANES), lambda i: (0, ROOM // 16, 0)),
            pl.BlockSpec(keys.shape, lambda i: (0, 0, 0)),
            pl.BlockSpec(values.shape, lambda i: (0, 0, 0)),
            pl.BlockSpec(memory_space=pl.ANY),
        ],
        out_specs=pl.BlockSpec((shards, 24, LANES), lambda i: (0, 0, 0)),
        compiler_params=room(24),
        cost_estimate=cost(5 * 10**8, 3 * 10**6, 10**6),
        name="attend",
    )(received, keys, values, after)


def join_kernel(parts_ref, after_ref, out_ref):
    parts = parts_ref[...].astype(F32)
    stat = parts[:, 16:24, :]
    first = iota(stat.shape, 2) < 64
    level = jnp.concatenate(
        [
            jnp.sum(jnp.where(first, stat, 0.0), axis=2, keepdims=True),
            jnp.sum(jnp.where(first, 0.0, stat), axis=2, keepdims=True),
        ],
        axis=1,
    )
    weights = jnp.exp(level - jnp.max(level, axis=0, keepdims=True))
    numer = jnp.sum(weights * parts[:, 0:16, :], axis=0, keepdims=True)
    target = numer / jnp.sum(weights, axis=0, keepdims=True)
    out_ref[...] = jnp.broadcast_to(target, out_ref.shape).astype(BF16)


def join(parts, after):
    shards = parts.shape[0]
    return pl.pallas_call(
        join_kernel,
        out_shape=jax.ShapeDtypeStruct((shards, 16, LANES), BF16),
        in_specs=[VMEM, pl.BlockSpec(memory_space=pl.ANY)],
        out_specs=VMEM,
        compiler_params=room(8),
        cost_estimate=cost(10**6, 4 * 10**5, 10**3),
        name="join_parts",
    )(parts, after)


def turn_kernel(recv_ref, out_ref):
    rows = recv_ref[:, 0:ROOM, :]
    out_ref[...] = rows.reshape(-1, HD).astype(F32).T.astype(BF16)


def turned(received):
    return pl.pallas_call(
        turn_kernel,
        out_shape=jax.ShapeDtypeStruct((HD, received.shape[0] * ROOM), BF16),
        in_specs=[VMEM],
        out_specs=VMEM,
        compiler_params=room(8),
        cost_estimate=cost(10**6, 10**6),
        name="turn_keys",
    )(received)


def system_kernel(
    shift, slots, me_ref, own_ref, size_ref, over_ref, idx_ref, recv_ref, *refs
):
    blocks, (spare_ref, probs_ref, sys_ref, ends_ref, keys_ref) = refs[:PARTS], refs[PARTS:]
    shards = recv_ref.shape[0]
    width = idx_ref.shape[1]
    count = shards * 8
    span = 256
    eye = iota((count, count), 0) == iota((count, count), 1)
    me = me_ref[0]
    fits = slots_of(me, own_ref)
    lane = iota((1, width), 1)
    source = iota((shards, width), 0)
    counts = []
    for f in range(FITS):
        shard = jnp.where(
            lane < size_ref[0, f], lax.shift_right_logical(idx_ref[f : f + 1, :], shift), -1
        )
        counts.append(jnp.sum(jnp.where(shard == source, 1.0, 0.0), axis=1, keepdims=True))
    for i, j in enumerate(slots):

        @pl.when(fits[j] >= 0)
        def _():
            fit = jnp.maximum(fits[j], 0)
            size = size_ref[0, fit]
            shard = jnp.where(
                lane < size, lax.shift_right_logical(idx_ref[pl.ds(fit, 1), :], shift), -1
            )

            @pl.when(over_ref[0] == 0)
            def _():
                first = jnp.zeros((shards, 1), F32)
                for f in range(FITS):
                    ahead = (f < fit) & (own_ref[0, f] // PARTS == me // PARTS)
                    first = first + counts[f] * ahead.astype(F32)
                held = jnp.where(shard == source, 1.0, 0.0)
                place, _ = running(held)
                rank = jnp.sum(held * (place - 1.0 + first), axis=0, keepdims=True)
                rank = rank.astype(jnp.int32)
                part = sum((rank >= k * ROOM).astype(jnp.int32) for k in range(1, PARTS))
                turn = (me - part) & (PARTS - 1)
                dest = shard * ROOM + rank - part * ROOM + turn * (shards * ROOM)
                dest = jnp.where(shard >= 0, dest, -1)
                block = lax.shift_right_arithmetic(dest, 8)
                offset = dest & (span - 1)
                pick = jnp.where(offset == iota((span, width), 0), 1.0, 0.0).astype(BF16)
                total = jnp.zeros((HD, width), F32)
                pieces = blocks[0].shape[1] // span
                for b in range(PARTS):
                    stacked = jnp.concatenate(
                        [blocks[b][:, n * span : (n + 1) * span] for n in range(pieces)], axis=0
                    )
                    found = dot(stacked, pick)
                    for n in range(pieces):
                        total = jnp.where(
                            block == b * pieces + n, found[n * HD : (n + 1) * HD], total
                        )
                keys_ref[...] = total.astype(BF16)

            @pl.when(over_ref[0] > 0)
            def _():
                pltpu.sync_copy(spare_ref.at[j], keys_ref)

            rows = recv_ref[:, ROOM:ROWS, :]
            second = (fit >= FITS_LAYER).astype(F32)
            query = jnp.where(second > 0.5, layer_rows(rows, 1), layer_rows(rows, 0)).astype(BF16)
            scores = dot(query, keys_ref[...]) * SCALE
            scores = jnp.where(lane < size, scores, -jnp.inf)
            expo = jnp.exp(scores - jnp.max(scores, axis=1, keepdims=True))
            probs = (expo / jnp.sum(expo, axis=1, keepdims=True)).astype(BF16)
            gram = dot(probs, probs, ((1,), (1,)))
            trace = jnp.sum(jnp.where(eye, gram, 0.0))
            ridge = RIDGE * trace / size.astype(F32)
            top = jnp.max(jnp.sum(gram, axis=1, keepdims=True))
            sys_ref[i] = gram + jnp.where(eye, ridge, 0.0)
            ends_ref[2 * i] = ridge
            ends_ref[2 * i + 1] = jnp.minimum(top, trace) + ridge
            probs_ref[i] = probs.astype(F32).T.astype(BF16)

        @pl.when(fits[j] < 0)
        def _():
            sys_ref[i] = jnp.where(eye, 1.0, 0.0)
            ends_ref[2 * i] = jnp.float32(1.0)
            ends_ref[2 * i + 1] = jnp.float32(1.0)


def systems(me, owners, sizes, over, indices, received, blocks, spare, shift, slots):
    count = received.shape[0] * 8
    return pl.pallas_call(
        lambda *refs: system_kernel(shift, slots, *refs),
        out_shape=(
            jax.ShapeDtypeStruct((len(slots), CMAX, count), BF16),
            jax.ShapeDtypeStruct((len(slots), count, count), F32),
            jax.ShapeDtypeStruct((2 * len(slots),), F32),
        ),
        in_specs=[SMEM] * 4 + [VMEM] * (2 + PARTS) + [pl.BlockSpec(memory_space=pl.ANY)],
        out_specs=(VMEM, VMEM, SMEM),
        scratch_shapes=[pltpu.VMEM((HD, CMAX), BF16)],
        compiler_params=room(32),
        cost_estimate=cost(len(slots) * 10**9, 3 * 10**6, 10**6),
        name="systems_%d" % slots[0],
    )(me, owners, sizes, over, indices, received, *blocks, spare)


def split(x):
    high = x.astype(BF16)
    return high, (x - high.astype(F32)).astype(BF16)


def split3(x):
    high, _ = split(x)
    rest = x - high.astype(F32)
    middle, low = split(rest)
    return high, middle, low


def product(a, b):
    (a_high, a_low), (b_high, b_low) = a, b
    return dot(
        jnp.concatenate([a_high, a_high, a_low], axis=1),
        jnp.concatenate([b_high, b_low, b_high], axis=0),
    )


def product_full(a, b):
    (a0, a1, a2), (b0, b1, b2) = split3(a), split3(b)
    return dot(
        jnp.concatenate([a0, a0, a1, a0, a1, a2], axis=1),
        jnp.concatenate([b0, b1, b0, b2, b1, b0], axis=0),
    )


def invert_kernel(*refs):
    groups = len(refs) // 2 - 1
    out_ref, parts_ref = refs[2 * groups :]
    systems, ends = [], []
    for sys_ref, ends_ref in zip(refs[:groups], refs[groups : 2 * groups]):
        for i in range(sys_ref.shape[0]):
            systems.append(sys_ref.at[i])
            ends.append((ends_ref[2 * i], ends_ref[2 * i + 1]))
    count = out_ref.shape[1]
    eye = iota((count, count), 0) == iota((count, count), 1)
    lows = []
    for j in range(SLOTS):
        low, high = ends[j]
        middle = 2.0 / (low + high)
        out_ref[j] = middle * (jnp.where(eye, 2.0, 0.0) - middle * systems[j][...])
        parts_ref[j, 0], parts_ref[j, 1] = split(systems[j][...])
        ratio = (high - low) / (high + low)
        lows.append(1.0 - ratio * ratio)

    def step(lows, full):
        nexts = []
        for j in range(SLOTS):
            held = out_ref[j]
            middle = 2.0 / (lows[j] + 1.0)
            parts = split(held)
            if full:
                images = product_full(systems[j][...], held)
            else:
                images = product((parts_ref[j, 0], parts_ref[j, 1]), parts)
            rest = jnp.where(eye, 1.0, 0.0) - middle * images
            out_ref[j] = middle * (held + product(parts, split(rest)))
            ratio = (1.0 - lows[j]) / (1.0 + lows[j])
            nexts.append(1.0 - ratio * ratio)
        return tuple(nexts)

    lows = lax.while_loop(
        lambda lows: functools.reduce(jnp.minimum, lows) < CLOSE,
        lambda lows: step(lows, False),
        tuple(lows),
    )
    step(lows, True)


def invert(systems, ends):
    shape = (SLOTS, *systems[0].shape[1:])
    return pl.pallas_call(
        invert_kernel,
        out_shape=jax.ShapeDtypeStruct(shape, F32),
        in_specs=[VMEM] * len(systems) + [SMEM] * len(ends),
        out_specs=VMEM,
        scratch_shapes=[pltpu.VMEM((SLOTS, 2, *shape[1:]), BF16)],
        compiler_params=room(16),
        cost_estimate=cost(5 * 10**9, 2 * 10**6),
        name="invert",
    )(*systems, *ends)


def values_kernel(me_ref, own_ref, inverse_ref, target_ref, *refs):
    probs_refs, out_ref = refs[:-1], refs[-1]
    held = [ref.at[i] for ref in probs_refs for i in range(ref.shape[0])]
    fits = slots_of(me_ref[0], own_ref)
    for j in range(SLOTS):

        @pl.when(fits[j] >= 0)
        def _():
            rows = target_ref[...]
            first_rows, second_rows = layer_rows(rows, 0), layer_rows(rows, 1)
            second = (fits[j] >= FITS_LAYER).astype(F32)
            target = jnp.where(second > 0.5, second_rows, first_rows).astype(BF16)
            weights = dot(
                jnp.concatenate(split3(inverse_ref[j]), axis=1),
                jnp.concatenate([target] * 3, axis=0),
            )
            high, low = split(weights)
            probs = held[j][...]
            result = dot(
                jnp.concatenate([probs, probs], axis=1), jnp.concatenate([high, low], axis=0)
            )
            out_ref[0, j] = result.astype(BF16)

        @pl.when(fits[j] < 0)
        def _():
            out_ref[0, j] = jnp.zeros(out_ref.shape[2:], BF16)


def fitted_values(me, owners, inverse, probs, target):
    return pl.pallas_call(
        values_kernel,
        out_shape=jax.ShapeDtypeStruct((1, SLOTS, CMAX, HD), BF16),
        in_specs=[SMEM, SMEM, VMEM, VMEM] + [VMEM] * len(probs),
        out_specs=VMEM,
        compiler_params=room(16),
        cost_estimate=cost(10**9, 4 * 10**6),
        name="fitted_values",
    )(me, owners, inverse, target, *probs)


def exchange(blocks):
    return lax.all_to_all(blocks, SEQ, split_axis=0, concat_axis=0, tiled=True)


def gathered_keys(me, owners, indices, keys):
    layers, local, width = keys.shape
    shards = lax.axis_size(SEQ)
    fits = indices.shape[0]
    fit_ids = jnp.arange(fits, dtype=jnp.int32)
    offset = indices - me[0] * local
    inside = (offset >= 0) & (offset < local)
    source = (fit_ids // FITS_LAYER)[:, None] * local + jnp.clip(offset, 0, local - 1)
    picked = jnp.take(keys.reshape(layers * local, width), source, axis=0)
    found = jnp.where(inside[..., None], picked, jnp.zeros((), picked.dtype))
    ring = [(k, (k + 1) % shards) for k in range(shards)]

    def pass_on(_, carried):
        moving, whole = carried
        moving = lax.ppermute(moving, SEQ, ring)
        return moving, whole + moving

    _, everything = lax.fori_loop(0, shards - 1, pass_on, (found, found))
    mine = owners[0] == me[0]
    earlier = jnp.sum(
        jnp.where(mine[None, :] & (fit_ids[:, None] > fit_ids[None, :]), 1, 0), axis=1
    )
    chosen = [
        everything[jnp.sum(jnp.where(mine & (earlier == slot), fit_ids, 0))]
        for slot in range(SLOTS)
    ]
    return jnp.swapaxes(jnp.stack(chosen), 1, 2)


def on_device(queries, keys, values, indices, sizes, owners):
    layers, _, local, width = keys.shape
    key_rows = keys.reshape(layers, local, width)
    value_rows = values.reshape(layers, local, width)
    positions = indices[0]
    shards = lax.axis_size(SEQ)
    me = lax.axis_index(SEQ).astype(jnp.int32).reshape(1)
    regrouped = lax.all_to_all(queries, "head", split_axis=1, concat_axis=2, tiled=True)
    own_rows = regrouped.reshape(1, 16, width)
    packed, over = pack_keys(me, owners, sizes, positions, key_rows, shards)
    packed = lax.dynamic_update_slice(
        packed, jnp.broadcast_to(own_rows, (shards, 16, width)), (0, ROOM, 0)
    )
    received = exchange(packed)
    spare = lax.cond(
        over[0] > 0,
        lambda: gathered_keys(me, owners, positions, key_rows),
        lambda: jnp.zeros((SLOTS, width, CMAX), BF16),
    )
    own_block = turned(received)
    blocks = [own_block] + [
        lax.ppermute(own_block, "seq_1", [(k, (k + d) % PARTS) for k in range(PARTS)])
        for d in range(1, PARTS)
    ]
    parts = exchange(attend(received, key_rows, value_rows, spare))
    shift = local.bit_length() - 1
    fitted = [
        systems(me, owners, sizes, over, positions, received, blocks, spare, shift, slots)
        for slots in ((0,), (1, 2))
    ]
    probs, system, ends = zip(*fitted)
    target = exchange(join(parts, system[0]))
    inverse = invert(system, ends)
    return fitted_values(me, owners, inverse, probs, target)


def solution(mesh):
    apart = Mesh(mesh.devices.reshape(mesh.shape["head"], 8, 4), ("head", "seq_0", "seq_1"))
    placed = (
        P(None, None, HEAD_SEQ, None),
        P(None, "head", SEQ, None),
        P(None, "head", SEQ, None),
        P("head", None, None),
        P("head", None),
        P("head", None),
    )
    return jax.shard_map(
        on_device,
        mesh=apart,
        in_specs=placed,
        out_specs=P("head", SEQ, None, None),
        check_vma=False,
    )
```

```python
import functools

import jax
import jax.numpy as jnp
from jax import lax
from jax.experimental import pallas as pl
from jax.experimental.pallas import tpu as pltpu
from jax.sharding import Mesh
from jax.sharding import PartitionSpec as P

FITS = 8
FITS_LAYER = 4
SLOTS = 3
CMAX = 1024
HD = 128
LANES = 128
ROOM = 48
ROWS = ROOM + 16
PARTS = 4
CLOSE = 0.97
STIFF = 0.004
RIDGE = 0.3
SCALE = HD ** (-0.5)
SEQ = ("seq_0", "seq_1")
HEAD_SEQ = ("head", "seq_0", "seq_1")
F32 = jnp.float32
BF16 = jnp.bfloat16


def room(mib):
    return pltpu.CompilerParams(vmem_limit_bytes=mib << 20)


SMEM = pl.BlockSpec(memory_space=pltpu.SMEM)
VMEM = pl.BlockSpec(memory_space=pltpu.VMEM)


def cost(flops, moved, exps=0):
    return pl.CostEstimate(flops=flops, transcendentals=exps, bytes_accessed=moved)


def iota(shape, dim):
    return lax.broadcasted_iota(jnp.int32, shape, dim)


def fiota(shape, dim):
    return iota(shape, dim).astype(F32)


def dot(a, b, dims=((1,), (0,))):
    return lax.dot_general(a, b, (dims, ((), ())), preferred_element_type=F32)


def running(mask):
    rows, width = mask.shape
    blocks = width // LANES
    upper = (iota((LANES, LANES), 0) <= iota((LANES, LANES), 1)).astype(BF16)
    stacked = jnp.concatenate(
        [mask[:, b * LANES : (b + 1) * LANES] for b in range(blocks)], axis=0
    )
    inner = dot(stacked.astype(BF16), upper)
    carry = jnp.zeros((rows, 1), F32)
    parts = []
    for b in range(blocks):
        part = inner[b * rows : (b + 1) * rows]
        parts.append(part + carry)
        carry = carry + part[:, LANES - 1 : LANES]
    return jnp.concatenate(parts, axis=1), carry


def send_kernel(shards, me_ref, own_ref, size_ref, idx_ref, keys_ref, send_ref, flag_ref):
    me = me_ref[0]
    local = keys_ref.shape[1]
    shift = local.bit_length() - 1
    fits, width = idx_ref.shape
    idx = idx_ref[...]
    row = iota((fits, width), 0)
    lane = iota((fits, width), 1)
    size = jnp.zeros((fits, width), jnp.int32)
    own = jnp.zeros((fits, LANES), jnp.int32)
    row1 = iota((fits, LANES), 0)
    lane1 = iota((fits, LANES), 1)
    for f in range(fits):
        size = jnp.where(row == f, size_ref[0, f], size)
        own = jnp.where(row1 == f, own_ref[0, f] // PARTS, own)
    shard = jnp.where(lane < size, lax.shift_right_logical(idx, shift), -1)
    counts = jnp.zeros((fits, LANES), F32)
    for s in range(shards):
        count = jnp.sum(jnp.where(shard == s, 1.0, 0.0), axis=1, keepdims=True)
        counts = jnp.where(lane1 == s, count, counts)
    total = jnp.zeros((fits, LANES), F32)
    before = jnp.zeros((fits, LANES), F32)
    for f in range(fits):
        shared = jnp.where(own == own_ref[0, f] // PARTS, counts[f : f + 1, :], 0.0)
        total = total + shared
        before = before + jnp.where(row1 > f, shared, 0.0)
    flag_ref[0] = (jnp.max(total) > PARTS * ROOM).astype(jnp.int32)
    first = jnp.sum(jnp.where(lane1 == me, before, 0.0), axis=1, keepdims=True)
    mine = shard == me
    held = jnp.where(mine, 1.0, 0.0)
    place, _ = running(held)
    place = jnp.where(mine, place - 1.0 + first, -1.0)
    spot = jnp.where(mine, idx - me * local + 1, 0).astype(F32)
    send_ref[...] = jnp.zeros(send_ref.shape, BF16)
    slot = fiota((PARTS * ROOM, width), 0)
    at = fiota((PARTS * ROOM, local), 1)
    for f in range(fits):
        here = place[f : f + 1, :] == slot
        pos = jnp.sum(jnp.where(here, spot[f : f + 1, :], 0.0), axis=1, keepdims=True) - 1.0
        pick = jnp.where(pos == at, 1.0, 0.0).astype(BF16)
        rows = dot(pick, keys_ref[f // FITS_LAYER])
        rows = rows.astype(BF16)
        to = own_ref[0, f] // PARTS * PARTS
        for part in range(PARTS):
            send_ref[to + part, 0:ROOM, :] += rows[part * ROOM : (part + 1) * ROOM]


def pack_keys(me, owners, sizes, indices, keys, shards):
    return pl.pallas_call(
        lambda *refs: send_kernel(shards, *refs),
        out_shape=(
            jax.ShapeDtypeStruct((shards, ROWS, LANES), BF16),
            jax.ShapeDtypeStruct((1,), jnp.int32),
        ),
        in_specs=[SMEM, SMEM, SMEM, VMEM, VMEM],
        out_specs=(VMEM, SMEM),
        compiler_params=room(24),
        cost_estimate=cost(10**9, 3 * 10**6),
        name="pack_keys",
    )(me, owners, sizes, indices, keys)


def slots_of(me, own_ref):
    found = [jnp.int32(-1)] * SLOTS
    seen = jnp.int32(0)
    for f in range(FITS):
        match = own_ref[0, f] == me
        for j in range(SLOTS):
            found[j] = jnp.where(match & (seen == j), f, found[j])
        seen = seen + match.astype(jnp.int32)
    return found


def layer_rows(rows, layer):
    wide = rows.astype(F32)[:, 8 * layer : 8 * layer + 8, :]
    return wide.reshape(-1, wide.shape[-1])


def attend_kernel(recv_ref, keys_ref, values_ref, out_ref):
    shards = recv_ref.shape[0]
    outs = []
    stat = jnp.zeros((shards * 8, LANES), F32)
    lane = iota(stat.shape, 1)
    for layer in range(2):
        query = layer_rows(recv_ref[...], layer).astype(BF16)
        scores = dot(query, keys_ref[layer], ((1,), (1,))) * SCALE
        peak = jnp.max(scores, axis=1, keepdims=True)
        weights = jnp.exp(scores - peak)
        total = jnp.sum(weights, axis=1, keepdims=True)
        numer = dot(weights.astype(BF16), values_ref[layer])
        outs.append((numer / total).reshape(shards, 8, HD))
        level = peak + jnp.log(total)
        high = level.astype(BF16).astype(F32)
        middle = (level - high).astype(BF16).astype(F32)
        for k, piece in enumerate((high, middle, level - high - middle)):
            stat = jnp.where(lane == 64 * layer + k, piece, stat)
    out_ref[...] = jnp.concatenate(outs + [stat.reshape(shards, 8, LANES)], axis=1).astype(BF16)


def attend(received, keys, values):
    shards = received.shape[0]
    return pl.pallas_call(
        attend_kernel,
        out_shape=jax.ShapeDtypeStruct((shards, 24, LANES), BF16),
        grid=(1,),
        in_specs=[
            pl.BlockSpec((shards, 16, LANES), lambda i: (0, ROOM // 16, 0)),
            pl.BlockSpec(keys.shape, lambda i: (0, 0, 0)),
            pl.BlockSpec(values.shape, lambda i: (0, 0, 0)),
        ],
        out_specs=pl.BlockSpec((shards, 24, LANES), lambda i: (0, 0, 0)),
        compiler_params=room(24),
        cost_estimate=cost(5 * 10**8, 3 * 10**6, 10**6),
        name="attend",
    )(received, keys, values)


def join_kernel(parts_ref, after_ref, out_ref):
    parts = parts_ref[...].astype(F32)
    stat = parts[:, 16:24, :]
    first = iota(stat.shape, 2) < 64
    level = jnp.concatenate(
        [
            jnp.sum(jnp.where(first, stat, 0.0), axis=2, keepdims=True),
            jnp.sum(jnp.where(first, 0.0, stat), axis=2, keepdims=True),
        ],
        axis=1,
    )
    weights = jnp.exp(level - jnp.max(level, axis=0, keepdims=True))
    numer = jnp.sum(weights * parts[:, 0:16, :], axis=0, keepdims=True)
    target = numer / jnp.sum(weights, axis=0, keepdims=True)
    out_ref[...] = jnp.broadcast_to(target, out_ref.shape).astype(BF16)


def join(parts, after):
    shards = parts.shape[0]
    return pl.pallas_call(
        join_kernel,
        out_shape=jax.ShapeDtypeStruct((shards, 16, LANES), BF16),
        in_specs=[VMEM, pl.BlockSpec(memory_space=pl.ANY)],
        out_specs=VMEM,
        compiler_params=room(8),
        cost_estimate=cost(10**6, 4 * 10**5, 10**3),
        name="join_parts",
    )(parts, after)


def turn_kernel(recv_ref, after_ref, out_ref):
    rows = recv_ref[:, 0:ROOM, :]
    out_ref[...] = rows.reshape(-1, HD).astype(F32).T.astype(BF16)


def turned(received, after):
    return pl.pallas_call(
        turn_kernel,
        out_shape=jax.ShapeDtypeStruct((HD, received.shape[0] * ROOM), BF16),
        in_specs=[VMEM, pl.BlockSpec(memory_space=pl.ANY)],
        out_specs=VMEM,
        compiler_params=room(8),
        cost_estimate=cost(10**6, 10**6),
        name="turn_keys",
    )(received, after)


def plan_kernel(
    shift, shards, me_ref, own_ref, size_ref, idx_ref, after_ref, dest_ref, used_ref
):
    width = idx_ref.shape[1]
    me = me_ref[0]
    fits = slots_of(me, own_ref)
    lane = iota((1, width), 1)
    source = iota((shards, width), 0)

    def shards_of(fit, size):
        place = lax.shift_right_logical(idx_ref[pl.ds(fit, 1), :], shift)
        return jnp.where(lane < size, place, -1)

    counts = []
    for f in range(FITS):
        shard = shards_of(f, size_ref[0, f])
        counts.append(jnp.sum(jnp.where(shard == source, 1.0, 0.0), axis=1, keepdims=True))
    dest_ref[...] = jnp.full(dest_ref.shape, -1, jnp.int32)
    for j in range(SLOTS):
        fit = jnp.maximum(fits[j], 0)
        shard = shards_of(fit, jnp.where(fits[j] >= 0, size_ref[0, fit], 0))
        first = jnp.zeros((shards, 1), F32)
        for f in range(FITS):
            ahead = (f < fit) & (own_ref[0, f] // PARTS == me // PARTS)
            first = first + counts[f] * ahead.astype(F32)
        held = jnp.where(shard == source, 1.0, 0.0)
        place, _ = running(held)
        rank = jnp.sum(held * (place - 1.0 + first), axis=0, keepdims=True).astype(jnp.int32)
        part = sum((rank >= k * ROOM).astype(jnp.int32) for k in range(1, PARTS))
        turn = (me - part) & (PARTS - 1)
        dest = shard * ROOM + rank - part * ROOM + turn * (shards * ROOM)
        dest_ref[j : j + 1, :] = jnp.where(shard >= 0, dest, -1)
        for b in range(PARTS):
            here = jnp.where((shard >= 0) & (turn == b), 1, 0)
            used_ref[j * PARTS + b] = jnp.max(here)


def plan(me, owners, sizes, indices, after, shards, shift):
    return pl.pallas_call(
        lambda *refs: plan_kernel(shift, shards, *refs),
        out_shape=(
            jax.ShapeDtypeStruct(indices.shape, jnp.int32),
            jax.ShapeDtypeStruct((SLOTS * PARTS,), jnp.int32),
        ),
        in_specs=[SMEM, SMEM, SMEM, VMEM, pl.BlockSpec(memory_space=pl.ANY)],
        out_specs=(VMEM, SMEM),
        compiler_params=room(8),
        cost_estimate=cost(10**10, 10**6),
        name="plan",
    )(me, owners, sizes, indices, after)


def system_kernel(slots, me_ref, own_ref, size_ref, over_ref, used_ref, dest_ref, recv_ref, *refs):
    blocks = refs[:PARTS]
    spare_ref, probs_ref, sys_ref, ends_ref, keys_ref, total_ref, held_ref, sems = refs[PARTS:]
    width = dest_ref.shape[1]
    count = recv_ref.shape[0] * 8
    span = 256
    eye = iota((count, count), 0) == iota((count, count), 1)
    fits = slots_of(me_ref[0], own_ref)
    lane = iota((1, width), 1)

    def copy_out(i):
        return pltpu.make_async_copy(held_ref.at[i], probs_ref.at[i], sems.at[i])

    for i, j in enumerate(slots):

        @pl.when(fits[j] >= 0)
        def _():
            fit = jnp.maximum(fits[j], 0)
            size = size_ref[0, fit]

            @pl.when(over_ref[0] == 0)
            def _():
                dest = dest_ref[j : j + 1, :]
                block = lax.shift_right_arithmetic(dest, 8)
                offset = dest & (span - 1)
                pick = jnp.where(offset == iota((span, width), 0), 1.0, 0.0).astype(BF16)
                total_ref[...] = jnp.zeros((HD, width), F32)
                pieces = blocks[0].shape[1] // span
                for b in range(PARTS):

                    @pl.when(used_ref[j * PARTS + b] > 0)
                    def _():
                        stacked = jnp.concatenate(
                            [blocks[b][:, n * span : (n + 1) * span] for n in range(pieces)],
                            axis=0,
                        )
                        found = dot(stacked, pick)
                        total = total_ref[...]
                        for n in range(pieces):
                            total = jnp.where(
                                block == b * pieces + n, found[n * HD : (n + 1) * HD], total
                            )
                        total_ref[...] = total

                keys_ref[...] = total_ref[...].astype(BF16)

            @pl.when(over_ref[0] > 0)
            def _():
                pltpu.sync_copy(spare_ref.at[j], keys_ref)

            rows = recv_ref[:, ROOM:ROWS, :]
            second = (fit >= FITS_LAYER).astype(F32)
            query = jnp.where(second > 0.5, layer_rows(rows, 1), layer_rows(rows, 0)).astype(BF16)
            scores = dot(query, keys_ref[...]) * SCALE
            scores = jnp.where(lane < size, scores, -jnp.inf)
            expo = jnp.exp(scores - jnp.max(scores, axis=1, keepdims=True))
            probs = (expo / jnp.sum(expo, axis=1, keepdims=True)).astype(BF16)
            held_ref[i] = probs.astype(F32).T.astype(BF16)
            copy_out(i).start()
            gram = dot(probs, probs, ((1,), (1,)))
            trace = jnp.sum(jnp.where(eye, gram, 0.0))
            ridge = RIDGE * trace / size.astype(F32)
            top = jnp.max(jnp.sum(gram, axis=1, keepdims=True))
            sys_ref[i] = gram + jnp.where(eye, ridge, 0.0)
            ends_ref[2 * i] = ridge
            ends_ref[2 * i + 1] = jnp.minimum(top, trace) + ridge

        @pl.when(fits[j] < 0)
        def _():
            sys_ref[i] = jnp.where(eye, 1.0, 0.0)
            ends_ref[2 * i] = jnp.float32(1.0)
            ends_ref[2 * i + 1] = jnp.float32(1.0)

    for i, j in enumerate(slots):

        @pl.when(fits[j] >= 0)
        def _():
            copy_out(i).wait()


def systems(me, owners, sizes, over, used, dest, received, blocks, spare, slots):
    count = received.shape[0] * 8
    return pl.pallas_call(
        lambda *refs: system_kernel(slots, *refs),
        out_shape=(
            pltpu.HBM((len(slots), CMAX, count), BF16),
            jax.ShapeDtypeStruct((len(slots), count, count), F32),
            jax.ShapeDtypeStruct((2 * len(slots),), F32),
        ),
        in_specs=[SMEM] * 5 + [VMEM] * (2 + PARTS) + [pl.BlockSpec(memory_space=pl.ANY)],
        out_specs=(pl.BlockSpec(memory_space=pltpu.HBM), VMEM, SMEM),
        scratch_shapes=[
            pltpu.VMEM((HD, CMAX), BF16),
            pltpu.VMEM((HD, CMAX), F32),
            pltpu.VMEM((len(slots), CMAX, count), BF16),
            pltpu.SemaphoreType.DMA((len(slots),)),
        ],
        compiler_params=room(32),
        cost_estimate=cost(len(slots) * 10**9, 3 * 10**6, 10**6),
        name="systems_%d" % slots[0],
    )(me, owners, sizes, over, used, dest, received, *blocks, spare)


def split(x):
    high = x.astype(BF16)
    return high, (x - high.astype(F32)).astype(BF16)


def split3(x):
    high, _ = split(x)
    rest = x - high.astype(F32)
    middle, low = split(rest)
    return high, middle, low


def product(a, b):
    (a_high, a_low), (b_high, b_low) = a, b
    return dot(
        jnp.concatenate([a_high, a_high, a_low], axis=1),
        jnp.concatenate([b_high, b_low, b_high], axis=0),
    )


def product_full(a, b):
    (a0, a1, a2), (b0, b1, b2) = split3(a), split3(b)
    return dot(
        jnp.concatenate([a0, a0, a1, a0, a1, a2], axis=1),
        jnp.concatenate([b0, b1, b0, b2, b1, b0], axis=0),
    )


def invert_kernel(*refs):
    groups = len(refs) // 2 - 1
    out_ref, parts_ref = refs[2 * groups :]
    systems, ends = [], []
    for sys_ref, ends_ref in zip(refs[:groups], refs[groups : 2 * groups]):
        for i in range(sys_ref.shape[0]):
            systems.append(sys_ref.at[i])
            ends.append((ends_ref[2 * i], ends_ref[2 * i + 1]))
    count = out_ref.shape[1]
    eye = iota((count, count), 0) == iota((count, count), 1)
    lows = []
    for j in range(SLOTS):
        low, high = ends[j]
        middle = 2.0 / (low + high)
        out_ref[j] = middle * (jnp.where(eye, 2.0, 0.0) - middle * systems[j][...])
        parts_ref[j, 0], parts_ref[j, 1] = split(systems[j][...])
        ratio = (high - low) / (high + low)
        lows.append(1.0 - ratio * ratio)

    def step(lows, last=False, full=False):
        nexts = []
        for j in range(SLOTS):
            held = out_ref[j]
            middle = 2.0 / (lows[j] + 1.0)
            parts = split(held)
            if full:
                images = product_full(systems[j][...], held)
            else:
                images = product((parts_ref[j, 0], parts_ref[j, 1]), parts)
            rest = jnp.where(eye, 1.0, 0.0) - middle * images
            if last and not full:
                moved = dot(parts[0], rest.astype(BF16))
            else:
                moved = product(parts, split(rest))
            out_ref[j] = middle * (held + moved)
            ratio = (1.0 - lows[j]) / (1.0 + lows[j])
            nexts.append(1.0 - ratio * ratio)
        return tuple(nexts)

    stiff = functools.reduce(jnp.minimum, lows) < STIFF
    lows = lax.while_loop(
        lambda lows: functools.reduce(jnp.minimum, lows) < CLOSE, step, tuple(lows)
    )

    @pl.when(stiff)
    def _():
        step(lows, full=True)

    @pl.when(jnp.logical_not(stiff))
    def _():
        step(lows, last=True)


def invert(systems, ends):
    shape = (SLOTS, *systems[0].shape[1:])
    return pl.pallas_call(
        invert_kernel,
        out_shape=jax.ShapeDtypeStruct(shape, F32),
        in_specs=[VMEM] * len(systems) + [SMEM] * len(ends),
        out_specs=VMEM,
        scratch_shapes=[pltpu.VMEM((SLOTS, 2, *shape[1:]), BF16)],
        compiler_params=room(16),
        cost_estimate=cost(5 * 10**9, 2 * 10**6),
        name="invert",
    )(*systems, *ends)


def values_kernel(me_ref, own_ref, inverse_ref, target_ref, *refs):
    probs_refs, out_ref = refs[:-1], refs[-1]
    held = [ref.at[i] for ref in probs_refs for i in range(ref.shape[0])]
    fits = slots_of(me_ref[0], own_ref)
    for j in range(SLOTS):

        @pl.when(fits[j] >= 0)
        def _():
            rows = target_ref[...]
            first_rows, second_rows = layer_rows(rows, 0), layer_rows(rows, 1)
            second = (fits[j] >= FITS_LAYER).astype(F32)
            target = jnp.where(second > 0.5, second_rows, first_rows).astype(BF16)
            weights = dot(
                jnp.concatenate(split3(inverse_ref[j]), axis=1),
                jnp.concatenate([target] * 3, axis=0),
            )
            high, low = split(weights)
            probs = held[j][...]
            result = dot(
                jnp.concatenate([probs, probs], axis=1), jnp.concatenate([high, low], axis=0)
            )
            out_ref[0, j] = result.astype(BF16)

        @pl.when(fits[j] < 0)
        def _():
            out_ref[0, j] = jnp.zeros(out_ref.shape[2:], BF16)


def fitted_values(me, owners, inverse, probs, target):
    return pl.pallas_call(
        values_kernel,
        out_shape=jax.ShapeDtypeStruct((1, SLOTS, CMAX, HD), BF16),
        in_specs=[SMEM, SMEM, VMEM, VMEM] + [VMEM] * len(probs),
        out_specs=VMEM,
        compiler_params=room(16),
        cost_estimate=cost(10**9, 4 * 10**6),
        name="fitted_values",
    )(me, owners, inverse, target, *probs)


def exchange(blocks):
    return lax.all_to_all(blocks, SEQ, split_axis=0, concat_axis=0, tiled=True)


def gathered_keys(me, owners, indices, keys):
    layers, local, width = keys.shape
    shards = lax.axis_size(SEQ)
    fits = indices.shape[0]
    fit_ids = jnp.arange(fits, dtype=jnp.int32)
    offset = indices - me[0] * local
    inside = (offset >= 0) & (offset < local)
    source = (fit_ids // FITS_LAYER)[:, None] * local + jnp.clip(offset, 0, local - 1)
    picked = jnp.take(keys.reshape(layers * local, width), source, axis=0)
    found = jnp.where(inside[..., None], picked, jnp.zeros((), picked.dtype))
    ring = [(k, (k + 1) % shards) for k in range(shards)]

    def pass_on(_, carried):
        moving, whole = carried
        moving = lax.ppermute(moving, SEQ, ring)
        return moving, whole + moving

    _, everything = lax.fori_loop(0, shards - 1, pass_on, (found, found))
    mine = owners[0] == me[0]
    earlier = jnp.sum(
        jnp.where(mine[None, :] & (fit_ids[:, None] > fit_ids[None, :]), 1, 0), axis=1
    )
    chosen = [
        everything[jnp.sum(jnp.where(mine & (earlier == slot), fit_ids, 0))]
        for slot in range(SLOTS)
    ]
    return jnp.swapaxes(jnp.stack(chosen), 1, 2)


def on_device(queries, keys, values, indices, sizes, owners):
    layers, _, local, width = keys.shape
    key_rows = keys.reshape(layers, local, width)
    value_rows = values.reshape(layers, local, width)
    positions = indices[0]
    shards = lax.axis_size(SEQ)
    me = lax.axis_index(SEQ).astype(jnp.int32).reshape(1)
    regrouped = lax.all_to_all(queries, "head", split_axis=1, concat_axis=2, tiled=True)
    own_rows = regrouped.reshape(1, 16, width)
    packed, over = pack_keys(me, owners, sizes, positions, key_rows, shards)
    packed = lax.dynamic_update_slice(
        packed, jnp.broadcast_to(own_rows, (shards, 16, width)), (0, ROOM, 0)
    )
    received = exchange(packed)
    spare = lax.cond(
        over[0] > 0,
        lambda: gathered_keys(me, owners, positions, key_rows),
        lambda: jnp.zeros((SLOTS, width, CMAX), BF16),
    )
    shift = local.bit_length() - 1
    dest, used = plan(me, owners, sizes, positions, spare, shards, shift)
    own_block = turned(received, dest)
    blocks = [own_block] + [
        lax.ppermute(own_block, "seq_1", [(k, (k + d) % PARTS) for k in range(PARTS)])
        for d in range(1, PARTS)
    ]
    parts = exchange(attend(received, key_rows, value_rows))
    fitted = [
        systems(me, owners, sizes, over, used, dest, received, blocks, spare, slots)
        for slots in ((0,), (1, 2))
    ]
    probs, system, ends = zip(*fitted)
    target = exchange(join(parts, system[0]))
    inverse = invert(system, ends)
    return fitted_values(me, owners, inverse, probs, target)


def solution(mesh):
    apart = Mesh(mesh.devices.reshape(mesh.shape["head"], 8, 4), ("head", "seq_0", "seq_1"))
    placed = (
        P(None, None, HEAD_SEQ, None),
        P(None, "head", SEQ, None),
        P(None, "head", SEQ, None),
        P("head", None, None),
        P("head", None),
        P("head", None),
    )
    return jax.shard_map(
        on_device,
        mesh=apart,
        in_specs=placed,
        out_specs=P("head", SEQ, None, None),
        check_vma=False,
    )
```

```python
import functools

import jax
import jax.numpy as jnp
from jax import lax
from jax.experimental import pallas as pl
from jax.experimental.pallas import tpu as pltpu
from jax.sharding import Mesh
from jax.sharding import PartitionSpec as P

FITS = 8
FITS_LAYER = 4
SLOTS = 3
CMAX = 1024
HD = 128
LANES = 128
ROOM = 48
ROWS = ROOM + 16
PARTS = 4
CLOSE = 0.97
STIFF = 0.004
RIDGE = 0.3
OVER, ME, OWNERS, SIZES, INFO = 0, 1, 2, 10, 32
SLOT_FIT, SLOT_SIZE, USED = 1, 4, 8
SCALE = HD ** (-0.5)
SEQ = ("seq_0", "seq_1")
HEAD_SEQ = ("head", "seq_0", "seq_1")
F32 = jnp.float32
BF16 = jnp.bfloat16


def room(mib):
    return pltpu.CompilerParams(vmem_limit_bytes=mib << 20)


SMEM = pl.BlockSpec(memory_space=pltpu.SMEM)
VMEM = pl.BlockSpec(memory_space=pltpu.VMEM)


def cost(flops, moved, exps=0):
    return pl.CostEstimate(flops=flops, transcendentals=exps, bytes_accessed=moved)


def iota(shape, dim):
    return lax.broadcasted_iota(jnp.int32, shape, dim)


def fiota(shape, dim):
    return iota(shape, dim).astype(F32)


def dot(a, b, dims=((1,), (0,))):
    return lax.dot_general(a, b, (dims, ((), ())), preferred_element_type=F32)


def running(mask):
    rows, width = mask.shape
    blocks = width // LANES
    upper = (iota((LANES, LANES), 0) <= iota((LANES, LANES), 1)).astype(BF16)
    stacked = jnp.concatenate(
        [mask[:, b * LANES : (b + 1) * LANES] for b in range(blocks)], axis=0
    )
    inner = dot(stacked.astype(BF16), upper)
    carry = jnp.zeros((rows, 1), F32)
    parts = []
    for b in range(blocks):
        part = inner[b * rows : (b + 1) * rows]
        parts.append(part + carry)
        carry = carry + part[:, LANES - 1 : LANES]
    return jnp.concatenate(parts, axis=1), carry


def send_kernel(shards, own_ref, size_ref, idx_ref, keys_ref, send_ref, info_ref):
    me = lax.axis_index(SEQ).astype(jnp.int32)
    local = keys_ref.shape[1]
    shift = local.bit_length() - 1
    fits, width = idx_ref.shape
    idx = idx_ref[...]
    row = iota((fits, width), 0)
    lane = iota((fits, width), 1)
    size = jnp.zeros((fits, width), jnp.int32)
    own = jnp.zeros((fits, LANES), jnp.int32)
    row1 = iota((fits, LANES), 0)
    lane1 = iota((fits, LANES), 1)
    for f in range(fits):
        size = jnp.where(row == f, size_ref[0, f], size)
        own = jnp.where(row1 == f, own_ref[0, f] // PARTS, own)
    shard = jnp.where(lane < size, lax.shift_right_logical(idx, shift), -1)
    counts = jnp.zeros((fits, LANES), F32)
    for s in range(shards):
        count = jnp.sum(jnp.where(shard == s, 1.0, 0.0), axis=1, keepdims=True)
        counts = jnp.where(lane1 == s, count, counts)
    total = jnp.zeros((fits, LANES), F32)
    before = jnp.zeros((fits, LANES), F32)
    for f in range(fits):
        shared = jnp.where(own == own_ref[0, f] // PARTS, counts[f : f + 1, :], 0.0)
        total = total + shared
        before = before + jnp.where(row1 > f, shared, 0.0)
    info_ref[OVER] = (jnp.max(total) > PARTS * ROOM).astype(jnp.int32)
    info_ref[ME] = me
    for f in range(fits):
        info_ref[OWNERS + f] = own_ref[0, f]
        info_ref[SIZES + f] = size_ref[0, f]
    first = jnp.sum(jnp.where(lane1 == me, before, 0.0), axis=1, keepdims=True)
    mine = shard == me
    held = jnp.where(mine, 1.0, 0.0)
    place, _ = running(held)
    place = jnp.where(mine, place - 1.0 + first, -1.0)
    spot = jnp.where(mine, idx - me * local + 1, 0).astype(F32)
    send_ref[...] = jnp.zeros(send_ref.shape, BF16)
    slot = fiota((PARTS * ROOM, width), 0)
    at = fiota((PARTS * ROOM, local), 1)
    for f in range(fits):
        here = place[f : f + 1, :] == slot
        pos = jnp.sum(jnp.where(here, spot[f : f + 1, :], 0.0), axis=1, keepdims=True) - 1.0
        pick = jnp.where(pos == at, 1.0, 0.0).astype(BF16)
        rows = dot(pick, keys_ref[f // FITS_LAYER])
        rows = rows.astype(BF16)
        to = own_ref[0, f] // PARTS * PARTS
        for part in range(PARTS):
            send_ref[to + part, 0:ROOM, :] += rows[part * ROOM : (part + 1) * ROOM]


def pack_keys(owners, sizes, indices, keys, shards):
    return pl.pallas_call(
        lambda *refs: send_kernel(shards, *refs),
        out_shape=(
            jax.ShapeDtypeStruct((shards, ROWS, LANES), BF16),
            jax.ShapeDtypeStruct((INFO,), jnp.int32),
        ),
        in_specs=[SMEM, SMEM, VMEM, VMEM],
        out_specs=(VMEM, SMEM),
        compiler_params=room(24),
        cost_estimate=cost(10**9, 3 * 10**6),
        name="pack_keys",
    )(owners, sizes, indices, keys)


def slots_of(me, info_ref):
    found = [jnp.int32(-1)] * SLOTS
    seen = jnp.int32(0)
    for f in range(FITS):
        match = info_ref[OWNERS + f] == me
        for j in range(SLOTS):
            found[j] = jnp.where(match & (seen == j), f, found[j])
        seen = seen + match.astype(jnp.int32)
    return found


def layer_rows(rows, layer):
    wide = rows.astype(F32)[:, 8 * layer : 8 * layer + 8, :]
    return wide.reshape(-1, wide.shape[-1])


def attend_kernel(recv_ref, keys_ref, values_ref, out_ref):
    shards = recv_ref.shape[0]
    outs = []
    stat = jnp.zeros((shards * 8, LANES), F32)
    lane = iota(stat.shape, 1)
    for layer in range(2):
        query = layer_rows(recv_ref[...], layer).astype(BF16)
        scores = dot(query, keys_ref[layer], ((1,), (1,))) * SCALE
        peak = jnp.max(scores, axis=1, keepdims=True)
        weights = jnp.exp(scores - peak)
        total = jnp.sum(weights, axis=1, keepdims=True)
        numer = dot(weights.astype(BF16), values_ref[layer])
        outs.append((numer / total).reshape(shards, 8, HD))
        level = peak + jnp.log(total)
        high = level.astype(BF16).astype(F32)
        middle = (level - high).astype(BF16).astype(F32)
        for k, piece in enumerate((high, middle, level - high - middle)):
            stat = jnp.where(lane == 64 * layer + k, piece, stat)
    out_ref[...] = jnp.concatenate(outs + [stat.reshape(shards, 8, LANES)], axis=1).astype(BF16)


def attend(received, keys, values):
    shards = received.shape[0]
    return pl.pallas_call(
        attend_kernel,
        out_shape=jax.ShapeDtypeStruct((shards, 24, LANES), BF16),
        grid=(1,),
        in_specs=[
            pl.BlockSpec((shards, 16, LANES), lambda i: (0, ROOM // 16, 0)),
            pl.BlockSpec(keys.shape, lambda i: (0, 0, 0)),
            pl.BlockSpec(values.shape, lambda i: (0, 0, 0)),
        ],
        out_specs=pl.BlockSpec((shards, 24, LANES), lambda i: (0, 0, 0)),
        compiler_params=room(24),
        cost_estimate=cost(5 * 10**8, 3 * 10**6, 10**6),
        name="attend",
    )(received, keys, values)


def join_kernel(parts_ref, after_ref, out_ref):
    parts = parts_ref[...].astype(F32)
    stat = parts[:, 16:24, :]
    first = iota(stat.shape, 2) < 64
    level = jnp.concatenate(
        [
            jnp.sum(jnp.where(first, stat, 0.0), axis=2, keepdims=True),
            jnp.sum(jnp.where(first, 0.0, stat), axis=2, keepdims=True),
        ],
        axis=1,
    )
    weights = jnp.exp(level - jnp.max(level, axis=0, keepdims=True))
    numer = jnp.sum(weights * parts[:, 0:16, :], axis=0, keepdims=True)
    target = numer / jnp.sum(weights, axis=0, keepdims=True)
    out_ref[...] = jnp.broadcast_to(target, out_ref.shape).astype(BF16)


def join(parts, after):
    shards = parts.shape[0]
    return pl.pallas_call(
        join_kernel,
        out_shape=jax.ShapeDtypeStruct((shards, 16, LANES), BF16),
        in_specs=[VMEM, pl.BlockSpec(memory_space=pl.ANY)],
        out_specs=VMEM,
        compiler_params=room(8),
        cost_estimate=cost(10**6, 4 * 10**5, 10**3),
        name="join_parts",
    )(parts, after)


def turn_kernel(recv_ref, after_ref, out_ref):
    rows = recv_ref[:, 0:ROOM, :]
    out_ref[...] = rows.reshape(-1, HD).astype(F32).T.astype(BF16)


def turned(received, after):
    return pl.pallas_call(
        turn_kernel,
        out_shape=jax.ShapeDtypeStruct((HD, received.shape[0] * ROOM), BF16),
        in_specs=[VMEM, pl.BlockSpec(memory_space=pl.ANY)],
        out_specs=VMEM,
        compiler_params=room(8),
        cost_estimate=cost(10**6, 10**6),
        name="turn_keys",
    )(received, after)


def plan_kernel(shift, shards, info_ref, idx_ref, after_ref, dest_ref, out_ref):
    width = idx_ref.shape[1]
    me = info_ref[ME]
    fits = slots_of(me, info_ref)
    lane = iota((1, width), 1)
    source = iota((shards, width), 0)

    def shards_of(fit, size):
        place = lax.shift_right_logical(idx_ref[pl.ds(fit, 1), :], shift)
        return jnp.where(lane < size, place, -1)

    counts = []
    for f in range(FITS):
        shard = shards_of(f, info_ref[SIZES + f])
        counts.append(jnp.sum(jnp.where(shard == source, 1.0, 0.0), axis=1, keepdims=True))
    dest_ref[...] = jnp.full(dest_ref.shape, -1, jnp.int32)
    out_ref[OVER] = info_ref[OVER]
    for j in range(SLOTS):
        fit = jnp.maximum(fits[j], 0)
        size = info_ref[SIZES + fit]
        out_ref[SLOT_FIT + j] = fits[j]
        out_ref[SLOT_SIZE + j] = size
        shard = shards_of(fit, jnp.where(fits[j] >= 0, size, 0))
        first = jnp.zeros((shards, 1), F32)
        for f in range(FITS):
            ahead = (f < fit) & (info_ref[OWNERS + f] // PARTS == me // PARTS)
            first = first + counts[f] * ahead.astype(F32)
        held = jnp.where(shard == source, 1.0, 0.0)
        place, _ = running(held)
        rank = jnp.sum(held * (place - 1.0 + first), axis=0, keepdims=True).astype(jnp.int32)
        part = sum((rank >= k * ROOM).astype(jnp.int32) for k in range(1, PARTS))
        turn = (me - part) & (PARTS - 1)
        dest = shard * ROOM + rank - part * ROOM + turn * (shards * ROOM)
        dest_ref[j : j + 1, :] = jnp.where(shard >= 0, dest, -1)
        for b in range(PARTS):
            here = jnp.where((shard >= 0) & (turn == b), 1, 0)
            out_ref[USED + j * PARTS + b] = jnp.max(here)


def plan(info, indices, after, shards, shift):
    return pl.pallas_call(
        lambda *refs: plan_kernel(shift, shards, *refs),
        out_shape=(
            jax.ShapeDtypeStruct(indices.shape, jnp.int32),
            jax.ShapeDtypeStruct((INFO,), jnp.int32),
        ),
        in_specs=[SMEM, VMEM, pl.BlockSpec(memory_space=pl.ANY)],
        out_specs=(VMEM, SMEM),
        compiler_params=room(8),
        cost_estimate=cost(10**10, 10**6),
        name="plan",
    )(info, indices, after)


def build_systems(slots, info_ref, dest_ref, recv_ref, blocks, spare_ref, keys_ref, total_ref):
    width = dest_ref.shape[1]
    count = recv_ref.shape[0] * 8
    span = 256
    number = len(slots)
    eye = iota((count, count), 0) == iota((count, count), 1)
    lane = iota((1, width), 1)

    @pl.when(info_ref[OVER] == 0)
    def _():
        dest = jnp.concatenate([dest_ref[j : j + 1, :] for j in slots], axis=1)
        block = lax.shift_right_arithmetic(dest, 8)
        offset = dest & (span - 1)
        pick = jnp.where(offset == iota((span, number * width), 0), 1.0, 0.0).astype(BF16)
        total_ref[...] = jnp.zeros(total_ref.shape, F32)
        pieces = blocks[0].shape[1] // span
        for b in range(PARTS):
            used = sum(info_ref[USED + j * PARTS + b] for j in slots)

            @pl.when(used > 0)
            def _():
                stacked = jnp.concatenate(
                    [blocks[b][:, n * span : (n + 1) * span] for n in range(pieces)], axis=0
                )
                found = dot(stacked, pick)
                total = total_ref[...]
                for n in range(pieces):
                    total = jnp.where(
                        block == b * pieces + n, found[n * HD : (n + 1) * HD], total
                    )
                total_ref[...] = total

        keys_ref[...] = total_ref[...].astype(BF16)

    @pl.when(info_ref[OVER] > 0)
    def _():
        for i, j in enumerate(slots):
            pltpu.sync_copy(spare_ref.at[j], keys_ref.at[:, pl.ds(i * width, width)])

    results = []
    rows = recv_ref[:, ROOM:ROWS, :]
    layers = layer_rows(rows, 0), layer_rows(rows, 1)
    for i, j in enumerate(slots):
        live = info_ref[SLOT_FIT + j] >= 0
        size = info_ref[SLOT_SIZE + j]
        second = (info_ref[SLOT_FIT + j] >= FITS_LAYER).astype(F32)
        query = jnp.where(second > 0.5, layers[1], layers[0]).astype(BF16)
        scores = dot(query, keys_ref[:, i * width : (i + 1) * width]) * SCALE
        scores = jnp.where(lane < size, scores, -jnp.inf)
        expo = jnp.exp(scores - jnp.max(scores, axis=1, keepdims=True))
        probs = (expo / jnp.sum(expo, axis=1, keepdims=True)).astype(BF16)
        turned_probs = probs.astype(F32).T.astype(BF16)
        gram = dot(probs, turned_probs)
        trace = jnp.sum(jnp.where(eye, gram, 0.0))
        ridge = RIDGE * trace / size.astype(F32)
        top = jnp.minimum(jnp.max(jnp.sum(gram, axis=1, keepdims=True)), trace) + ridge
        taken = live.astype(F32)
        system = jnp.where(taken > 0.5, gram, 0.0) + jnp.where(
            eye, jnp.where(live, ridge, 1.0), 0.0
        )
        ends = jnp.where(live, ridge, 1.0), jnp.where(live, top, 1.0)
        results.append((system, turned_probs, ends))
    return results


def any_of(slots, info_ref):
    return functools.reduce(jnp.maximum, [info_ref[SLOT_FIT + j] for j in slots]) >= 0


def first_kernel(info_ref, dest_ref, recv_ref, *refs):
    blocks = refs[:PARTS]
    spare_ref, probs_ref, sys_ref, ends_ref, keys_ref, total_ref, held_ref, sem = refs[PARTS:]
    copy = pltpu.make_async_copy(held_ref, probs_ref.at[0], sem)
    count = sys_ref.shape[0]
    live = any_of((0,), info_ref)

    @pl.when(live)
    def _():
        ((system, probs, ends),) = build_systems(
            (0,), info_ref, dest_ref, recv_ref, blocks, spare_ref, keys_ref, total_ref
        )
        held_ref[...] = probs
        copy.start()
        sys_ref[...] = system
        ends_ref[...] = jnp.where(iota((8, LANES), 0) == 0, ends[0], ends[1])
        copy.wait()

    @pl.when(jnp.logical_not(live))
    def _():
        eye = iota((count, count), 0) == iota((count, count), 1)
        sys_ref[...] = jnp.where(eye, 1.0, 0.0)
        ends_ref[...] = jnp.full((8, LANES), 1.0, F32)


def first_system(info, dest, received, blocks, spare):
    count = received.shape[0] * 8
    return pl.pallas_call(
        first_kernel,
        out_shape=(
            pltpu.HBM((1, CMAX, count), BF16),
            jax.ShapeDtypeStruct((count, count), F32),
            jax.ShapeDtypeStruct((8, LANES), F32),
        ),
        in_specs=[SMEM] + [VMEM] * (2 + PARTS) + [pl.BlockSpec(memory_space=pl.ANY)],
        out_specs=(pl.BlockSpec(memory_space=pltpu.HBM), VMEM, VMEM),
        scratch_shapes=[
            pltpu.VMEM((HD, CMAX), BF16),
            pltpu.VMEM((HD, CMAX), F32),
            pltpu.VMEM((CMAX, count), BF16),
            pltpu.SemaphoreType.DMA(()),
        ],
        compiler_params=room(24),
        cost_estimate=cost(10**9, 3 * 10**6, 10**6),
        name="first_system",
    )(info, dest, received, *blocks, spare)


def split(x):
    high = x.astype(BF16)
    return high, (x - high.astype(F32)).astype(BF16)


def split3(x):
    high, _ = split(x)
    rest = x - high.astype(F32)
    middle, low = split(rest)
    return high, middle, low


def product(a, b):
    (a_high, a_low), (b_high, b_low) = a, b
    return dot(
        jnp.concatenate([a_high, a_high, a_low], axis=1),
        jnp.concatenate([b_high, b_low, b_high], axis=0),
    )


def product_full(a, b):
    (a0, a1, a2), (b0, b1, b2) = split3(a), split3(b)
    return dot(
        jnp.concatenate([a0, a0, a1, a0, a1, a2], axis=1),
        jnp.concatenate([b0, b1, b0, b2, b1, b0], axis=0),
    )


def other_kernel(info_ref, dest_ref, recv_ref, *refs):
    blocks = refs[:PARTS]
    spare_ref, first_ref, ends_ref, probs_ref, inverse_ref = refs[PARTS : PARTS + 5]
    keys_ref, total_ref, held_ref, sys_ref, parts_ref, out_ref, low_ref, sem, last_sem = refs[
        PARTS + 5 :
    ]
    last_copy = pltpu.make_async_copy(out_ref, inverse_ref, last_sem)
    copy = pltpu.make_async_copy(held_ref, probs_ref, sem)
    count = out_ref.shape[1]
    eye = iota((count, count), 0) == iota((count, count), 1)
    more = any_of((1, 2), info_ref)

    def start(j, system, low, high):
        middle = 2.0 / (low + high)
        sys_ref[j] = system
        out_ref[j] = middle * (jnp.where(eye, 2.0, 0.0) - middle * system)
        parts_ref[j, 0], parts_ref[j, 1] = split(system)
        ratio = (high - low) / (high + low)
        low_ref[j] = 1.0 - ratio * ratio

    @pl.when(more)
    def _():
        found = build_systems(
            (1, 2), info_ref, dest_ref, recv_ref, blocks, spare_ref, keys_ref, total_ref
        )
        for i, (system, probs, ends) in enumerate(found):
            held_ref[i] = probs
            start(i + 1, system, *ends)
        copy.start()

    start(0, first_ref[...], jnp.max(ends_ref[0:1, :]), jnp.max(ends_ref[1:2, :]))

    def step(slots, lows, last=False, full=False):
        nexts = []
        for j in slots:
            held = out_ref[j]
            middle = 2.0 / (lows[j] + 1.0)
            parts = split(held)
            if full:
                images = product_full(sys_ref[j], held)
            else:
                images = product((parts_ref[j, 0], parts_ref[j, 1]), parts)
            rest = jnp.where(eye, 1.0, 0.0) - middle * images
            if last:
                moved = dot(parts[0], rest.astype(BF16))
            else:
                moved = product(parts, split(rest))
            out_ref[j] = middle * (held + moved)
            ratio = (1.0 - lows[j]) / (1.0 + lows[j])
            nexts.append(1.0 - ratio * ratio)
        return tuple(nexts)

    def solve(slots):
        lows = tuple(low_ref[j] for j in slots)
        stiff = functools.reduce(jnp.minimum, lows) < STIFF
        lows = lax.while_loop(
            lambda lows: functools.reduce(jnp.minimum, lows) < CLOSE,
            functools.partial(step, slots),
            lows,
        )

        @pl.when(stiff)
        def _():
            step(slots, lows, full=True)

        @pl.when(jnp.logical_not(stiff))
        def _():
            step(slots, lows, last=True)

    @pl.when(more)
    def _():
        solve((0, 1, 2))
        copy.wait()

    @pl.when(jnp.logical_not(more))
    def _():
        solve((0,))

    last_copy.start()
    last_copy.wait()


def other_systems(info, dest, received, blocks, spare, first, ends):
    count = received.shape[0] * 8
    return pl.pallas_call(
        other_kernel,
        out_shape=(
            pltpu.HBM((SLOTS - 1, CMAX, count), BF16),
            pltpu.HBM((SLOTS, count, count), F32),
        ),
        in_specs=[SMEM]
        + [VMEM] * (2 + PARTS)
        + [pl.BlockSpec(memory_space=pl.ANY), VMEM, VMEM],
        out_specs=(pl.BlockSpec(memory_space=pltpu.HBM), pl.BlockSpec(memory_space=pltpu.HBM)),
        scratch_shapes=[
            pltpu.VMEM((HD, 2 * CMAX), BF16),
            pltpu.VMEM((HD, 2 * CMAX), F32),
            pltpu.VMEM((SLOTS - 1, CMAX, count), BF16),
            pltpu.VMEM((SLOTS, count, count), F32),
            pltpu.VMEM((SLOTS, 2, count, count), BF16),
            pltpu.VMEM((SLOTS, count, count), F32),
            pltpu.SMEM((SLOTS,), F32),
            pltpu.SemaphoreType.DMA(()),
            pltpu.SemaphoreType.DMA(()),
        ],
        compiler_params=room(32),
        cost_estimate=cost(8 * 10**9, 4 * 10**6, 10**6),
        name="other_systems",
    )(info, dest, received, *blocks, spare, first, ends)


def values_kernel(
    info_ref, target_ref, inverse_ref, first_ref, probs_ref, out_ref, inv, held, result, sems
):
    fits = [info_ref[SLOT_FIT + j] for j in range(SLOTS)]

    def copies(j):
        source = first_ref.at[0] if j == 0 else probs_ref.at[j - 1]
        return (
            pltpu.make_async_copy(inverse_ref.at[j], inv.at[j], sems.at[0, j]),
            pltpu.make_async_copy(source, held.at[j], sems.at[1, j]),
        )

    def copy_out(j):
        return pltpu.make_async_copy(result.at[j], out_ref.at[0, j], sems.at[2, j])

    for j in range(SLOTS):

        @pl.when(fits[j] >= 0)
        def _():
            for copy in copies(j):
                copy.start()

    for j in range(SLOTS):

        @pl.when(fits[j] < 0)
        def _():
            result[j] = jnp.zeros(result.shape[1:], BF16)
            copy_out(j).start()

    for j in range(SLOTS):

        @pl.when(fits[j] >= 0)
        def _():
            rows = target_ref[...]
            first_rows, second_rows = layer_rows(rows, 0), layer_rows(rows, 1)
            second = (fits[j] >= FITS_LAYER).astype(F32)
            target = jnp.where(second > 0.5, second_rows, first_rows).astype(BF16)
            for copy in copies(j):
                copy.wait()
            weights = dot(
                jnp.concatenate(split3(inv[j]), axis=1),
                jnp.concatenate([target] * 3, axis=0),
            )
            high, low = split(weights)
            probs = held[j]
            result[j] = dot(
                jnp.concatenate([probs, probs], axis=1), jnp.concatenate([high, low], axis=0)
            ).astype(BF16)
            copy_out(j).start()

    for j in range(SLOTS):
        copy_out(j).wait()


def fitted_values(info, inverse, first, probs, target):
    anywhere = pl.BlockSpec(memory_space=pltpu.HBM)
    count = inverse.shape[1]
    return pl.pallas_call(
        values_kernel,
        out_shape=pltpu.HBM((1, SLOTS, CMAX, HD), BF16),
        in_specs=[SMEM, VMEM, anywhere, anywhere, anywhere],
        out_specs=pl.BlockSpec(memory_space=pltpu.HBM),
        scratch_shapes=[
            pltpu.VMEM((SLOTS, count, count), F32),
            pltpu.VMEM((SLOTS, CMAX, count), BF16),
            pltpu.VMEM((SLOTS, CMAX, HD), BF16),
            pltpu.SemaphoreType.DMA((3, SLOTS)),
        ],
        compiler_params=room(16),
        cost_estimate=cost(10**9, 4 * 10**6),
        name="fitted_values",
    )(info, target, inverse, first, probs)


def exchange(blocks):
    return lax.all_to_all(blocks, SEQ, split_axis=0, concat_axis=0, tiled=True)


def gathered_keys(owners, indices, keys):
    layers, local, width = keys.shape
    shards = lax.axis_size(SEQ)
    me = lax.axis_index(SEQ)
    fits = indices.shape[0]
    fit_ids = jnp.arange(fits, dtype=jnp.int32)
    offset = indices - me * local
    inside = (offset >= 0) & (offset < local)
    source = (fit_ids // FITS_LAYER)[:, None] * local + jnp.clip(offset, 0, local - 1)
    picked = jnp.take(keys.reshape(layers * local, width), source, axis=0)
    found = jnp.where(inside[..., None], picked, jnp.zeros((), picked.dtype))
    ring = [(k, (k + 1) % shards) for k in range(shards)]

    def pass_on(_, carried):
        moving, whole = carried
        moving = lax.ppermute(moving, SEQ, ring)
        return moving, whole + moving

    _, everything = lax.fori_loop(0, shards - 1, pass_on, (found, found))
    mine = owners[0] == me
    earlier = jnp.sum(
        jnp.where(mine[None, :] & (fit_ids[:, None] > fit_ids[None, :]), 1, 0), axis=1
    )
    chosen = [
        everything[jnp.sum(jnp.where(mine & (earlier == slot), fit_ids, 0))]
        for slot in range(SLOTS)
    ]
    return jnp.swapaxes(jnp.stack(chosen), 1, 2)


def on_device(queries, keys, values, indices, sizes, owners):
    layers, _, local, width = keys.shape
    key_rows = keys.reshape(layers, local, width)
    value_rows = values.reshape(layers, local, width)
    positions = indices[0]
    shards = lax.axis_size(SEQ)
    regrouped = lax.all_to_all(queries, "head", split_axis=1, concat_axis=2, tiled=True)
    own_rows = regrouped.reshape(1, 16, width)
    packed, info = pack_keys(owners, sizes, positions, key_rows, shards)
    packed = lax.dynamic_update_slice(
        packed, jnp.broadcast_to(own_rows, (shards, 16, width)), (0, ROOM, 0)
    )
    received = exchange(packed)
    spare = lax.cond(
        info[OVER] > 0,
        lambda: gathered_keys(owners, positions, key_rows),
        lambda: jnp.zeros((SLOTS, width, CMAX), BF16),
    )
    dest, owned = plan(info, positions, spare, shards, local.bit_length() - 1)
    own_block = turned(received, dest)
    blocks = [own_block] + [
        lax.ppermute(own_block, "seq_1", [(k, (k + d) % PARTS) for k in range(PARTS)])
        for d in range(1, PARTS)
    ]
    parts = exchange(attend(received, key_rows, value_rows))
    first_probs, first, ends = first_system(owned, dest, received, blocks, spare)
    target = exchange(join(parts, first))
    probs, inverse = other_systems(owned, dest, received, blocks, spare, first, ends)
    return fitted_values(owned, inverse, first_probs, probs, target)


def solution(mesh):
    apart = Mesh(mesh.devices.reshape(mesh.shape["head"], 8, 4), ("head", "seq_0", "seq_1"))
    placed = (
        P(None, None, HEAD_SEQ, None),
        P(None, "head", SEQ, None),
        P(None, "head", SEQ, None),
        P("head", None, None),
        P("head", None),
        P("head", None),
    )
    return jax.shard_map(
        on_device,
        mesh=apart,
        in_specs=placed,
        out_specs=P("head", SEQ, None, None),
        check_vma=False,
    )
```

```python
import functools

import jax
import jax.numpy as jnp
from jax import lax
from jax.experimental import pallas as pl
from jax.experimental.pallas import tpu as pltpu
from jax.sharding import Mesh
from jax.sharding import PartitionSpec as P

FITS = 8
FITS_LAYER = 4
SLOTS = 3
CMAX = 1024
HD = 128
LANES = 128
ROOM = 48
ROWS = ROOM + 16
PARTS = 4
CLOSE = 0.97
STIFF = 0.004
RIDGE = 0.3
DEALT = (0, 1, 3, 2)
OVER, ME, OWNERS, SIZES, INFO = 0, 1, 2, 10, 32
SLOT_FIT, SLOT_SIZE, USED = 1, 4, 8
SCALE = HD ** (-0.5)
SEQ = ("seq_0", "seq_1")
HEAD_SEQ = ("head", "seq_0", "seq_1")
F32 = jnp.float32
BF16 = jnp.bfloat16


def room(mib):
    return pltpu.CompilerParams(vmem_limit_bytes=mib << 20)


SMEM = pl.BlockSpec(memory_space=pltpu.SMEM)
VMEM = pl.BlockSpec(memory_space=pltpu.VMEM)


def cost(flops, moved, exps=0):
    return pl.CostEstimate(flops=flops, transcendentals=exps, bytes_accessed=moved)


def iota(shape, dim):
    return lax.broadcasted_iota(jnp.int32, shape, dim)


def fiota(shape, dim):
    return iota(shape, dim).astype(F32)


def dot(a, b, dims=((1,), (0,))):
    return lax.dot_general(a, b, (dims, ((), ())), preferred_element_type=F32)


def running(mask):
    rows, width = mask.shape
    blocks = width // LANES
    upper = (iota((LANES, LANES), 0) <= iota((LANES, LANES), 1)).astype(BF16)
    stacked = jnp.concatenate(
        [mask[:, b * LANES : (b + 1) * LANES] for b in range(blocks)], axis=0
    )
    inner = dot(stacked.astype(BF16), upper)
    carry = jnp.zeros((rows, 1), F32)
    parts = []
    for b in range(blocks):
        part = inner[b * rows : (b + 1) * rows]
        parts.append(part + carry)
        carry = carry + part[:, LANES - 1 : LANES]
    return jnp.concatenate(parts, axis=1), carry


def heaviest(owner_of):
    owners = [owner_of(f) for f in range(FITS)]
    number = [sum((a == b).astype(jnp.int32) for b in owners) for a in owners]
    places = []
    for f in range(FITS):
        best, place = jnp.int32(0), jnp.int32(0)
        for g in range(FITS):
            better = (owners[g] // PARTS == owners[f] // PARTS) & (number[g] > best)
            best = jnp.where(better, number[g], best)
            place = jnp.where(better, owners[g] & (PARTS - 1), place)
        places.append(place)
    return places


def send_kernel(shards, own_ref, size_ref, idx_ref, keys_ref, send_ref, info_ref):
    me = lax.axis_index(SEQ).astype(jnp.int32)
    local = keys_ref.shape[1]
    shift = local.bit_length() - 1
    fits, width = idx_ref.shape
    idx = idx_ref[...]
    row = iota((fits, width), 0)
    lane = iota((fits, width), 1)
    size = jnp.zeros((fits, width), jnp.int32)
    own = jnp.zeros((fits, LANES), jnp.int32)
    row1 = iota((fits, LANES), 0)
    lane1 = iota((fits, LANES), 1)
    for f in range(fits):
        size = jnp.where(row == f, size_ref[0, f], size)
        own = jnp.where(row1 == f, own_ref[0, f] // PARTS, own)
    shard = jnp.where(lane < size, lax.shift_right_logical(idx, shift), -1)
    counts = jnp.zeros((fits, LANES), F32)
    for s in range(shards):
        count = jnp.sum(jnp.where(shard == s, 1.0, 0.0), axis=1, keepdims=True)
        counts = jnp.where(lane1 == s, count, counts)
    total = jnp.zeros((fits, LANES), F32)
    before = jnp.zeros((fits, LANES), F32)
    for f in range(fits):
        shared = jnp.where(own == own_ref[0, f] // PARTS, counts[f : f + 1, :], 0.0)
        total = total + shared
        before = before + jnp.where(row1 > f, shared, 0.0)
    info_ref[OVER] = (jnp.max(total) > PARTS * ROOM).astype(jnp.int32)
    info_ref[ME] = me
    for f in range(fits):
        info_ref[OWNERS + f] = own_ref[0, f]
        info_ref[SIZES + f] = size_ref[0, f]
    first = jnp.sum(jnp.where(lane1 == me, before, 0.0), axis=1, keepdims=True)
    mine = shard == me
    held = jnp.where(mine, 1.0, 0.0)
    place, _ = running(held)
    place = jnp.where(mine, place - 1.0 + first, -1.0)
    spot = jnp.where(mine, idx - me * local + 1, 0).astype(F32)
    send_ref[...] = jnp.zeros(send_ref.shape, BF16)
    slot = fiota((PARTS * ROOM, width), 0)
    at = fiota((PARTS * ROOM, local), 1)
    middle = heaviest(lambda f: own_ref[0, f])
    for f in range(fits):
        here = place[f : f + 1, :] == slot
        pos = jnp.sum(jnp.where(here, spot[f : f + 1, :], 0.0), axis=1, keepdims=True) - 1.0
        pick = jnp.where(pos == at, 1.0, 0.0).astype(BF16)
        rows = dot(pick, keys_ref[f // FITS_LAYER])
        rows = rows.astype(BF16)
        to = own_ref[0, f] // PARTS * PARTS
        for part, step in enumerate(DEALT):
            place_along = (middle[f] + step) & (PARTS - 1)
            send_ref[to + place_along, 0:ROOM, :] += rows[part * ROOM : (part + 1) * ROOM]


def pack_keys(owners, sizes, indices, keys, shards):
    return pl.pallas_call(
        lambda *refs: send_kernel(shards, *refs),
        out_shape=(
            jax.ShapeDtypeStruct((shards, ROWS, LANES), BF16),
            jax.ShapeDtypeStruct((INFO,), jnp.int32),
        ),
        in_specs=[SMEM, SMEM, VMEM, VMEM],
        out_specs=(VMEM, SMEM),
        compiler_params=room(24),
        cost_estimate=cost(10**9, 3 * 10**6),
        name="pack_keys",
    )(owners, sizes, indices, keys)


def slots_of(me, info_ref):
    found = [jnp.int32(-1)] * SLOTS
    seen = jnp.int32(0)
    for f in range(FITS):
        match = info_ref[OWNERS + f] == me
        for j in range(SLOTS):
            found[j] = jnp.where(match & (seen == j), f, found[j])
        seen = seen + match.astype(jnp.int32)
    return found


def layer_rows(rows, layer):
    wide = rows.astype(F32)[:, 8 * layer : 8 * layer + 8, :]
    return wide.reshape(-1, wide.shape[-1])


def attend_kernel(recv_ref, keys_ref, values_ref, out_ref):
    shards = recv_ref.shape[0]
    outs = []
    stat = jnp.zeros((shards * 8, LANES), F32)
    lane = iota(stat.shape, 1)
    for layer in range(2):
        query = layer_rows(recv_ref[...], layer).astype(BF16)
        scores = dot(query, keys_ref[layer], ((1,), (1,))) * SCALE
        peak = jnp.max(scores, axis=1, keepdims=True)
        weights = jnp.exp(scores - peak)
        total = jnp.sum(weights, axis=1, keepdims=True)
        numer = dot(weights.astype(BF16), values_ref[layer])
        outs.append((numer / total).reshape(shards, 8, HD))
        level = peak + jnp.log(total)
        high = level.astype(BF16).astype(F32)
        middle = (level - high).astype(BF16).astype(F32)
        for k, piece in enumerate((high, middle, level - high - middle)):
            stat = jnp.where(lane == 64 * layer + k, piece, stat)
    out_ref[...] = jnp.concatenate(outs + [stat.reshape(shards, 8, LANES)], axis=1).astype(BF16)


def attend(received, keys, values):
    shards = received.shape[0]
    return pl.pallas_call(
        attend_kernel,
        out_shape=jax.ShapeDtypeStruct((shards, 24, LANES), BF16),
        grid=(1,),
        in_specs=[
            pl.BlockSpec((shards, 16, LANES), lambda i: (0, ROOM // 16, 0)),
            pl.BlockSpec(keys.shape, lambda i: (0, 0, 0)),
            pl.BlockSpec(values.shape, lambda i: (0, 0, 0)),
        ],
        out_specs=pl.BlockSpec((shards, 24, LANES), lambda i: (0, 0, 0)),
        compiler_params=room(24),
        cost_estimate=cost(5 * 10**8, 3 * 10**6, 10**6),
        name="attend",
    )(received, keys, values)


def join_kernel(parts_ref, after_ref, out_ref):
    parts = parts_ref[...].astype(F32)
    stat = parts[:, 16:24, :]
    first = iota(stat.shape, 2) < 64
    level = jnp.concatenate(
        [
            jnp.sum(jnp.where(first, stat, 0.0), axis=2, keepdims=True),
            jnp.sum(jnp.where(first, 0.0, stat), axis=2, keepdims=True),
        ],
        axis=1,
    )
    weights = jnp.exp(level - jnp.max(level, axis=0, keepdims=True))
    numer = jnp.sum(weights * parts[:, 0:16, :], axis=0, keepdims=True)
    target = numer / jnp.sum(weights, axis=0, keepdims=True)
    out_ref[...] = jnp.broadcast_to(target, out_ref.shape).astype(BF16)


def join(parts, after):
    shards = parts.shape[0]
    return pl.pallas_call(
        join_kernel,
        out_shape=jax.ShapeDtypeStruct((shards, 16, LANES), BF16),
        in_specs=[VMEM, pl.BlockSpec(memory_space=pl.ANY)],
        out_specs=VMEM,
        compiler_params=room(8),
        cost_estimate=cost(10**6, 4 * 10**5, 10**3),
        name="join_parts",
    )(parts, after)


def turn_kernel(recv_ref, after_ref, out_ref):
    rows = recv_ref[:, 0:ROOM, :]
    out_ref[...] = rows.reshape(-1, HD).astype(F32).T.astype(BF16)


def turned(received, after):
    return pl.pallas_call(
        turn_kernel,
        out_shape=jax.ShapeDtypeStruct((HD, received.shape[0] * ROOM), BF16),
        in_specs=[VMEM, pl.BlockSpec(memory_space=pl.ANY)],
        out_specs=VMEM,
        compiler_params=room(8),
        cost_estimate=cost(10**6, 10**6),
        name="turn_keys",
    )(received, after)


def plan_kernel(shift, shards, info_ref, idx_ref, after_ref, dest_ref, out_ref):
    width = idx_ref.shape[1]
    me = info_ref[ME]
    fits = slots_of(me, info_ref)
    lane = iota((1, width), 1)
    source = iota((shards, width), 0)

    def shards_of(fit, size):
        place = lax.shift_right_logical(idx_ref[pl.ds(fit, 1), :], shift)
        return jnp.where(lane < size, place, -1)

    middle = heaviest(lambda f: info_ref[OWNERS + f])
    counts = []
    for f in range(FITS):
        shard = shards_of(f, info_ref[SIZES + f])
        counts.append(jnp.sum(jnp.where(shard == source, 1.0, 0.0), axis=1, keepdims=True))
    dest_ref[...] = jnp.full(dest_ref.shape, -1, jnp.int32)
    out_ref[OVER] = info_ref[OVER]
    for j in range(SLOTS):
        fit = jnp.maximum(fits[j], 0)
        size = info_ref[SIZES + fit]
        out_ref[SLOT_FIT + j] = fits[j]
        out_ref[SLOT_SIZE + j] = size
        shard = shards_of(fit, jnp.where(fits[j] >= 0, size, 0))
        first = jnp.zeros((shards, 1), F32)
        for f in range(FITS):
            ahead = (f < fit) & (info_ref[OWNERS + f] // PARTS == me // PARTS)
            first = first + counts[f] * ahead.astype(F32)
        held = jnp.where(shard == source, 1.0, 0.0)
        place, _ = running(held)
        rank = jnp.sum(held * (place - 1.0 + first), axis=0, keepdims=True).astype(jnp.int32)
        part = sum((rank >= k * ROOM).astype(jnp.int32) for k in range(1, PARTS))
        center = sum(jnp.where(fit == f, middle[f], 0) for f in range(FITS))
        step = jnp.full(part.shape, DEALT[0], jnp.int32)
        for k in range(1, PARTS):
            step = jnp.where(part == k, DEALT[k], step)
        turn = (me - center - step) & (PARTS - 1)
        dest = shard * ROOM + rank - part * ROOM + turn * (shards * ROOM)
        dest_ref[j : j + 1, :] = jnp.where(shard >= 0, dest, -1)
        for b in range(PARTS):
            here = jnp.where((shard >= 0) & (turn == b), 1, 0)
            out_ref[USED + j * PARTS + b] = jnp.max(here)


def plan(info, indices, after, shards, shift):
    return pl.pallas_call(
        lambda *refs: plan_kernel(shift, shards, *refs),
        out_shape=(
            jax.ShapeDtypeStruct(indices.shape, jnp.int32),
            jax.ShapeDtypeStruct((INFO,), jnp.int32),
        ),
        in_specs=[SMEM, VMEM, pl.BlockSpec(memory_space=pl.ANY)],
        out_specs=(VMEM, SMEM),
        compiler_params=room(8),
        cost_estimate=cost(10**10, 10**6),
        name="plan",
    )(info, indices, after)


def any_of(slots, info_ref):
    return functools.reduce(jnp.maximum, [info_ref[SLOT_FIT + j] for j in slots]) >= 0


def add_found(slots, turns, blocks, info_ref, dest_ref, total_ref):
    span = 256
    width = dest_ref.shape[1]
    columns = slice(slots[0] * width, (slots[-1] + 1) * width)
    dest = jnp.concatenate([dest_ref[j : j + 1, :] for j in slots], axis=1)
    block = lax.shift_right_arithmetic(dest, 8)
    offset = dest & (span - 1)
    for b, block_ref in zip(turns, blocks):
        used = sum(info_ref[USED + j * PARTS + b] for j in slots)

        @pl.when(used > 0)
        def _():
            pick = jnp.where(offset == iota((span, offset.shape[1]), 0), 1.0, 0.0).astype(BF16)
            pieces = block_ref.shape[1] // span
            stacked = jnp.concatenate(
                [block_ref[:, n * span : (n + 1) * span] for n in range(pieces)], axis=0
            )
            found = dot(stacked, pick)
            total = total_ref[:, columns]
            for n in range(pieces):
                total = jnp.where(block == b * pieces + n, found[n * HD : (n + 1) * HD], total)
            total_ref[:, columns] = total


def order_kernel(info_ref, dest_ref, *refs):
    blocks, (out_ref, total_ref) = refs[: PARTS - 1], refs[PARTS - 1 :]
    width = dest_ref.shape[1]
    turns = (0, 1, PARTS - 1)
    total_ref[...] = jnp.zeros(total_ref.shape, F32)
    more = any_of((1, 2), info_ref)

    @pl.when(more)
    def _():
        add_found((0, 1, 2), turns, blocks, info_ref, dest_ref, total_ref)
        out_ref[...] = total_ref[...].astype(BF16)

    @pl.when(jnp.logical_not(more))
    def _():
        add_found((0,), turns, blocks, info_ref, dest_ref, total_ref)
        out_ref[...] = total_ref[...].astype(BF16)


def ordered(info, dest, blocks):
    return pl.pallas_call(
        order_kernel,
        out_shape=jax.ShapeDtypeStruct((HD, SLOTS * CMAX), BF16),
        in_specs=[SMEM] + [VMEM] * PARTS,
        out_specs=VMEM,
        scratch_shapes=[pltpu.VMEM((HD, SLOTS * CMAX), F32)],
        compiler_params=room(24),
        cost_estimate=cost(4 * 10**9, 3 * 10**6),
        name="order_keys",
    )(info, dest, *blocks)


def build_systems(slots, info_ref, recv_ref, keys_ref):
    count = recv_ref.shape[0] * 8
    width = CMAX
    eye = iota((count, count), 0) == iota((count, count), 1)
    lane = iota((1, width), 1)
    results = []
    rows = recv_ref[:, ROOM:ROWS, :]
    layers = layer_rows(rows, 0), layer_rows(rows, 1)
    for j in slots:
        live = info_ref[SLOT_FIT + j] >= 0
        size = info_ref[SLOT_SIZE + j]
        second = (info_ref[SLOT_FIT + j] >= FITS_LAYER).astype(F32)
        query = jnp.where(second > 0.5, layers[1], layers[0]).astype(BF16)
        scores = dot(query, keys_ref[:, j * width : (j + 1) * width]) * SCALE
        scores = jnp.where(lane < size, scores, -jnp.inf)
        expo = jnp.exp(scores - jnp.max(scores, axis=1, keepdims=True))
        probs = (expo / jnp.sum(expo, axis=1, keepdims=True)).astype(BF16)
        turned_probs = probs.astype(F32).T.astype(BF16)
        gram = dot(probs, turned_probs)
        trace = jnp.sum(jnp.where(eye, gram, 0.0))
        ridge = RIDGE * trace / size.astype(F32)
        top = jnp.minimum(jnp.max(jnp.sum(gram, axis=1, keepdims=True)), trace) + ridge
        taken = live.astype(F32)
        system = jnp.where(taken > 0.5, gram, 0.0) + jnp.where(
            eye, jnp.where(live, ridge, 1.0), 0.0
        )
        ends = jnp.where(live, ridge, 1.0), jnp.where(live, top, 1.0)
        results.append((system, turned_probs, ends))
    return results


def system_kernel(
    info_ref, dest_ref, recv_ref, block_ref, part_ref, spare_ref, probs_ref, sys_ref, ends_ref,
    keys_ref, total_ref, held_ref, sems
):
    count = sys_ref.shape[1]
    width = dest_ref.shape[1]
    eye = iota((count, count), 0) == iota((count, count), 1)
    opposite = PARTS // 2
    far = sum(info_ref[USED + j * PARTS + opposite] for j in range(SLOTS))
    keys_ref[...] = part_ref[...]

    @pl.when((info_ref[OVER] == 0) & (far > 0))
    def _():
        total_ref[...] = part_ref[...].astype(F32)
        add_found((0, 1, 2), (opposite,), (block_ref,), info_ref, dest_ref, total_ref)
        keys_ref[...] = total_ref[...].astype(BF16)

    @pl.when(info_ref[OVER] > 0)
    def _():
        for j in range(SLOTS):
            pltpu.sync_copy(spare_ref.at[j], keys_ref.at[:, pl.ds(j * width, width)])

    def copy(j):
        return pltpu.make_async_copy(held_ref.at[j], probs_ref.at[j], sems.at[j])

    def fill(slots):
        live = any_of(slots, info_ref)

        @pl.when(live)
        def _():
            found = build_systems(slots, info_ref, recv_ref, keys_ref)
            for j, (system, probs, ends) in zip(slots, found):
                held_ref[j] = probs
                copy(j).start()
                sys_ref[j] = system
                ends_ref[j] = jnp.where(iota((8, LANES), 0) == 0, ends[0], ends[1])

        @pl.when(jnp.logical_not(live))
        def _():
            for j in slots:
                sys_ref[j] = jnp.where(eye, 1.0, 0.0)
                ends_ref[j] = jnp.full((8, LANES), 1.0, F32)

    groups = (0,), (1, 2)
    for slots in groups:
        fill(slots)
    for slots in groups:

        @pl.when(any_of(slots, info_ref))
        def _():
            for j in slots:
                copy(j).wait()


def systems(info, dest, received, block, part, spare):
    count = received.shape[0] * 8
    return pl.pallas_call(
        system_kernel,
        out_shape=(
            pltpu.HBM((SLOTS, CMAX, count), BF16),
            jax.ShapeDtypeStruct((SLOTS, count, count), F32),
            jax.ShapeDtypeStruct((SLOTS, 8, LANES), F32),
        ),
        in_specs=[SMEM] + [VMEM] * 4 + [pl.BlockSpec(memory_space=pltpu.HBM)],
        out_specs=(pl.BlockSpec(memory_space=pltpu.HBM), VMEM, VMEM),
        scratch_shapes=[
            pltpu.VMEM((HD, SLOTS * CMAX), BF16),
            pltpu.VMEM((HD, SLOTS * CMAX), F32),
            pltpu.VMEM((SLOTS, CMAX, count), BF16),
            pltpu.SemaphoreType.DMA((SLOTS,)),
        ],
        compiler_params=room(32),
        cost_estimate=cost(3 * 10**9, 3 * 10**6, 10**6),
        name="systems",
    )(info, dest, received, block, part, pltpu.with_memory_space_constraint(spare, pltpu.HBM))


def split(x):
    high = x.astype(BF16)
    return high, (x - high.astype(F32)).astype(BF16)


def split3(x):
    high, _ = split(x)
    rest = x - high.astype(F32)
    middle, low = split(rest)
    return high, middle, low


def product(a, b):
    (a_high, a_low), (b_high, b_low) = a, b
    return dot(
        jnp.concatenate([a_high, a_high, a_low], axis=1),
        jnp.concatenate([b_high, b_low, b_high], axis=0),
    )


def product_full(a, b):
    (a0, a1, a2), (b0, b1, b2) = split3(a), split3(b)
    return dot(
        jnp.concatenate([a0, a0, a1, a0, a1, a2], axis=1),
        jnp.concatenate([b0, b1, b0, b2, b1, b0], axis=0),
    )


def invert_kernel(info_ref, sys_ref, ends_ref, inverse_ref, parts_ref, out_ref, low_ref, sem):
    count = sys_ref.shape[1]
    eye = iota((count, count), 0) == iota((count, count), 1)
    more = any_of((1, 2), info_ref)
    copy = pltpu.make_async_copy(out_ref, inverse_ref, sem)

    def start(slots):
        lows = []
        for j in slots:
            low = jnp.max(ends_ref[j, 0:1, :])
            high = jnp.max(ends_ref[j, 1:2, :])
            middle = 2.0 / (low + high)
            system = sys_ref[j]
            out_ref[j] = middle * (jnp.where(eye, 2.0, 0.0) - middle * system)
            parts_ref[j, 0], parts_ref[j, 1] = split(system)
            ratio = (high - low) / (high + low)
            lows.append(1.0 - ratio * ratio)
        return tuple(lows)

    def step(slots, lows, last=False, full=False):
        nexts = []
        for j, lowest in zip(slots, lows):
            held = out_ref[j]
            middle = 2.0 / (lowest + 1.0)
            parts = split(held)
            if full:
                images = product_full(sys_ref[j], held)
            else:
                images = product((parts_ref[j, 0], parts_ref[j, 1]), parts)
            rest = jnp.where(eye, 1.0, 0.0) - middle * images
            if last:
                moved = dot(parts[0], rest.astype(BF16))
            else:
                moved = product(parts, split(rest))
            out_ref[j] = middle * (held + moved)
            ratio = (1.0 - lowest) / (1.0 + lowest)
            nexts.append(1.0 - ratio * ratio)
        return tuple(nexts)

    def solve(slots):
        lows = start(slots)
        stiff = functools.reduce(jnp.minimum, lows) < STIFF
        lows = lax.while_loop(
            lambda lows: functools.reduce(jnp.minimum, lows) < CLOSE,
            functools.partial(step, slots),
            lows,
        )

        @pl.when(stiff)
        def _():
            step(slots, lows, full=True)

        @pl.when(jnp.logical_not(stiff))
        def _():
            step(slots, lows, last=True)

    @pl.when(more)
    def _():
        solve((0, 1, 2))

    @pl.when(jnp.logical_not(more))
    def _():
        solve((0,))

    copy.start()
    copy.wait()


def invert(info, system, ends):
    return pl.pallas_call(
        invert_kernel,
        out_shape=pltpu.HBM(system.shape, F32),
        in_specs=[SMEM, VMEM, VMEM],
        out_specs=pl.BlockSpec(memory_space=pltpu.HBM),
        scratch_shapes=[
            pltpu.VMEM((SLOTS, 2, *system.shape[1:]), BF16),
            pltpu.VMEM(system.shape, F32),
            pltpu.SMEM((SLOTS,), F32),
            pltpu.SemaphoreType.DMA(()),
        ],
        compiler_params=room(16),
        cost_estimate=cost(5 * 10**9, 2 * 10**6),
        name="invert",
    )(info, system, ends)


def values_kernel(
    info_ref, target_ref, inverse_ref, probs_ref, out_ref, inv, held, result, sems
):
    fits = [info_ref[SLOT_FIT + j] for j in range(SLOTS)]

    def copies(j):
        return (
            pltpu.make_async_copy(inverse_ref.at[j], inv.at[j], sems.at[0, j]),
            pltpu.make_async_copy(probs_ref.at[j], held.at[j], sems.at[1, j]),
        )

    def copy_out(j):
        return pltpu.make_async_copy(result.at[j], out_ref.at[0, j], sems.at[2, j])

    for j in range(SLOTS):

        @pl.when(fits[j] >= 0)
        def _():
            for copy in copies(j):
                copy.start()

    for j in range(SLOTS):

        @pl.when(fits[j] < 0)
        def _():
            result[j] = jnp.zeros(result.shape[1:], BF16)
            copy_out(j).start()

    for j in range(SLOTS):

        @pl.when(fits[j] >= 0)
        def _():
            rows = target_ref[...]
            first_rows, second_rows = layer_rows(rows, 0), layer_rows(rows, 1)
            second = (fits[j] >= FITS_LAYER).astype(F32)
            target = jnp.where(second > 0.5, second_rows, first_rows).astype(BF16)
            for copy in copies(j):
                copy.wait()
            weights = dot(
                jnp.concatenate(split3(inv[j]), axis=1),
                jnp.concatenate([target] * 3, axis=0),
            )
            high, low = split(weights)
            probs = held[j]
            result[j] = dot(
                jnp.concatenate([probs, probs], axis=1), jnp.concatenate([high, low], axis=0)
            ).astype(BF16)
            copy_out(j).start()

    for j in range(SLOTS):
        copy_out(j).wait()


def fitted_values(info, inverse, probs, target):
    anywhere = pl.BlockSpec(memory_space=pltpu.HBM)
    count = inverse.shape[1]
    return pl.pallas_call(
        values_kernel,
        out_shape=pltpu.HBM((1, SLOTS, CMAX, HD), BF16),
        in_specs=[SMEM, VMEM, anywhere, anywhere],
        out_specs=pl.BlockSpec(memory_space=pltpu.HBM),
        scratch_shapes=[
            pltpu.VMEM((SLOTS, count, count), F32),
            pltpu.VMEM((SLOTS, CMAX, count), BF16),
            pltpu.VMEM((SLOTS, CMAX, HD), BF16),
            pltpu.SemaphoreType.DMA((3, SLOTS)),
        ],
        compiler_params=room(16),
        cost_estimate=cost(10**9, 4 * 10**6),
        name="fitted_values",
    )(
        info,
        target,
        pltpu.with_memory_space_constraint(inverse, pltpu.HBM),
        pltpu.with_memory_space_constraint(probs, pltpu.HBM),
    )


def exchange(blocks):
    return lax.all_to_all(blocks, SEQ, split_axis=0, concat_axis=0, tiled=True)


def gathered_keys(owners, indices, keys):
    layers, local, width = keys.shape
    shards = lax.axis_size(SEQ)
    me = lax.axis_index(SEQ)
    fits = indices.shape[0]
    fit_ids = jnp.arange(fits, dtype=jnp.int32)
    offset = indices - me * local
    inside = (offset >= 0) & (offset < local)
    source = (fit_ids // FITS_LAYER)[:, None] * local + jnp.clip(offset, 0, local - 1)
    picked = jnp.take(keys.reshape(layers * local, width), source, axis=0)
    found = jnp.where(inside[..., None], picked, jnp.zeros((), picked.dtype))
    ring = [(k, (k + 1) % shards) for k in range(shards)]

    def pass_on(_, carried):
        moving, whole = carried
        moving = lax.ppermute(moving, SEQ, ring)
        return moving, whole + moving

    _, everything = lax.fori_loop(0, shards - 1, pass_on, (found, found))
    mine = owners[0] == me
    earlier = jnp.sum(
        jnp.where(mine[None, :] & (fit_ids[:, None] > fit_ids[None, :]), 1, 0), axis=1
    )
    chosen = [
        everything[jnp.sum(jnp.where(mine & (earlier == slot), fit_ids, 0))]
        for slot in range(SLOTS)
    ]
    return jnp.swapaxes(jnp.stack(chosen), 1, 2)


def on_device(queries, keys, values, indices, sizes, owners):
    layers, _, local, width = keys.shape
    key_rows = keys.reshape(layers, local, width)
    value_rows = values.reshape(layers, local, width)
    positions = indices[0]
    shards = lax.axis_size(SEQ)
    regrouped = lax.all_to_all(queries, "head", split_axis=1, concat_axis=2, tiled=True)
    own_rows = regrouped.reshape(1, 16, width)
    packed, info = pack_keys(owners, sizes, positions, key_rows, shards)
    packed = lax.dynamic_update_slice(
        packed, jnp.broadcast_to(own_rows, (shards, 16, width)), (0, ROOM, 0)
    )
    received = exchange(packed)
    spare = lax.cond(
        info[OVER] > 0,
        lambda: gathered_keys(owners, positions, key_rows),
        lambda: jnp.zeros((SLOTS, width, CMAX), BF16),
    )
    dest, owned = plan(info, positions, spare, shards, local.bit_length() - 1)
    own_block = turned(received, dest)
    near, back, far = (
        lax.ppermute(own_block, "seq_1", [(k, (k + d) % PARTS) for k in range(PARTS)])
        for d in (1, PARTS - 1, PARTS // 2)
    )
    parts = exchange(attend(received, key_rows, value_rows))
    ordering = ordered(owned, dest, (own_block, near, back))
    probs, system, ends = systems(owned, dest, received, far, ordering, spare)
    target = exchange(join(parts, system))
    inverse = invert(owned, system, ends)
    return fitted_values(owned, inverse, probs, target)


def solution(mesh):
    apart = Mesh(mesh.devices.reshape(mesh.shape["head"], 8, 4), ("head", "seq_0", "seq_1"))
    placed = (
        P(None, None, HEAD_SEQ, None),
        P(None, "head", SEQ, None),
        P(None, "head", SEQ, None),
        P("head", None, None),
        P("head", None),
        P("head", None),
    )
    return jax.shard_map(
        on_device,
        mesh=apart,
        in_specs=placed,
        out_specs=P("head", SEQ, None, None),
        check_vma=False,
    )
```

```python
import functools

import jax
import jax.numpy as jnp
from jax import lax
from jax.experimental import pallas as pl
from jax.experimental.pallas import tpu as pltpu
from jax.sharding import Mesh
from jax.sharding import PartitionSpec as P

FITS = 8
FITS_LAYER = 4
SLOTS = 3
CMAX = 1024
HD = 128
LANES = 128
ROOM = 48
ROWS = ROOM + 16
PARTS = 4
CLOSE = 0.97
STIFF = 0.004
RIDGE = 0.3
DEALT = (0, 1, 3, 2)
OVER, ME, OWNERS, SIZES, INFO = 0, 1, 2, 10, 32
SLOT_FIT, SLOT_SIZE, USED = 1, 4, 8
SCALE = HD ** (-0.5)
SEQ = ("seq_0", "seq_1")
HEAD_SEQ = ("head", "seq_0", "seq_1")
F32 = jnp.float32
BF16 = jnp.bfloat16


def room(mib):
    return pltpu.CompilerParams(vmem_limit_bytes=mib << 20)


SMEM = pl.BlockSpec(memory_space=pltpu.SMEM)
VMEM = pl.BlockSpec(memory_space=pltpu.VMEM)


def cost(flops, moved, exps=0):
    return pl.CostEstimate(flops=flops, transcendentals=exps, bytes_accessed=moved)


def iota(shape, dim):
    return lax.broadcasted_iota(jnp.int32, shape, dim)


def fiota(shape, dim):
    return iota(shape, dim).astype(F32)


def dot(a, b, dims=((1,), (0,))):
    return lax.dot_general(a, b, (dims, ((), ())), preferred_element_type=F32)


def running(mask):
    rows, width = mask.shape
    blocks = width // LANES
    upper = (iota((LANES, LANES), 0) <= iota((LANES, LANES), 1)).astype(BF16)
    stacked = jnp.concatenate(
        [mask[:, b * LANES : (b + 1) * LANES] for b in range(blocks)], axis=0
    )
    inner = dot(stacked.astype(BF16), upper)
    carry = jnp.zeros((rows, 1), F32)
    parts = []
    for b in range(blocks):
        part = inner[b * rows : (b + 1) * rows]
        parts.append(part + carry)
        carry = carry + part[:, LANES - 1 : LANES]
    return jnp.concatenate(parts, axis=1), carry


def heaviest(owner_of):
    owners = [owner_of(f) for f in range(FITS)]
    number = [sum((a == b).astype(jnp.int32) for b in owners) for a in owners]
    places = []
    for f in range(FITS):
        best, place = jnp.int32(0), jnp.int32(0)
        for g in range(FITS):
            better = (owners[g] // PARTS == owners[f] // PARTS) & (number[g] > best)
            best = jnp.where(better, number[g], best)
            place = jnp.where(better, owners[g] & (PARTS - 1), place)
        places.append(place)
    return places


def send_kernel(
    shards, own_hbm, size_hbm, idx_ref, keys_ref, send_ref, info_ref, own_ref, size_ref, sems
):
    copies = [
        pltpu.make_async_copy(own_hbm, own_ref, sems.at[0]),
        pltpu.make_async_copy(size_hbm, size_ref, sems.at[1]),
    ]
    for copy in copies:
        copy.start()
    send_ref[...] = jnp.zeros(send_ref.shape, BF16)
    for copy in copies:
        copy.wait()
    me = lax.axis_index(SEQ).astype(jnp.int32)
    local = keys_ref.shape[1]
    shift = local.bit_length() - 1
    fits, width = idx_ref.shape
    idx = idx_ref[...]
    row = iota((fits, width), 0)
    lane = iota((fits, width), 1)
    size = jnp.zeros((fits, width), jnp.int32)
    own = jnp.zeros((fits, LANES), jnp.int32)
    row1 = iota((fits, LANES), 0)
    lane1 = iota((fits, LANES), 1)
    for f in range(fits):
        size = jnp.where(row == f, size_ref[0, f], size)
        own = jnp.where(row1 == f, own_ref[0, f] // PARTS, own)
    shard = jnp.where(lane < size, lax.shift_right_logical(idx, shift), -1)
    counts = jnp.zeros((fits, LANES), F32)
    for s in range(shards):
        count = jnp.sum(jnp.where(shard == s, 1.0, 0.0), axis=1, keepdims=True)
        counts = jnp.where(lane1 == s, count, counts)
    total = jnp.zeros((fits, LANES), F32)
    before = jnp.zeros((fits, LANES), F32)
    for f in range(fits):
        shared = jnp.where(own == own_ref[0, f] // PARTS, counts[f : f + 1, :], 0.0)
        total = total + shared
        before = before + jnp.where(row1 > f, shared, 0.0)
    info_ref[OVER] = (jnp.max(total) > PARTS * ROOM).astype(jnp.int32)
    info_ref[ME] = me
    for f in range(fits):
        info_ref[OWNERS + f] = own_ref[0, f]
        info_ref[SIZES + f] = size_ref[0, f]
    first = jnp.sum(jnp.where(lane1 == me, before, 0.0), axis=1, keepdims=True)
    mine = shard == me
    held = jnp.where(mine, 1.0, 0.0)
    place, _ = running(held)
    place = jnp.where(mine, place - 1.0 + first, -1.0)
    spot = jnp.where(mine, idx - me * local + 1, 0).astype(F32)
    slot = fiota((PARTS * ROOM, width), 0)
    at = fiota((PARTS * ROOM, local), 1)
    middle = heaviest(lambda f: own_ref[0, f])
    for f in range(fits):
        here = place[f : f + 1, :] == slot
        pos = jnp.sum(jnp.where(here, spot[f : f + 1, :], 0.0), axis=1, keepdims=True) - 1.0
        pick = jnp.where(pos == at, 1.0, 0.0).astype(BF16)
        rows = dot(pick, keys_ref[f // FITS_LAYER])
        rows = rows.astype(BF16)
        to = own_ref[0, f] // PARTS * PARTS
        for part, step in enumerate(DEALT):
            place_along = (middle[f] + step) & (PARTS - 1)
            send_ref[to + place_along, 0:ROOM, :] += rows[part * ROOM : (part + 1) * ROOM]


def pack_keys(owners, sizes, indices, keys, shards):
    return pl.pallas_call(
        lambda *refs: send_kernel(shards, *refs),
        out_shape=(
            jax.ShapeDtypeStruct((shards, ROWS, LANES), BF16),
            jax.ShapeDtypeStruct((INFO,), jnp.int32),
        ),
        in_specs=[pl.BlockSpec(memory_space=pltpu.HBM)] * 2 + [VMEM, VMEM],
        out_specs=(VMEM, SMEM),
        scratch_shapes=[
            pltpu.SMEM((1, FITS), jnp.int32),
            pltpu.SMEM((1, FITS), jnp.int32),
            pltpu.SemaphoreType.DMA((2,)),
        ],
        compiler_params=room(24),
        cost_estimate=cost(10**9, 3 * 10**6),
        name="pack_keys",
    )(
        pltpu.with_memory_space_constraint(owners, pltpu.HBM),
        pltpu.with_memory_space_constraint(sizes, pltpu.HBM),
        indices,
        keys,
    )


def slots_of(me, info_ref):
    found = [jnp.int32(-1)] * SLOTS
    seen = jnp.int32(0)
    for f in range(FITS):
        match = info_ref[OWNERS + f] == me
        for j in range(SLOTS):
            found[j] = jnp.where(match & (seen == j), f, found[j])
        seen = seen + match.astype(jnp.int32)
    return found


def layer_rows(rows, layer):
    wide = rows.astype(F32)[:, 8 * layer : 8 * layer + 8, :]
    return wide.reshape(-1, wide.shape[-1])


def attend_kernel(recv_ref, keys_ref, values_ref, out_ref):
    shards = recv_ref.shape[0]
    outs = []
    stat = jnp.zeros((shards * 8, LANES), F32)
    lane = iota(stat.shape, 1)
    for layer in range(2):
        query = layer_rows(recv_ref[...], layer).astype(BF16)
        scores = dot(query, keys_ref[layer], ((1,), (1,))) * SCALE
        peak = jnp.max(scores, axis=1, keepdims=True)
        weights = jnp.exp(scores - peak)
        total = jnp.sum(weights, axis=1, keepdims=True)
        numer = dot(weights.astype(BF16), values_ref[layer])
        outs.append((numer / total).reshape(shards, 8, HD))
        level = peak + jnp.log(total)
        high = level.astype(BF16).astype(F32)
        middle = (level - high).astype(BF16).astype(F32)
        for k, piece in enumerate((high, middle, level - high - middle)):
            stat = jnp.where(lane == 64 * layer + k, piece, stat)
    out_ref[:, 0:16, :] = jnp.concatenate(outs, axis=1).astype(BF16)
    out_ref[:, 16:24, :] = stat.reshape(shards, 8, LANES).astype(BF16)


def attend(received, keys, values):
    shards = received.shape[0]
    return pl.pallas_call(
        attend_kernel,
        out_shape=jax.ShapeDtypeStruct((shards, 24, LANES), BF16),
        grid=(1,),
        in_specs=[
            pl.BlockSpec((shards, 16, LANES), lambda i: (0, ROOM // 16, 0)),
            pl.BlockSpec(keys.shape, lambda i: (0, 0, 0)),
            pl.BlockSpec(values.shape, lambda i: (0, 0, 0)),
        ],
        out_specs=pl.BlockSpec((shards, 24, LANES), lambda i: (0, 0, 0)),
        compiler_params=room(24),
        cost_estimate=cost(5 * 10**8, 3 * 10**6, 10**6),
        name="attend",
    )(received, keys, values)


def join_kernel(parts_ref, after_ref, out_ref):
    parts = parts_ref[...].astype(F32)
    stat = parts[:, 16:24, :]
    first = iota(stat.shape, 2) < 64
    level = jnp.concatenate(
        [
            jnp.sum(jnp.where(first, stat, 0.0), axis=2, keepdims=True),
            jnp.sum(jnp.where(first, 0.0, stat), axis=2, keepdims=True),
        ],
        axis=1,
    )
    weights = jnp.exp(level - jnp.max(level, axis=0, keepdims=True))
    numer = jnp.sum(weights * parts[:, 0:16, :], axis=0, keepdims=True)
    target = numer / jnp.sum(weights, axis=0, keepdims=True)
    out_ref[...] = jnp.broadcast_to(target, out_ref.shape).astype(BF16)


def join(parts, after):
    shards = parts.shape[0]
    return pl.pallas_call(
        join_kernel,
        out_shape=jax.ShapeDtypeStruct((shards, 16, LANES), BF16),
        in_specs=[VMEM, pl.BlockSpec(memory_space=pl.ANY)],
        out_specs=VMEM,
        compiler_params=room(8),
        cost_estimate=cost(10**6, 4 * 10**5, 10**3),
        name="join_parts",
    )(parts, after)


def turn_kernel(recv_ref, after_ref, out_ref):
    rows = recv_ref[:, 0:ROOM, :]
    out_ref[...] = rows.reshape(-1, HD).astype(F32).T.astype(BF16)


def turned(received, after):
    return pl.pallas_call(
        turn_kernel,
        out_shape=jax.ShapeDtypeStruct((HD, received.shape[0] * ROOM), BF16),
        in_specs=[VMEM, pl.BlockSpec(memory_space=pl.ANY)],
        out_specs=VMEM,
        compiler_params=room(8),
        cost_estimate=cost(10**6, 10**6),
        name="turn_keys",
    )(received, after)


def plan_kernel(shift, shards, info_ref, idx_ref, after_ref, dest_ref, out_ref):
    width = idx_ref.shape[1]
    me = info_ref[ME]
    fits = slots_of(me, info_ref)
    lane = iota((1, width), 1)
    source = iota((shards, width), 0)

    def shards_of(fit, size):
        place = lax.shift_right_logical(idx_ref[pl.ds(fit, 1), :], shift)
        return jnp.where(lane < size, place, -1)

    middle = heaviest(lambda f: info_ref[OWNERS + f])
    counts = []
    for f in range(FITS):
        shard = shards_of(f, info_ref[SIZES + f])
        counts.append(jnp.sum(jnp.where(shard == source, 1.0, 0.0), axis=1, keepdims=True))
    dest_ref[...] = jnp.full(dest_ref.shape, -1, jnp.int32)
    out_ref[OVER] = info_ref[OVER]
    for j in range(SLOTS):
        fit = jnp.maximum(fits[j], 0)
        size = info_ref[SIZES + fit]
        out_ref[SLOT_FIT + j] = fits[j]
        out_ref[SLOT_SIZE + j] = size
        shard = shards_of(fit, jnp.where(fits[j] >= 0, size, 0))
        first = jnp.zeros((shards, 1), F32)
        for f in range(FITS):
            ahead = (f < fit) & (info_ref[OWNERS + f] // PARTS == me // PARTS)
            first = first + counts[f] * ahead.astype(F32)
        held = jnp.where(shard == source, 1.0, 0.0)
        place, _ = running(held)
        rank = jnp.sum(held * (place - 1.0 + first), axis=0, keepdims=True).astype(jnp.int32)
        part = sum((rank >= k * ROOM).astype(jnp.int32) for k in range(1, PARTS))
        center = sum(jnp.where(fit == f, middle[f], 0) for f in range(FITS))
        step = jnp.full(part.shape, DEALT[0], jnp.int32)
        for k in range(1, PARTS):
            step = jnp.where(part == k, DEALT[k], step)
        turn = (me - center - step) & (PARTS - 1)
        dest = shard * ROOM + rank - part * ROOM + turn * (shards * ROOM)
        dest_ref[j : j + 1, :] = jnp.where(shard >= 0, dest, -1)
        for b in range(PARTS):
            here = jnp.where((shard >= 0) & (turn == b), 1, 0)
            out_ref[USED + j * PARTS + b] = jnp.max(here)


def plan(info, indices, after, shards, shift):
    return pl.pallas_call(
        lambda *refs: plan_kernel(shift, shards, *refs),
        out_shape=(
            jax.ShapeDtypeStruct(indices.shape, jnp.int32),
            jax.ShapeDtypeStruct((INFO,), jnp.int32),
        ),
        in_specs=[SMEM, VMEM, pl.BlockSpec(memory_space=pl.ANY)],
        out_specs=(VMEM, SMEM),
        compiler_params=room(8),
        cost_estimate=cost(10**10, 10**6),
        name="plan",
    )(info, indices, after)


def any_of(slots, info_ref):
    return functools.reduce(jnp.maximum, [info_ref[SLOT_FIT + j] for j in slots]) >= 0


def add_found(slots, turns, blocks, info_ref, dest_ref, total_ref):
    span = 256
    width = dest_ref.shape[1]
    columns = slice(slots[0] * width, (slots[-1] + 1) * width)
    dest = jnp.concatenate([dest_ref[j : j + 1, :] for j in slots], axis=1)
    block = lax.shift_right_arithmetic(dest, 8)
    offset = dest & (span - 1)
    for b, block_ref in zip(turns, blocks):
        used = sum(info_ref[USED + j * PARTS + b] for j in slots)

        @pl.when(used > 0)
        def _():
            pick = jnp.where(offset == iota((span, offset.shape[1]), 0), 1.0, 0.0).astype(BF16)
            pieces = block_ref.shape[1] // span
            stacked = jnp.concatenate(
                [block_ref[:, n * span : (n + 1) * span] for n in range(pieces)], axis=0
            )
            found = dot(stacked, pick)
            total = total_ref[:, columns]
            for n in range(pieces):
                total = jnp.where(block == b * pieces + n, found[n * HD : (n + 1) * HD], total)
            total_ref[:, columns] = total


def order_kernel(turn, info_ref, dest_ref, block_ref, *refs):
    out_ref, total_ref = refs[-2:]
    if turn == 0:
        total_ref[...] = jnp.zeros(total_ref.shape, F32)
    else:
        total_ref[...] = refs[0][...].astype(F32)
    for j in range(SLOTS):
        add_found((j,), (turn,), (block_ref,), info_ref, dest_ref, total_ref)
    out_ref[...] = total_ref[...].astype(BF16)


def ordered(turn, info, dest, block, before):
    anywhere = pl.BlockSpec(memory_space=pl.ANY)
    return pl.pallas_call(
        lambda *refs: order_kernel(turn, *refs),
        out_shape=jax.ShapeDtypeStruct((HD, SLOTS * CMAX), BF16),
        in_specs=[SMEM, VMEM, VMEM, VMEM if turn else anywhere],
        out_specs=VMEM,
        scratch_shapes=[pltpu.VMEM((HD, SLOTS * CMAX), F32)],
        compiler_params=room(16),
        cost_estimate=cost(2 * 10**9, 3 * 10**6),
        name="order_%d" % turn,
    )(info, dest, block, before)


def build_systems(slots, info_ref, recv_ref, keys_ref):
    count = recv_ref.shape[0] * 8
    width = CMAX
    eye = iota((count, count), 0) == iota((count, count), 1)
    lane = iota((1, width), 1)
    results = []
    rows = recv_ref[:, ROOM:ROWS, :]
    layers = layer_rows(rows, 0), layer_rows(rows, 1)
    for j in slots:
        live = info_ref[SLOT_FIT + j] >= 0
        size = info_ref[SLOT_SIZE + j]
        second = (info_ref[SLOT_FIT + j] >= FITS_LAYER).astype(F32)
        query = jnp.where(second > 0.5, layers[1], layers[0]).astype(BF16)
        scores = dot(query, keys_ref[:, j * width : (j + 1) * width]) * SCALE
        scores = jnp.where(lane < size, scores, -jnp.inf)
        expo = jnp.exp(scores - jnp.max(scores, axis=1, keepdims=True))
        probs = (expo / jnp.sum(expo, axis=1, keepdims=True)).astype(BF16)
        turned_probs = probs.astype(F32).T.astype(BF16)
        gram = dot(probs, turned_probs)
        trace = jnp.sum(jnp.where(eye, gram, 0.0))
        ridge = RIDGE * trace / size.astype(F32)
        top = jnp.minimum(jnp.max(jnp.sum(gram, axis=1, keepdims=True)), trace) + ridge
        taken = live.astype(F32)
        system = jnp.where(taken > 0.5, gram, 0.0) + jnp.where(
            eye, jnp.where(live, ridge, 1.0), 0.0
        )
        ends = jnp.where(live, ridge, 1.0), jnp.where(live, top, 1.0)
        results.append((system, turned_probs, ends))
    return results


def system_kernel(
    info_ref, dest_ref, recv_ref, back_ref, far_ref, part_ref, spare_ref, probs_ref, sys_ref, ends_ref,
    keys_ref, total_ref, held_ref, sems
):
    count = sys_ref.shape[1]
    width = dest_ref.shape[1]
    eye = iota((count, count), 0) == iota((count, count), 1)
    turns = PARTS - 1, PARTS // 2
    late = sum(info_ref[USED + j * PARTS + turn] for j in range(SLOTS) for turn in turns)
    keys_ref[...] = part_ref[...]

    @pl.when((info_ref[OVER] == 0) & (late > 0))
    def _():
        total_ref[...] = part_ref[...].astype(F32)
        for j in range(SLOTS):
            add_found((j,), turns, (back_ref, far_ref), info_ref, dest_ref, total_ref)
        keys_ref[...] = total_ref[...].astype(BF16)

    @pl.when(info_ref[OVER] > 0)
    def _():
        for j in range(SLOTS):
            pltpu.sync_copy(spare_ref.at[j], keys_ref.at[:, pl.ds(j * width, width)])

    def copy(j):
        return pltpu.make_async_copy(held_ref.at[j], probs_ref.at[j], sems.at[j])

    def fill(slots):
        live = any_of(slots, info_ref)

        @pl.when(live)
        def _():
            found = build_systems(slots, info_ref, recv_ref, keys_ref)
            for j, (system, probs, ends) in zip(slots, found):
                held_ref[j] = probs
                copy(j).start()
                sys_ref[j] = system
                ends_ref[j] = jnp.where(iota((8, LANES), 0) == 0, ends[0], ends[1])

        @pl.when(jnp.logical_not(live))
        def _():
            for j in slots:
                sys_ref[j] = jnp.where(eye, 1.0, 0.0)
                ends_ref[j] = jnp.full((8, LANES), 1.0, F32)

    groups = (0,), (1, 2)
    for slots in groups:
        fill(slots)
    for slots in groups:

        @pl.when(any_of(slots, info_ref))
        def _():
            for j in slots:
                copy(j).wait()


def systems(info, dest, received, back, far, part, spare):
    count = received.shape[0] * 8
    return pl.pallas_call(
        system_kernel,
        out_shape=(
            pltpu.HBM((SLOTS, CMAX, count), BF16),
            jax.ShapeDtypeStruct((SLOTS, count, count), F32),
            jax.ShapeDtypeStruct((SLOTS, 8, LANES), F32),
        ),
        in_specs=[SMEM] + [VMEM] * 5 + [pl.BlockSpec(memory_space=pltpu.HBM)],
        out_specs=(pl.BlockSpec(memory_space=pltpu.HBM), VMEM, VMEM),
        scratch_shapes=[
            pltpu.VMEM((HD, SLOTS * CMAX), BF16),
            pltpu.VMEM((HD, SLOTS * CMAX), F32),
            pltpu.VMEM((SLOTS, CMAX, count), BF16),
            pltpu.SemaphoreType.DMA((SLOTS,)),
        ],
        compiler_params=room(32),
        cost_estimate=cost(3 * 10**9, 3 * 10**6, 10**6),
        name="systems",
    )(
        info,
        dest,
        received,
        back,
        far,
        part,
        pltpu.with_memory_space_constraint(spare, pltpu.HBM),
    )


def split(x):
    high = x.astype(BF16)
    return high, (x - high.astype(F32)).astype(BF16)


def split3(x):
    high, _ = split(x)
    rest = x - high.astype(F32)
    middle, low = split(rest)
    return high, middle, low


def product(a, b):
    (a_high, a_low), (b_high, b_low) = a, b
    return dot(
        jnp.concatenate([a_high, a_high, a_low], axis=1),
        jnp.concatenate([b_high, b_low, b_high], axis=0),
    )


def product_full(a, b):
    (a0, a1, a2), (b0, b1, b2) = split3(a), split3(b)
    return dot(
        jnp.concatenate([a0, a0, a1, a0, a1, a2], axis=1),
        jnp.concatenate([b0, b1, b0, b2, b1, b0], axis=0),
    )


def invert_kernel(info_ref, sys_ref, ends_ref, inverse_ref, parts_ref, out_ref, low_ref, sem):
    count = sys_ref.shape[1]
    eye = iota((count, count), 0) == iota((count, count), 1)
    more = any_of((1, 2), info_ref)
    copy = pltpu.make_async_copy(out_ref, inverse_ref, sem)

    def start(slots):
        lows = []
        for j in slots:
            low = jnp.max(ends_ref[j, 0:1, :])
            high = jnp.max(ends_ref[j, 1:2, :])
            middle = 2.0 / (low + high)
            system = sys_ref[j]
            out_ref[j] = middle * (jnp.where(eye, 2.0, 0.0) - middle * system)
            parts_ref[j, 0], parts_ref[j, 1] = split(system)
            ratio = (high - low) / (high + low)
            lows.append(1.0 - ratio * ratio)
        return tuple(lows)

    def step(slots, lows, last=False, full=False):
        nexts = []
        for j, lowest in zip(slots, lows):
            held = out_ref[j]
            middle = 2.0 / (lowest + 1.0)
            parts = split(held)
            if full:
                images = product_full(sys_ref[j], held)
            else:
                images = product((parts_ref[j, 0], parts_ref[j, 1]), parts)
            rest = jnp.where(eye, 1.0, 0.0) - middle * images
            if last:
                moved = dot(parts[0], rest.astype(BF16))
            else:
                moved = product(parts, split(rest))
            out_ref[j] = middle * (held + moved)
            ratio = (1.0 - lowest) / (1.0 + lowest)
            nexts.append(1.0 - ratio * ratio)
        return tuple(nexts)

    def solve(slots):
        lows = start(slots)
        stiff = functools.reduce(jnp.minimum, lows) < STIFF
        lows = lax.while_loop(
            lambda lows: functools.reduce(jnp.minimum, lows) < CLOSE,
            functools.partial(step, slots),
            lows,
        )

        @pl.when(stiff)
        def _():
            step(slots, lows, full=True)

        @pl.when(jnp.logical_not(stiff))
        def _():
            step(slots, lows, last=True)

    @pl.when(more)
    def _():
        solve((0, 1, 2))

    @pl.when(jnp.logical_not(more))
    def _():
        solve((0,))

    copy.start()
    copy.wait()


def invert(info, system, ends):
    return pl.pallas_call(
        invert_kernel,
        out_shape=pltpu.HBM(system.shape, F32),
        in_specs=[SMEM, VMEM, VMEM],
        out_specs=pl.BlockSpec(memory_space=pltpu.HBM),
        scratch_shapes=[
            pltpu.VMEM((SLOTS, 2, *system.shape[1:]), BF16),
            pltpu.VMEM(system.shape, F32),
            pltpu.SMEM((SLOTS,), F32),
            pltpu.SemaphoreType.DMA(()),
        ],
        compiler_params=room(16),
        cost_estimate=cost(5 * 10**9, 2 * 10**6),
        name="invert",
    )(info, system, ends)


def values_kernel(
    info_ref, target_ref, inverse_ref, probs_ref, out_ref, inv, held, result, sems
):
    fits = [info_ref[SLOT_FIT + j] for j in range(SLOTS)]

    def copies(j):
        return (
            pltpu.make_async_copy(inverse_ref.at[j], inv.at[j], sems.at[0, j]),
            pltpu.make_async_copy(probs_ref.at[j], held.at[j], sems.at[1, j]),
        )

    def copy_out(j):
        return pltpu.make_async_copy(result.at[j], out_ref.at[0, j], sems.at[2, j])

    for j in range(SLOTS):

        @pl.when(fits[j] >= 0)
        def _():
            for copy in copies(j):
                copy.start()

    for j in range(SLOTS):

        @pl.when(fits[j] < 0)
        def _():
            result[j] = jnp.zeros(result.shape[1:], BF16)
            copy_out(j).start()

    for j in range(SLOTS):

        @pl.when(fits[j] >= 0)
        def _():
            rows = target_ref[...]
            first_rows, second_rows = layer_rows(rows, 0), layer_rows(rows, 1)
            second = (fits[j] >= FITS_LAYER).astype(F32)
            target = jnp.where(second > 0.5, second_rows, first_rows).astype(BF16)
            for copy in copies(j):
                copy.wait()
            weights = dot(
                jnp.concatenate(split3(inv[j]), axis=1),
                jnp.concatenate([target] * 3, axis=0),
            )
            high, low = split(weights)
            probs = held[j]
            result[j] = dot(
                jnp.concatenate([probs, probs], axis=1), jnp.concatenate([high, low], axis=0)
            ).astype(BF16)
            copy_out(j).start()

    for j in range(SLOTS):
        copy_out(j).wait()


def fitted_values(info, inverse, probs, target):
    anywhere = pl.BlockSpec(memory_space=pltpu.HBM)
    count = inverse.shape[1]
    return pl.pallas_call(
        values_kernel,
        out_shape=pltpu.HBM((1, SLOTS, CMAX, HD), BF16),
        in_specs=[SMEM, VMEM, anywhere, anywhere],
        out_specs=pl.BlockSpec(memory_space=pltpu.HBM),
        scratch_shapes=[
            pltpu.VMEM((SLOTS, count, count), F32),
            pltpu.VMEM((SLOTS, CMAX, count), BF16),
            pltpu.VMEM((SLOTS, CMAX, HD), BF16),
            pltpu.SemaphoreType.DMA((3, SLOTS)),
        ],
        compiler_params=room(16),
        cost_estimate=cost(10**9, 4 * 10**6),
        name="fitted_values",
    )(
        info,
        target,
        pltpu.with_memory_space_constraint(inverse, pltpu.HBM),
        pltpu.with_memory_space_constraint(probs, pltpu.HBM),
    )


def exchange(blocks):
    return lax.all_to_all(blocks, SEQ, split_axis=0, concat_axis=0, tiled=True)


def gathered_keys(owners, indices, keys):
    layers, local, width = keys.shape
    shards = lax.axis_size(SEQ)
    me = lax.axis_index(SEQ)
    fits = indices.shape[0]
    fit_ids = jnp.arange(fits, dtype=jnp.int32)
    offset = indices - me * local
    inside = (offset >= 0) & (offset < local)
    source = (fit_ids // FITS_LAYER)[:, None] * local + jnp.clip(offset, 0, local - 1)
    picked = jnp.take(keys.reshape(layers * local, width), source, axis=0)
    found = jnp.where(inside[..., None], picked, jnp.zeros((), picked.dtype))
    ring = [(k, (k + 1) % shards) for k in range(shards)]

    def pass_on(_, carried):
        moving, whole = carried
        moving = lax.ppermute(moving, SEQ, ring)
        return moving, whole + moving

    _, everything = lax.fori_loop(0, shards - 1, pass_on, (found, found))
    mine = owners[0] == me
    earlier = jnp.sum(
        jnp.where(mine[None, :] & (fit_ids[:, None] > fit_ids[None, :]), 1, 0), axis=1
    )
    chosen = [
        everything[jnp.sum(jnp.where(mine & (earlier == slot), fit_ids, 0))]
        for slot in range(SLOTS)
    ]
    return jnp.swapaxes(jnp.stack(chosen), 1, 2)


def on_device(queries, keys, values, indices, sizes, owners):
    layers, _, local, width = keys.shape
    key_rows = keys.reshape(layers, local, width)
    value_rows = values.reshape(layers, local, width)
    positions = indices[0]
    shards = lax.axis_size(SEQ)
    regrouped = lax.all_to_all(queries, "head", split_axis=1, concat_axis=2, tiled=True)
    own_rows = regrouped.reshape(1, 16, width)
    packed, info = pack_keys(owners, sizes, positions, key_rows, shards)
    packed = lax.dynamic_update_slice(
        packed, jnp.broadcast_to(own_rows, (shards, 16, width)), (0, ROOM, 0)
    )
    received = exchange(packed)
    spare = lax.cond(
        info[OVER] > 0,
        lambda: gathered_keys(owners, positions, key_rows),
        lambda: jnp.zeros((SLOTS, width, CMAX), BF16),
    )
    dest, owned = plan(info, positions, spare, shards, local.bit_length() - 1)
    own_block = turned(received, dest)
    near, back, far = (
        lax.ppermute(own_block, "seq_1", [(k, (k + d) % PARTS) for k in range(PARTS)])
        for d in (1, PARTS - 1, PARTS // 2)
    )
    attended = attend(received, key_rows, value_rows)
    parts = exchange(attended)
    ordering = ordered(0, owned, dest, own_block, attended)
    ordering = ordered(1, owned, dest, near, ordering)
    probs, system, ends = systems(owned, dest, received, back, far, ordering, spare)
    target = exchange(join(parts, system))
    inverse = invert(owned, system, ends)
    return fitted_values(owned, inverse, probs, target)


def solution(mesh):
    apart = Mesh(mesh.devices.reshape(mesh.shape["head"], 8, 4), ("head", "seq_0", "seq_1"))
    placed = (
        P(None, None, HEAD_SEQ, None),
        P(None, "head", SEQ, None),
        P(None, "head", SEQ, None),
        P("head", None, None),
        P("head", None),
        P("head", None),
    )
    return jax.shard_map(
        on_device,
        mesh=apart,
        in_specs=placed,
        out_specs=P("head", SEQ, None, None),
        check_vma=False,
    )
```

```python
import functools

import jax
import jax.numpy as jnp
from jax import lax
from jax.experimental import pallas as pl
from jax.experimental.pallas import tpu as pltpu
from jax.sharding import Mesh
from jax.sharding import PartitionSpec as P

FITS = 8
FITS_LAYER = 4
SLOTS = 3
CMAX = 1024
HD = 128
LANES = 128
ROOM = 48
ROWS = ROOM + 16
PARTS = 4
CLOSE = 0.97
STIFF = 0.004
BOUND = 1.001
RIDGE = 0.3
DEALT = (0, 1, 3, 2)
OVER, ME, OWNERS, SIZES, INFO = 0, 1, 2, 10, 32
SLOT_FIT, SLOT_SIZE, USED = 1, 4, 8
SCALE = HD ** (-0.5)
SEQ = ("seq_0", "seq_1")
HEAD_SEQ = ("head", "seq_0", "seq_1")
F32 = jnp.float32
BF16 = jnp.bfloat16


def room(mib):
    return pltpu.CompilerParams(vmem_limit_bytes=mib << 20)


SMEM = pl.BlockSpec(memory_space=pltpu.SMEM)
VMEM = pl.BlockSpec(memory_space=pltpu.VMEM)


def cost(flops, moved, exps=0):
    return pl.CostEstimate(flops=flops, transcendentals=exps, bytes_accessed=moved)


def iota(shape, dim):
    return lax.broadcasted_iota(jnp.int32, shape, dim)


def fiota(shape, dim):
    return iota(shape, dim).astype(F32)


def dot(a, b, dims=((1,), (0,))):
    return lax.dot_general(a, b, (dims, ((), ())), preferred_element_type=F32)


def running(mask):
    rows, width = mask.shape
    blocks = width // LANES
    upper = (iota((LANES, LANES), 0) <= iota((LANES, LANES), 1)).astype(BF16)
    stacked = jnp.concatenate(
        [mask[:, b * LANES : (b + 1) * LANES] for b in range(blocks)], axis=0
    )
    inner = dot(stacked.astype(BF16), upper)
    carry = jnp.zeros((rows, 1), F32)
    parts = []
    for b in range(blocks):
        part = inner[b * rows : (b + 1) * rows]
        parts.append(part + carry)
        carry = carry + part[:, LANES - 1 : LANES]
    return jnp.concatenate(parts, axis=1), carry


def heaviest(owner_of):
    owners = [owner_of(f) for f in range(FITS)]
    number = [sum((a == b).astype(jnp.int32) for b in owners) for a in owners]
    places = []
    for f in range(FITS):
        best, place = jnp.int32(0), jnp.int32(0)
        for g in range(FITS):
            better = (owners[g] // PARTS == owners[f] // PARTS) & (number[g] > best)
            best = jnp.where(better, number[g], best)
            place = jnp.where(better, owners[g] & (PARTS - 1), place)
        places.append(place)
    return places


def send_kernel(
    shards, own_hbm, size_hbm, idx_ref, keys_ref, send_ref, info_ref, own_ref, size_ref, sems
):
    copies = [
        pltpu.make_async_copy(own_hbm, own_ref, sems.at[0]),
        pltpu.make_async_copy(size_hbm, size_ref, sems.at[1]),
    ]
    for copy in copies:
        copy.start()
    send_ref[...] = jnp.zeros(send_ref.shape, BF16)
    for copy in copies:
        copy.wait()
    me = lax.axis_index(SEQ).astype(jnp.int32)
    local = keys_ref.shape[1]
    shift = local.bit_length() - 1
    fits, width = idx_ref.shape
    idx = idx_ref[...]
    row = iota((fits, width), 0)
    lane = iota((fits, width), 1)
    size = jnp.zeros((fits, width), jnp.int32)
    own = jnp.zeros((fits, LANES), jnp.int32)
    row1 = iota((fits, LANES), 0)
    lane1 = iota((fits, LANES), 1)
    for f in range(fits):
        size = jnp.where(row == f, size_ref[0, f], size)
        own = jnp.where(row1 == f, own_ref[0, f] // PARTS, own)
    shard = jnp.where(lane < size, lax.shift_right_logical(idx, shift), -1)
    counts = jnp.zeros((fits, LANES), F32)
    for s in range(shards):
        count = jnp.sum(jnp.where(shard == s, 1.0, 0.0), axis=1, keepdims=True)
        counts = jnp.where(lane1 == s, count, counts)
    total = jnp.zeros((fits, LANES), F32)
    before = jnp.zeros((fits, LANES), F32)
    for f in range(fits):
        shared = jnp.where(own == own_ref[0, f] // PARTS, counts[f : f + 1, :], 0.0)
        total = total + shared
        before = before + jnp.where(row1 > f, shared, 0.0)
    info_ref[OVER] = (jnp.max(total) > PARTS * ROOM).astype(jnp.int32)
    info_ref[ME] = me
    for f in range(fits):
        info_ref[OWNERS + f] = own_ref[0, f]
        info_ref[SIZES + f] = size_ref[0, f]
    first = jnp.sum(jnp.where(lane1 == me, before, 0.0), axis=1, keepdims=True)
    mine = shard == me
    held = jnp.where(mine, 1.0, 0.0)
    place, _ = running(held)
    place = jnp.where(mine, place - 1.0 + first, -1.0)
    spot = jnp.where(mine, idx - me * local + 1, 0).astype(F32)
    slot = fiota((PARTS * ROOM, width), 0)
    at = fiota((PARTS * ROOM, local), 1)
    middle = heaviest(lambda f: own_ref[0, f])
    for f in range(fits):
        here = place[f : f + 1, :] == slot
        pos = jnp.sum(jnp.where(here, spot[f : f + 1, :], 0.0), axis=1, keepdims=True) - 1.0
        pick = jnp.where(pos == at, 1.0, 0.0).astype(BF16)
        rows = dot(pick, keys_ref[f // FITS_LAYER])
        rows = rows.astype(BF16)
        to = own_ref[0, f] // PARTS * PARTS
        for part, step in enumerate(DEALT):
            place_along = (middle[f] + step) & (PARTS - 1)
            send_ref[to + place_along, 0:ROOM, :] += rows[part * ROOM : (part + 1) * ROOM]


def pack_keys(owners, sizes, indices, keys, shards):
    return pl.pallas_call(
        lambda *refs: send_kernel(shards, *refs),
        out_shape=(
            jax.ShapeDtypeStruct((shards, ROWS, LANES), BF16),
            jax.ShapeDtypeStruct((INFO,), jnp.int32),
        ),
        in_specs=[pl.BlockSpec(memory_space=pltpu.HBM)] * 2 + [VMEM, VMEM],
        out_specs=(VMEM, SMEM),
        scratch_shapes=[
            pltpu.SMEM((1, FITS), jnp.int32),
            pltpu.SMEM((1, FITS), jnp.int32),
            pltpu.SemaphoreType.DMA((2,)),
        ],
        compiler_params=room(24),
        cost_estimate=cost(10**9, 3 * 10**6),
        name="pack_keys",
    )(
        pltpu.with_memory_space_constraint(owners, pltpu.HBM),
        pltpu.with_memory_space_constraint(sizes, pltpu.HBM),
        indices,
        keys,
    )


def slots_of(me, info_ref):
    found = [jnp.int32(-1)] * SLOTS
    seen = jnp.int32(0)
    for f in range(FITS):
        match = info_ref[OWNERS + f] == me
        for j in range(SLOTS):
            found[j] = jnp.where(match & (seen == j), f, found[j])
        seen = seen + match.astype(jnp.int32)
    return found


def layer_rows(rows, layer):
    wide = rows.astype(F32)[:, 8 * layer : 8 * layer + 8, :]
    return wide.reshape(-1, wide.shape[-1])


def attend_kernel(recv_ref, keys_ref, values_ref, out_ref):
    shards = recv_ref.shape[0]
    outs = []
    stat = jnp.zeros((shards * 8, LANES), F32)
    lane = iota(stat.shape, 1)
    for layer in range(2):
        query = layer_rows(recv_ref[...], layer).astype(BF16)
        scores = dot(query, keys_ref[layer], ((1,), (1,))) * SCALE
        peak = jnp.max(scores, axis=1, keepdims=True)
        weights = jnp.exp(scores - peak)
        total = jnp.sum(weights, axis=1, keepdims=True)
        numer = dot(weights.astype(BF16), values_ref[layer])
        outs.append((numer / total).reshape(shards, 8, HD))
        level = peak + jnp.log(total)
        high = level.astype(BF16).astype(F32)
        middle = (level - high).astype(BF16).astype(F32)
        for k, piece in enumerate((high, middle, level - high - middle)):
            stat = jnp.where(lane == 64 * layer + k, piece, stat)
    out_ref[:, 0:16, :] = jnp.concatenate(outs, axis=1).astype(BF16)
    out_ref[:, 16:24, :] = stat.reshape(shards, 8, LANES).astype(BF16)


def attend(received, keys, values):
    shards = received.shape[0]
    return pl.pallas_call(
        attend_kernel,
        out_shape=jax.ShapeDtypeStruct((shards, 24, LANES), BF16),
        grid=(1,),
        in_specs=[
            pl.BlockSpec((shards, 16, LANES), lambda i: (0, ROOM // 16, 0)),
            pl.BlockSpec(keys.shape, lambda i: (0, 0, 0)),
            pl.BlockSpec(values.shape, lambda i: (0, 0, 0)),
        ],
        out_specs=pl.BlockSpec((shards, 24, LANES), lambda i: (0, 0, 0)),
        compiler_params=room(24),
        cost_estimate=cost(5 * 10**8, 3 * 10**6, 10**6),
        name="attend",
    )(received, keys, values)


def join_kernel(parts_ref, after_ref, out_ref):
    parts = parts_ref[...].astype(F32)
    stat = parts[:, 16:24, :]
    first = iota(stat.shape, 2) < 64
    level = jnp.concatenate(
        [
            jnp.sum(jnp.where(first, stat, 0.0), axis=2, keepdims=True),
            jnp.sum(jnp.where(first, 0.0, stat), axis=2, keepdims=True),
        ],
        axis=1,
    )
    weights = jnp.exp(level - jnp.max(level, axis=0, keepdims=True))
    numer = jnp.sum(weights * parts[:, 0:16, :], axis=0, keepdims=True)
    target = numer / jnp.sum(weights, axis=0, keepdims=True)
    out_ref[...] = jnp.broadcast_to(target, out_ref.shape).astype(BF16)


def join(parts, after):
    shards = parts.shape[0]
    return pl.pallas_call(
        join_kernel,
        out_shape=jax.ShapeDtypeStruct((shards, 16, LANES), BF16),
        in_specs=[VMEM, pl.BlockSpec(memory_space=pl.ANY)],
        out_specs=VMEM,
        compiler_params=room(8),
        cost_estimate=cost(10**6, 4 * 10**5, 10**3),
        name="join_parts",
    )(parts, after)


def turn_kernel(recv_ref, after_ref, out_ref):
    rows = recv_ref[:, 0:ROOM, :]
    out_ref[...] = rows.reshape(-1, HD).astype(F32).T.astype(BF16)


def turned(received, after):
    return pl.pallas_call(
        turn_kernel,
        out_shape=jax.ShapeDtypeStruct((HD, received.shape[0] * ROOM), BF16),
        in_specs=[VMEM, pl.BlockSpec(memory_space=pl.ANY)],
        out_specs=VMEM,
        compiler_params=room(8),
        cost_estimate=cost(10**6, 10**6),
        name="turn_keys",
    )(received, after)


def plan_kernel(shift, shards, info_ref, idx_ref, after_ref, dest_ref, out_ref):
    width = idx_ref.shape[1]
    me = info_ref[ME]
    fits = slots_of(me, info_ref)
    lane = iota((1, width), 1)
    source = iota((shards, width), 0)

    def shards_of(fit, size):
        place = lax.shift_right_logical(idx_ref[pl.ds(fit, 1), :], shift)
        return jnp.where(lane < size, place, -1)

    middle = heaviest(lambda f: info_ref[OWNERS + f])
    counts = []
    for f in range(FITS):
        shard = shards_of(f, info_ref[SIZES + f])
        counts.append(jnp.sum(jnp.where(shard == source, 1.0, 0.0), axis=1, keepdims=True))
    dest_ref[...] = jnp.full(dest_ref.shape, -1, jnp.int32)
    out_ref[OVER] = info_ref[OVER]
    for j in range(SLOTS):
        fit = jnp.maximum(fits[j], 0)
        size = info_ref[SIZES + fit]
        out_ref[SLOT_FIT + j] = fits[j]
        out_ref[SLOT_SIZE + j] = size
        shard = shards_of(fit, jnp.where(fits[j] >= 0, size, 0))
        first = jnp.zeros((shards, 1), F32)
        for f in range(FITS):
            ahead = (f < fit) & (info_ref[OWNERS + f] // PARTS == me // PARTS)
            first = first + counts[f] * ahead.astype(F32)
        held = jnp.where(shard == source, 1.0, 0.0)
        place, _ = running(held)
        rank = jnp.sum(held * (place - 1.0 + first), axis=0, keepdims=True).astype(jnp.int32)
        part = sum((rank >= k * ROOM).astype(jnp.int32) for k in range(1, PARTS))
        center = sum(jnp.where(fit == f, middle[f], 0) for f in range(FITS))
        step = jnp.full(part.shape, DEALT[0], jnp.int32)
        for k in range(1, PARTS):
            step = jnp.where(part == k, DEALT[k], step)
        turn = (me - center - step) & (PARTS - 1)
        dest = shard * ROOM + rank - part * ROOM + turn * (shards * ROOM)
        dest_ref[j : j + 1, :] = jnp.where(shard >= 0, dest, -1)
        for b in range(PARTS):
            here = jnp.where((shard >= 0) & (turn == b), 1, 0)
            out_ref[USED + j * PARTS + b] = jnp.max(here)


def plan(info, indices, after, shards, shift):
    return pl.pallas_call(
        lambda *refs: plan_kernel(shift, shards, *refs),
        out_shape=(
            jax.ShapeDtypeStruct(indices.shape, jnp.int32),
            jax.ShapeDtypeStruct((INFO,), jnp.int32),
        ),
        in_specs=[SMEM, VMEM, pl.BlockSpec(memory_space=pl.ANY)],
        out_specs=(VMEM, SMEM),
        compiler_params=room(8),
        cost_estimate=cost(10**10, 10**6),
        name="plan",
    )(info, indices, after)


def any_of(slots, info_ref):
    return functools.reduce(jnp.maximum, [info_ref[SLOT_FIT + j] for j in slots]) >= 0


def add_found(slots, turns, blocks, info_ref, dest_ref, total_ref, base=0):
    span = 256
    width = dest_ref.shape[1]
    columns = slice((slots[0] - base) * width, (slots[-1] + 1 - base) * width)
    dest = jnp.concatenate([dest_ref[j : j + 1, :] for j in slots], axis=1)
    block = lax.shift_right_arithmetic(dest, 8)
    offset = dest & (span - 1)
    for b, block_ref in zip(turns, blocks):
        used = sum(info_ref[USED + j * PARTS + b] for j in slots)

        @pl.when(used > 0)
        def _():
            pick = jnp.where(offset == iota((span, offset.shape[1]), 0), 1.0, 0.0).astype(BF16)
            pieces = block_ref.shape[1] // span
            stacked = jnp.concatenate(
                [block_ref[:, n * span : (n + 1) * span] for n in range(pieces)], axis=0
            )
            found = dot(stacked, pick)
            total = total_ref[:, columns]
            for n in range(pieces):
                total = jnp.where(block == b * pieces + n, found[n * HD : (n + 1) * HD], total)
            total_ref[:, columns] = total


def order_kernel(turn, info_ref, dest_ref, block_ref, before_ref, out_ref, total_ref, *held):
    if turn == 0:
        total_ref[...] = jnp.zeros(total_ref.shape, F32)
    else:
        total_ref[...] = before_ref[...].astype(F32)
    for j in range(SLOTS):
        add_found((j,), (turn,), (block_ref,), info_ref, dest_ref, total_ref)
    if turn == 0:
        out_ref[...] = total_ref[...].astype(BF16)
    else:
        held_ref, sem = held
        held_ref[...] = total_ref[...].astype(BF16)
        copy = pltpu.make_async_copy(held_ref, out_ref, sem)
        copy.start()
        copy.wait()


def ordered(turn, info, dest, block, before):
    shape = (HD, SLOTS * CMAX)
    anywhere = pl.BlockSpec(memory_space=pl.ANY)
    in_hbm = pl.BlockSpec(memory_space=pltpu.HBM)
    return pl.pallas_call(
        lambda *refs: order_kernel(turn, *refs),
        out_shape=pltpu.HBM(shape, BF16) if turn else jax.ShapeDtypeStruct(shape, BF16),
        in_specs=[SMEM, VMEM, VMEM, VMEM if turn else anywhere],
        out_specs=in_hbm if turn else VMEM,
        scratch_shapes=[pltpu.VMEM(shape, F32)]
        + ([pltpu.VMEM(shape, BF16), pltpu.SemaphoreType.DMA(())] if turn else []),
        compiler_params=room(16),
        cost_estimate=cost(2 * 10**9, 3 * 10**6),
        name="order_%d" % turn,
    )(info, dest, block, before)


def build_systems(slots, info_ref, recv_ref, keys_ref):
    count = recv_ref.shape[0] * 8
    width = CMAX
    eye = iota((count, count), 0) == iota((count, count), 1)
    lane = iota((1, width), 1)
    results = []
    rows = recv_ref[:, ROOM:ROWS, :]
    layers = layer_rows(rows, 0), layer_rows(rows, 1)
    for j in slots:
        live = info_ref[SLOT_FIT + j] >= 0
        size = info_ref[SLOT_SIZE + j]
        second = (info_ref[SLOT_FIT + j] >= FITS_LAYER).astype(F32)
        query = jnp.where(second > 0.5, layers[1], layers[0]).astype(BF16)
        scores = dot(query, keys_ref[:, (j - slots[0]) * width : (j - slots[0] + 1) * width]) * SCALE
        scores = jnp.where(lane < size, scores, -jnp.inf)
        expo = jnp.exp(scores - jnp.max(scores, axis=1, keepdims=True))
        probs = (expo / jnp.sum(expo, axis=1, keepdims=True)).astype(BF16)
        turned_probs = probs.astype(F32).T.astype(BF16)
        gram = dot(probs, turned_probs)
        trace = jnp.sum(jnp.where(eye, gram, 0.0))
        ridge = RIDGE * trace / size.astype(F32)
        sums = jnp.sum(gram, axis=0, keepdims=True)
        ratios = jnp.sum(gram * sums, axis=1, keepdims=True) / jnp.sum(gram, axis=1, keepdims=True)
        top = jnp.minimum(BOUND * jnp.max(ratios), trace) + ridge
        taken = live.astype(F32)
        system = jnp.where(taken > 0.5, gram, 0.0) + jnp.where(
            eye, jnp.where(live, ridge, 1.0), 0.0
        )
        ends = jnp.where(live, ridge, 1.0), jnp.where(live, top, 1.0)
        results.append((system, turned_probs, ends))
    return results


def system_kernel(
    slots, info_ref, dest_ref, recv_ref, back_ref, far_ref, part_ref, spare_ref, probs_ref, sys_ref,
    ends_ref, keys_ref, total_ref, held_ref, sem
):
    count = sys_ref.shape[1]
    width = dest_ref.shape[1]
    turns = PARTS - 1, PARTS // 2
    late = sum(info_ref[USED + j * PARTS + turn] for j in slots for turn in turns)
    live = any_of(slots, info_ref)
    copy = pltpu.make_async_copy(held_ref, probs_ref, sem)

    @pl.when(live)
    def _():
        pltpu.sync_copy(part_ref.at[:, pl.ds(slots[0] * width, len(slots) * width)], keys_ref)

        @pl.when((info_ref[OVER] == 0) & (late > 0))
        def _():
            total_ref[...] = keys_ref[...].astype(F32)
            for j in slots:
                add_found(
                    (j,), turns, (back_ref, far_ref), info_ref, dest_ref, total_ref, slots[0]
                )
            keys_ref[...] = total_ref[...].astype(BF16)

        @pl.when(info_ref[OVER] > 0)
        def _():
            for i, j in enumerate(slots):
                pltpu.sync_copy(spare_ref.at[j], keys_ref.at[:, pl.ds(i * width, width)])

        found = build_systems(slots, info_ref, recv_ref, keys_ref)
        for i, (system, probs, ends) in enumerate(found):
            held_ref[i] = probs
            sys_ref[i] = system
            ends_ref[i] = jnp.where(iota((8, LANES), 0) == 0, ends[0], ends[1])
        copy.start()
        copy.wait()

    @pl.when(jnp.logical_not(live))
    def _():
        eye = iota((count, count), 0) == iota((count, count), 1)
        for i in range(len(slots)):
            sys_ref[i] = jnp.where(eye, 1.0, 0.0)
            ends_ref[i] = jnp.full((8, LANES), 1.0, F32)


def systems(slots, info, dest, received, back, far, part, spare):
    count = received.shape[0] * 8
    number = len(slots)
    return pl.pallas_call(
        lambda *refs: system_kernel(slots, *refs),
        out_shape=(
            pltpu.HBM((number, CMAX, count), BF16),
            jax.ShapeDtypeStruct((number, count, count), F32),
            jax.ShapeDtypeStruct((number, 8, LANES), F32),
        ),
        in_specs=[SMEM] + [VMEM] * 4 + [pl.BlockSpec(memory_space=pltpu.HBM)] * 2,
        out_specs=(pl.BlockSpec(memory_space=pltpu.HBM), VMEM, VMEM),
        scratch_shapes=[
            pltpu.VMEM((HD, number * CMAX), BF16),
            pltpu.VMEM((HD, number * CMAX), F32),
            pltpu.VMEM((number, CMAX, count), BF16),
            pltpu.SemaphoreType.DMA(()),
        ],
        compiler_params=room(24),
        cost_estimate=cost(number * 10**9, 3 * 10**6, 10**6),
        name="systems_%d" % slots[0],
    )(
        info,
        dest,
        received,
        back,
        far,
        pltpu.with_memory_space_constraint(part, pltpu.HBM),
        pltpu.with_memory_space_constraint(spare, pltpu.HBM),
    )


def split(x):
    high = x.astype(BF16)
    return high, (x - high.astype(F32)).astype(BF16)


def split3(x):
    high, _ = split(x)
    rest = x - high.astype(F32)
    middle, low = split(rest)
    return high, middle, low


def product(a, b):
    (a_high, a_low), (b_high, b_low) = a, b
    return dot(
        jnp.concatenate([a_high, a_high, a_low], axis=1),
        jnp.concatenate([b_high, b_low, b_high], axis=0),
    )


def product_full(a, b):
    (a0, a1, a2), (b0, b1, b2) = split3(a), split3(b)
    return dot(
        jnp.concatenate([a0, a0, a1, a0, a1, a2], axis=1),
        jnp.concatenate([b0, b1, b0, b2, b1, b0], axis=0),
    )


def invert_kernel(
    info_ref, first_ref, first_ends_ref, other_ref, other_ends_ref, inverse_ref, parts_ref, out_ref, sem
):
    count = first_ref.shape[1]
    held_systems = [first_ref.at[0], other_ref.at[0], other_ref.at[1]]
    held_ends = [first_ends_ref.at[0], other_ends_ref.at[0], other_ends_ref.at[1]]
    eye = iota((count, count), 0) == iota((count, count), 1)
    more = any_of((1, 2), info_ref)
    copy = pltpu.make_async_copy(out_ref, inverse_ref, sem)

    def start(slots):
        lows = []
        for j in slots:
            low = jnp.max(held_ends[j][0:1, :])
            high = jnp.max(held_ends[j][1:2, :])
            middle = 2.0 / (low + high)
            system = held_systems[j][...]
            out_ref[j] = middle * (jnp.where(eye, 2.0, 0.0) - middle * system)
            parts_ref[j, 0], parts_ref[j, 1] = split(system)
            ratio = (high - low) / (high + low)
            lows.append(1.0 - ratio * ratio)
        return tuple(lows)

    def step(slots, lows, last=False, full=False):
        nexts = []
        for j, lowest in zip(slots, lows):
            held = out_ref[j]
            middle = 2.0 / (lowest + 1.0)
            parts = split(held)
            if full:
                images = product_full(held_systems[j][...], held)
            else:
                images = product((parts_ref[j, 0], parts_ref[j, 1]), parts)
            rest = jnp.where(eye, 1.0, 0.0) - middle * images
            if last:
                moved = dot(parts[0], rest.astype(BF16))
            else:
                moved = product(parts, split(rest))
            out_ref[j] = middle * (held + moved)
            ratio = (1.0 - lowest) / (1.0 + lowest)
            nexts.append(1.0 - ratio * ratio)
        return tuple(nexts)

    def solve(slots):
        lows = start(slots)
        stiff = functools.reduce(jnp.minimum, lows) < STIFF
        lows = lax.while_loop(
            lambda lows: functools.reduce(jnp.minimum, lows) < CLOSE,
            functools.partial(step, slots),
            lows,
        )

        @pl.when(stiff)
        def _():
            step(slots, lows, full=True)

        @pl.when(jnp.logical_not(stiff))
        def _():
            step(slots, lows, last=True)

    @pl.when(more)
    def _():
        solve((0, 1, 2))

    @pl.when(jnp.logical_not(more))
    def _():
        solve((0,))

    copy.start()
    copy.wait()


def invert(info, first, first_ends, other, other_ends):
    shape = (SLOTS, *first.shape[1:])
    return pl.pallas_call(
        invert_kernel,
        out_shape=pltpu.HBM(shape, F32),
        in_specs=[SMEM] + [VMEM] * 4,
        out_specs=pl.BlockSpec(memory_space=pltpu.HBM),
        scratch_shapes=[
            pltpu.VMEM((SLOTS, 2, *shape[1:]), BF16),
            pltpu.VMEM(shape, F32),
            pltpu.SemaphoreType.DMA(()),
        ],
        compiler_params=room(16),
        cost_estimate=cost(5 * 10**9, 2 * 10**6),
        name="invert",
    )(info, first, first_ends, other, other_ends)


def values_kernel(
    info_ref, target_ref, inverse_ref, first_ref, other_ref, out_ref, inv, held, result, sems
):
    fits = [info_ref[SLOT_FIT + j] for j in range(SLOTS)]
    sources = [first_ref.at[0], other_ref.at[0], other_ref.at[1]]
    more = any_of((1, 2), info_ref)

    def copies(j):
        return (
            pltpu.make_async_copy(inverse_ref.at[j], inv.at[j], sems.at[0, j]),
            pltpu.make_async_copy(sources[j], held.at[j], sems.at[1, j]),
        )

    def copy_out(j):
        return pltpu.make_async_copy(result.at[j], out_ref.at[0, j], sems.at[2, j])

    def clear(j):
        result[j] = jnp.zeros(result.shape[1:], BF16)
        copy_out(j).start()

    def fill(slots):
        for j in slots:
            for copy in copies(j):
                copy.start()
        rows = target_ref[...]
        layers = layer_rows(rows, 0), layer_rows(rows, 1)
        for j in slots:
            for copy in copies(j):
                copy.wait()
        weights = []
        for j in slots:
            second = (fits[j] >= FITS_LAYER).astype(F32)
            target = jnp.where(second > 0.5, layers[1], layers[0]).astype(BF16)
            weights.append(
                dot(
                    jnp.concatenate(split3(inv[j]), axis=1),
                    jnp.concatenate([target] * 3, axis=0),
                )
            )
        for j, weight in zip(slots, weights):
            high, low = split(weight)
            probs = held[j]
            found = dot(
                jnp.concatenate([probs, probs], axis=1), jnp.concatenate([high, low], axis=0)
            )
            taken = (fits[j] >= 0).astype(F32)
            result[j] = jnp.where(taken > 0.5, found, 0.0).astype(BF16)
            copy_out(j).start()

    @pl.when(more)
    def _():
        fill((0, 1, 2))

    @pl.when(jnp.logical_not(more))
    def _():
        clear(1)
        clear(2)

        @pl.when(fits[0] >= 0)
        def _():
            fill((0,))

        @pl.when(fits[0] < 0)
        def _():
            clear(0)

    for j in range(SLOTS):
        copy_out(j).wait()


def fitted_values(info, inverse, first, other, target):
    anywhere = pl.BlockSpec(memory_space=pltpu.HBM)
    count = inverse.shape[1]
    return pl.pallas_call(
        values_kernel,
        out_shape=pltpu.HBM((1, SLOTS, CMAX, HD), BF16),
        in_specs=[SMEM, VMEM, anywhere, anywhere, anywhere],
        out_specs=pl.BlockSpec(memory_space=pltpu.HBM),
        scratch_shapes=[
            pltpu.VMEM((SLOTS, count, count), F32),
            pltpu.VMEM((SLOTS, CMAX, count), BF16),
            pltpu.VMEM((SLOTS, CMAX, HD), BF16),
            pltpu.SemaphoreType.DMA((3, SLOTS)),
        ],
        compiler_params=room(16),
        cost_estimate=cost(10**9, 4 * 10**6),
        name="fitted_values",
    )(
        info,
        target,
        pltpu.with_memory_space_constraint(inverse, pltpu.HBM),
        pltpu.with_memory_space_constraint(first, pltpu.HBM),
        pltpu.with_memory_space_constraint(other, pltpu.HBM),
    )


def exchange(blocks):
    return lax.all_to_all(blocks, SEQ, split_axis=0, concat_axis=0, tiled=True)


def gathered_keys(owners, indices, keys):
    layers, local, width = keys.shape
    shards = lax.axis_size(SEQ)
    me = lax.axis_index(SEQ)
    fits = indices.shape[0]
    fit_ids = jnp.arange(fits, dtype=jnp.int32)
    offset = indices - me * local
    inside = (offset >= 0) & (offset < local)
    source = (fit_ids // FITS_LAYER)[:, None] * local + jnp.clip(offset, 0, local - 1)
    picked = jnp.take(keys.reshape(layers * local, width), source, axis=0)
    found = jnp.where(inside[..., None], picked, jnp.zeros((), picked.dtype))
    ring = [(k, (k + 1) % shards) for k in range(shards)]

    def pass_on(_, carried):
        moving, whole = carried
        moving = lax.ppermute(moving, SEQ, ring)
        return moving, whole + moving

    _, everything = lax.fori_loop(0, shards - 1, pass_on, (found, found))
    mine = owners[0] == me
    earlier = jnp.sum(
        jnp.where(mine[None, :] & (fit_ids[:, None] > fit_ids[None, :]), 1, 0), axis=1
    )
    chosen = [
        everything[jnp.sum(jnp.where(mine & (earlier == slot), fit_ids, 0))]
        for slot in range(SLOTS)
    ]
    return jnp.swapaxes(jnp.stack(chosen), 1, 2)


def on_device(queries, keys, values, indices, sizes, owners):
    layers, _, local, width = keys.shape
    key_rows = keys.reshape(layers, local, width)
    value_rows = values.reshape(layers, local, width)
    positions = indices[0]
    shards = lax.axis_size(SEQ)
    regrouped = lax.all_to_all(queries, "head", split_axis=1, concat_axis=2, tiled=True)
    own_rows = regrouped.reshape(1, 16, width)
    packed, info = pack_keys(owners, sizes, positions, key_rows, shards)
    packed = lax.dynamic_update_slice(
        packed, jnp.broadcast_to(own_rows, (shards, 16, width)), (0, ROOM, 0)
    )
    received = exchange(packed)
    spare = lax.cond(
        info[OVER] > 0,
        lambda: gathered_keys(owners, positions, key_rows),
        lambda: jnp.zeros((SLOTS, width, CMAX), BF16),
    )
    dest, owned = plan(info, positions, spare, shards, local.bit_length() - 1)
    own_block = turned(received, dest)
    near, back, far = (
        lax.ppermute(own_block, "seq_1", [(k, (k + d) % PARTS) for k in range(PARTS)])
        for d in (1, PARTS - 1, PARTS // 2)
    )
    attended = attend(received, key_rows, value_rows)
    parts = exchange(attended)
    ordering = ordered(0, owned, dest, own_block, attended)
    ordering = ordered(1, owned, dest, near, ordering)
    late = dest, received, back, far, ordering, spare
    first_probs, first, first_ends = systems((0,), owned, *late)
    target = exchange(join(parts, first))
    other_probs, other, other_ends = systems((1, 2), owned, *late)
    inverse = invert(owned, first, first_ends, other, other_ends)
    return fitted_values(owned, inverse, first_probs, other_probs, target)


def solution(mesh):
    apart = Mesh(mesh.devices.reshape(mesh.shape["head"], 8, 4), ("head", "seq_0", "seq_1"))
    placed = (
        P(None, None, HEAD_SEQ, None),
        P(None, "head", SEQ, None),
        P(None, "head", SEQ, None),
        P("head", None, None),
        P("head", None),
        P("head", None),
    )
    return jax.shard_map(
        on_device,
        mesh=apart,
        in_specs=placed,
        out_specs=P("head", SEQ, None, None),
        check_vma=False,
    )
```

```python
import functools

import jax
import jax.numpy as jnp
from jax import lax
from jax.experimental import pallas as pl
from jax.experimental.pallas import tpu as pltpu
from jax.sharding import Mesh
from jax.sharding import PartitionSpec as P

FITS = 8
FITS_LAYER = 4
SLOTS = 3
CMAX = 1024
HD = 128
LANES = 128
ROOM = 48
ROWS = ROOM + 16
PARTS = 4
CLOSE = 0.97
STIFF = 0.004
BOUND = 1.001
RIDGE = 0.3
DEALT = (0, 1, 3, 2)
OVER, ME, OWNERS, SIZES, INFO = 0, 1, 2, 10, 32
SLOT_FIT, SLOT_SIZE, USED = 1, 4, 8
SCALE = HD ** (-0.5)
SEQ = ("seq_0", "seq_1")
HEAD_SEQ = ("head", "seq_0", "seq_1")
F32 = jnp.float32
BF16 = jnp.bfloat16


def room(mib):
    return pltpu.CompilerParams(vmem_limit_bytes=mib << 20)


SMEM = pl.BlockSpec(memory_space=pltpu.SMEM)
VMEM = pl.BlockSpec(memory_space=pltpu.VMEM)


def cost(flops, moved, exps=0):
    return pl.CostEstimate(flops=flops, transcendentals=exps, bytes_accessed=moved)


def iota(shape, dim):
    return lax.broadcasted_iota(jnp.int32, shape, dim)


def fiota(shape, dim):
    return iota(shape, dim).astype(F32)


def dot(a, b, dims=((1,), (0,))):
    return lax.dot_general(a, b, (dims, ((), ())), preferred_element_type=F32)


def running(mask):
    rows, width = mask.shape
    blocks = width // LANES
    upper = (iota((LANES, LANES), 0) <= iota((LANES, LANES), 1)).astype(BF16)
    stacked = jnp.concatenate(
        [mask[:, b * LANES : (b + 1) * LANES] for b in range(blocks)], axis=0
    )
    inner = dot(stacked.astype(BF16), upper)
    carry = jnp.zeros((rows, 1), F32)
    parts = []
    for b in range(blocks):
        part = inner[b * rows : (b + 1) * rows]
        parts.append(part + carry)
        carry = carry + part[:, LANES - 1 : LANES]
    return jnp.concatenate(parts, axis=1), carry


def heaviest(owner_of):
    owners = [owner_of(f) for f in range(FITS)]
    number = [sum((a == b).astype(jnp.int32) for b in owners) for a in owners]
    places = []
    for f in range(FITS):
        best, place = jnp.int32(0), jnp.int32(0)
        for g in range(FITS):
            better = (owners[g] // PARTS == owners[f] // PARTS) & (number[g] > best)
            best = jnp.where(better, number[g], best)
            place = jnp.where(better, owners[g] & (PARTS - 1), place)
        places.append(place)
    return places


def send_kernel(
    shards, own_hbm, size_hbm, idx_ref, keys_ref, send_ref, info_ref, own_ref, size_ref, sems
):
    copies = [
        pltpu.make_async_copy(own_hbm, own_ref, sems.at[0]),
        pltpu.make_async_copy(size_hbm, size_ref, sems.at[1]),
    ]
    for copy in copies:
        copy.start()
    send_ref[...] = jnp.zeros(send_ref.shape, BF16)
    for copy in copies:
        copy.wait()
    me = lax.axis_index(SEQ).astype(jnp.int32)
    local = keys_ref.shape[1]
    shift = local.bit_length() - 1
    fits, width = idx_ref.shape
    idx = idx_ref[...]
    row = iota((fits, width), 0)
    lane = iota((fits, width), 1)
    size = jnp.zeros((fits, width), jnp.int32)
    own = jnp.zeros((fits, LANES), jnp.int32)
    row1 = iota((fits, LANES), 0)
    lane1 = iota((fits, LANES), 1)
    for f in range(fits):
        size = jnp.where(row == f, size_ref[0, f], size)
        own = jnp.where(row1 == f, own_ref[0, f] // PARTS, own)
    shard = jnp.where(lane < size, lax.shift_right_logical(idx, shift), -1)
    counts = jnp.zeros((fits, LANES), F32)
    for s in range(shards):
        count = jnp.sum(jnp.where(shard == s, 1.0, 0.0), axis=1, keepdims=True)
        counts = jnp.where(lane1 == s, count, counts)
    total = jnp.zeros((fits, LANES), F32)
    before = jnp.zeros((fits, LANES), F32)
    for f in range(fits):
        shared = jnp.where(own == own_ref[0, f] // PARTS, counts[f : f + 1, :], 0.0)
        total = total + shared
        before = before + jnp.where(row1 > f, shared, 0.0)
    info_ref[OVER] = (jnp.max(total) > PARTS * ROOM).astype(jnp.int32)
    info_ref[ME] = me
    for f in range(fits):
        info_ref[OWNERS + f] = own_ref[0, f]
        info_ref[SIZES + f] = size_ref[0, f]
    first = jnp.sum(jnp.where(lane1 == me, before, 0.0), axis=1, keepdims=True)
    mine = shard == me
    held = jnp.where(mine, 1.0, 0.0)
    place, _ = running(held)
    place = jnp.where(mine, place - 1.0 + first, -1.0)
    spot = jnp.where(mine, idx - me * local + 1, 0).astype(F32)
    slot = fiota((PARTS * ROOM, width), 0)
    at = fiota((PARTS * ROOM, local), 1)
    middle = heaviest(lambda f: own_ref[0, f])
    for f in range(fits):
        here = place[f : f + 1, :] == slot
        pos = jnp.sum(jnp.where(here, spot[f : f + 1, :], 0.0), axis=1, keepdims=True) - 1.0
        pick = jnp.where(pos == at, 1.0, 0.0).astype(BF16)
        rows = dot(pick, keys_ref[f // FITS_LAYER])
        rows = rows.astype(BF16)
        to = own_ref[0, f] // PARTS * PARTS
        for part, step in enumerate(DEALT):
            place_along = (middle[f] + step) & (PARTS - 1)
            send_ref[to + place_along, 0:ROOM, :] += rows[part * ROOM : (part + 1) * ROOM]


def pack_keys(owners, sizes, indices, keys, shards):
    return pl.pallas_call(
        lambda *refs: send_kernel(shards, *refs),
        out_shape=(
            jax.ShapeDtypeStruct((shards, ROWS, LANES), BF16),
            jax.ShapeDtypeStruct((INFO,), jnp.int32),
        ),
        in_specs=[pl.BlockSpec(memory_space=pltpu.HBM)] * 2 + [VMEM, VMEM],
        out_specs=(VMEM, SMEM),
        scratch_shapes=[
            pltpu.SMEM((1, FITS), jnp.int32),
            pltpu.SMEM((1, FITS), jnp.int32),
            pltpu.SemaphoreType.DMA((2,)),
        ],
        compiler_params=room(24),
        cost_estimate=cost(10**9, 3 * 10**6),
        name="pack_keys",
    )(
        pltpu.with_memory_space_constraint(owners, pltpu.HBM),
        pltpu.with_memory_space_constraint(sizes, pltpu.HBM),
        indices,
        keys,
    )


def slots_of(me, info_ref):
    found = [jnp.int32(-1)] * SLOTS
    seen = jnp.int32(0)
    for f in range(FITS):
        match = info_ref[OWNERS + f] == me
        for j in range(SLOTS):
            found[j] = jnp.where(match & (seen == j), f, found[j])
        seen = seen + match.astype(jnp.int32)
    return found


def layer_rows(rows, layer):
    wide = rows.astype(F32)[:, 8 * layer : 8 * layer + 8, :]
    return wide.reshape(-1, wide.shape[-1])


def attend_kernel(recv_ref, keys_ref, values_ref, out_ref):
    shards = recv_ref.shape[0]
    outs = []
    stat = jnp.zeros((shards * 8, LANES), F32)
    lane = iota(stat.shape, 1)
    for layer in range(2):
        query = layer_rows(recv_ref[...], layer).astype(BF16)
        scores = dot(query, keys_ref[layer], ((1,), (1,))) * SCALE
        peak = jnp.max(scores, axis=1, keepdims=True)
        weights = jnp.exp(scores - peak)
        total = jnp.sum(weights, axis=1, keepdims=True)
        numer = dot(weights.astype(BF16), values_ref[layer])
        outs.append((numer / total).reshape(shards, 8, HD))
        level = peak + jnp.log(total)
        high = level.astype(BF16).astype(F32)
        middle = (level - high).astype(BF16).astype(F32)
        for k, piece in enumerate((high, middle, level - high - middle)):
            stat = jnp.where(lane == 64 * layer + k, piece, stat)
    out_ref[:, 0:16, :] = jnp.concatenate(outs, axis=1).astype(BF16)
    out_ref[:, 16:24, :] = stat.reshape(shards, 8, LANES).astype(BF16)


def attend(received, keys, values):
    shards = received.shape[0]
    return pl.pallas_call(
        attend_kernel,
        out_shape=jax.ShapeDtypeStruct((shards, 24, LANES), BF16),
        grid=(1,),
        in_specs=[
            pl.BlockSpec((shards, 16, LANES), lambda i: (0, ROOM // 16, 0)),
            pl.BlockSpec(keys.shape, lambda i: (0, 0, 0)),
            pl.BlockSpec(values.shape, lambda i: (0, 0, 0)),
        ],
        out_specs=pl.BlockSpec((shards, 24, LANES), lambda i: (0, 0, 0)),
        compiler_params=room(24),
        cost_estimate=cost(5 * 10**8, 3 * 10**6, 10**6),
        name="attend",
    )(received, keys, values)


def join_kernel(parts_ref, after_ref, out_ref):
    parts = parts_ref[...].astype(F32)
    stat = parts[:, 16:24, :]
    first = iota(stat.shape, 2) < 64
    level = jnp.concatenate(
        [
            jnp.sum(jnp.where(first, stat, 0.0), axis=2, keepdims=True),
            jnp.sum(jnp.where(first, 0.0, stat), axis=2, keepdims=True),
        ],
        axis=1,
    )
    weights = jnp.exp(level - jnp.max(level, axis=0, keepdims=True))
    numer = jnp.sum(weights * parts[:, 0:16, :], axis=0, keepdims=True)
    target = numer / jnp.sum(weights, axis=0, keepdims=True)
    out_ref[...] = jnp.broadcast_to(target, out_ref.shape).astype(BF16)


def join(parts, after):
    shards = parts.shape[0]
    return pl.pallas_call(
        join_kernel,
        out_shape=jax.ShapeDtypeStruct((shards, 16, LANES), BF16),
        in_specs=[VMEM, pl.BlockSpec(memory_space=pl.ANY)],
        out_specs=VMEM,
        compiler_params=room(8),
        cost_estimate=cost(10**6, 4 * 10**5, 10**3),
        name="join_parts",
    )(parts, after)


def turn_kernel(recv_ref, after_ref, out_ref):
    rows = recv_ref[:, 0:ROOM, :]
    out_ref[...] = rows.reshape(-1, HD).astype(F32).T.astype(BF16)


def turned(received, after):
    return pl.pallas_call(
        turn_kernel,
        out_shape=jax.ShapeDtypeStruct((HD, received.shape[0] * ROOM), BF16),
        in_specs=[VMEM, pl.BlockSpec(memory_space=pl.ANY)],
        out_specs=VMEM,
        compiler_params=room(8),
        cost_estimate=cost(10**6, 10**6),
        name="turn_keys",
    )(received, after)


def plan_kernel(shift, shards, info_ref, idx_ref, after_ref, dest_ref, out_ref):
    width = idx_ref.shape[1]
    me = info_ref[ME]
    fits = slots_of(me, info_ref)
    lane = iota((1, width), 1)
    source = iota((shards, width), 0)

    def shards_of(fit, size):
        place = lax.shift_right_logical(idx_ref[pl.ds(fit, 1), :], shift)
        return jnp.where(lane < size, place, -1)

    middle = heaviest(lambda f: info_ref[OWNERS + f])
    counts = []
    for f in range(FITS):
        shard = shards_of(f, info_ref[SIZES + f])
        counts.append(jnp.sum(jnp.where(shard == source, 1.0, 0.0), axis=1, keepdims=True))
    dest_ref[...] = jnp.full(dest_ref.shape, -1, jnp.int32)
    out_ref[OVER] = info_ref[OVER]
    for j in range(SLOTS):
        fit = jnp.maximum(fits[j], 0)
        size = info_ref[SIZES + fit]
        out_ref[SLOT_FIT + j] = fits[j]
        out_ref[SLOT_SIZE + j] = size
        shard = shards_of(fit, jnp.where(fits[j] >= 0, size, 0))
        first = jnp.zeros((shards, 1), F32)
        for f in range(FITS):
            ahead = (f < fit) & (info_ref[OWNERS + f] // PARTS == me // PARTS)
            first = first + counts[f] * ahead.astype(F32)
        held = jnp.where(shard == source, 1.0, 0.0)
        place, _ = running(held)
        rank = jnp.sum(held * (place - 1.0 + first), axis=0, keepdims=True).astype(jnp.int32)
        part = sum((rank >= k * ROOM).astype(jnp.int32) for k in range(1, PARTS))
        center = sum(jnp.where(fit == f, middle[f], 0) for f in range(FITS))
        step = jnp.full(part.shape, DEALT[0], jnp.int32)
        for k in range(1, PARTS):
            step = jnp.where(part == k, DEALT[k], step)
        turn = (me - center - step) & (PARTS - 1)
        dest = shard * ROOM + rank - part * ROOM + turn * (shards * ROOM)
        dest_ref[j : j + 1, :] = jnp.where(shard >= 0, dest, -1)
        for b in range(PARTS):
            here = jnp.where((shard >= 0) & (turn == b), 1, 0)
            out_ref[USED + j * PARTS + b] = jnp.max(here)


def plan(info, indices, after, shards, shift):
    return pl.pallas_call(
        lambda *refs: plan_kernel(shift, shards, *refs),
        out_shape=(
            jax.ShapeDtypeStruct(indices.shape, jnp.int32),
            jax.ShapeDtypeStruct((INFO,), jnp.int32),
        ),
        in_specs=[SMEM, VMEM, pl.BlockSpec(memory_space=pl.ANY)],
        out_specs=(VMEM, SMEM),
        compiler_params=room(8),
        cost_estimate=cost(10**10, 10**6),
        name="plan",
    )(info, indices, after)


def any_of(slots, info_ref):
    return functools.reduce(jnp.maximum, [info_ref[SLOT_FIT + j] for j in slots]) >= 0


def add_found(slots, turns, blocks, info_ref, dest_ref, total_ref, base=0):
    span = 256
    width = dest_ref.shape[1]
    columns = slice((slots[0] - base) * width, (slots[-1] + 1 - base) * width)
    dest = jnp.concatenate([dest_ref[j : j + 1, :] for j in slots], axis=1)
    block = lax.shift_right_arithmetic(dest, 8)
    offset = dest & (span - 1)
    for b, block_ref in zip(turns, blocks):
        used = sum(info_ref[USED + j * PARTS + b] for j in slots)

        @pl.when(used > 0)
        def _():
            pick = jnp.where(offset == iota((span, offset.shape[1]), 0), 1.0, 0.0).astype(BF16)
            pieces = block_ref.shape[1] // span
            stacked = jnp.concatenate(
                [block_ref[:, n * span : (n + 1) * span] for n in range(pieces)], axis=0
            )
            found = dot(stacked, pick)
            total = total_ref[:, columns]
            for n in range(pieces):
                total = jnp.where(block == b * pieces + n, found[n * HD : (n + 1) * HD], total)
            total_ref[:, columns] = total


def order_kernel(turn, info_ref, dest_ref, block_ref, before_ref, out_ref, total_ref, *held):
    if turn == 0:
        total_ref[...] = jnp.zeros(total_ref.shape, F32)
    else:
        total_ref[...] = before_ref[...].astype(F32)
    for j in range(SLOTS):
        add_found((j,), (turn,), (block_ref,), info_ref, dest_ref, total_ref)
    if turn == 0:
        out_ref[...] = total_ref[...].astype(BF16)
    else:
        held_ref, sem = held
        held_ref[...] = total_ref[...].astype(BF16)
        copy = pltpu.make_async_copy(held_ref, out_ref, sem)
        copy.start()
        copy.wait()


def ordered(turn, info, dest, block, before):
    shape = (HD, SLOTS * CMAX)
    anywhere = pl.BlockSpec(memory_space=pl.ANY)
    in_hbm = pl.BlockSpec(memory_space=pltpu.HBM)
    return pl.pallas_call(
        lambda *refs: order_kernel(turn, *refs),
        out_shape=pltpu.HBM(shape, BF16) if turn else jax.ShapeDtypeStruct(shape, BF16),
        in_specs=[SMEM, VMEM, VMEM, VMEM if turn else anywhere],
        out_specs=in_hbm if turn else VMEM,
        scratch_shapes=[pltpu.VMEM(shape, F32)]
        + ([pltpu.VMEM(shape, BF16), pltpu.SemaphoreType.DMA(())] if turn else []),
        compiler_params=room(16),
        cost_estimate=cost(2 * 10**9, 3 * 10**6),
        name="order_%d" % turn,
    )(info, dest, block, before)


def build_systems(slots, info_ref, recv_ref, keys_ref):
    count = recv_ref.shape[0] * 8
    width = CMAX
    eye = iota((count, count), 0) == iota((count, count), 1)
    lane = iota((1, width), 1)
    results = []
    rows = recv_ref[:, ROOM:ROWS, :]
    layers = layer_rows(rows, 0), layer_rows(rows, 1)
    for j in slots:
        live = info_ref[SLOT_FIT + j] >= 0
        size = info_ref[SLOT_SIZE + j]
        second = (info_ref[SLOT_FIT + j] >= FITS_LAYER).astype(F32)
        query = jnp.where(second > 0.5, layers[1], layers[0]).astype(BF16)
        scores = dot(query, keys_ref[:, (j - slots[0]) * width : (j - slots[0] + 1) * width]) * SCALE
        scores = jnp.where(lane < size, scores, -jnp.inf)
        expo = jnp.exp(scores - jnp.max(scores, axis=1, keepdims=True))
        probs = (expo / jnp.sum(expo, axis=1, keepdims=True)).astype(BF16)
        turned_probs = probs.astype(F32).T.astype(BF16)
        gram = dot(probs, turned_probs)
        trace = jnp.sum(jnp.where(eye, gram, 0.0))
        ridge = RIDGE * trace / size.astype(F32)
        sums = jnp.sum(gram, axis=0, keepdims=True)
        ratios = jnp.sum(gram * sums, axis=1, keepdims=True) / jnp.sum(gram, axis=1, keepdims=True)
        top = jnp.minimum(BOUND * jnp.max(ratios), trace) + ridge
        taken = live.astype(F32)
        system = jnp.where(taken > 0.5, gram, 0.0) + jnp.where(
            eye, jnp.where(live, ridge, 1.0), 0.0
        )
        ends = jnp.where(live, ridge, 1.0), jnp.where(live, top, 1.0)
        results.append((system, turned_probs, ends))
    return results


def found_systems(
    slots, info_ref, dest_ref, recv_ref, back_ref, far_ref, part_ref, spare_ref, keys_ref, total_ref
):
    width = dest_ref.shape[1]
    turns = PARTS - 1, PARTS // 2
    late = sum(info_ref[USED + j * PARTS + turn] for j in slots for turn in turns)
    pltpu.sync_copy(part_ref.at[:, pl.ds(slots[0] * width, len(slots) * width)], keys_ref)

    @pl.when((info_ref[OVER] == 0) & (late > 0))
    def _():
        total_ref[...] = keys_ref[...].astype(F32)
        for j in slots:
            add_found((j,), turns, (back_ref, far_ref), info_ref, dest_ref, total_ref, slots[0])
        keys_ref[...] = total_ref[...].astype(BF16)

    @pl.when(info_ref[OVER] > 0)
    def _():
        for i, j in enumerate(slots):
            pltpu.sync_copy(spare_ref.at[j], keys_ref.at[:, pl.ds(i * width, width)])

    return build_systems(slots, info_ref, recv_ref, keys_ref)


def first_kernel(
    info_ref, dest_ref, recv_ref, back_ref, far_ref, part_ref, spare_ref, probs_ref, sys_ref,
    ends_ref, keys_ref, total_ref, held_ref, sem
):
    live = any_of((0,), info_ref)
    copy = pltpu.make_async_copy(held_ref, probs_ref, sem)

    @pl.when(live)
    def _():
        ((system, probs, ends),) = found_systems(
            (0,), info_ref, dest_ref, recv_ref, back_ref, far_ref, part_ref, spare_ref, keys_ref,
            total_ref
        )
        held_ref[0] = probs
        copy.start()
        sys_ref[0] = system
        ends_ref[0] = jnp.where(iota((8, LANES), 0) == 0, ends[0], ends[1])
        copy.wait()

    @pl.when(jnp.logical_not(live))
    def _():
        sys_ref[...] = jnp.zeros(sys_ref.shape, F32)
        ends_ref[...] = jnp.full(ends_ref.shape, 1.0, F32)


def first_system(info, dest, received, back, far, part, spare):
    count = received.shape[0] * 8
    in_hbm = pl.BlockSpec(memory_space=pltpu.HBM)
    return pl.pallas_call(
        first_kernel,
        out_shape=(
            pltpu.HBM((1, CMAX, count), BF16),
            jax.ShapeDtypeStruct((1, count, count), F32),
            jax.ShapeDtypeStruct((1, 8, LANES), F32),
        ),
        in_specs=[SMEM] + [VMEM] * 4 + [in_hbm] * 2,
        out_specs=(in_hbm, VMEM, VMEM),
        scratch_shapes=[
            pltpu.VMEM((HD, CMAX), BF16),
            pltpu.VMEM((HD, CMAX), F32),
            pltpu.VMEM((1, CMAX, count), BF16),
            pltpu.SemaphoreType.DMA(()),
        ],
        compiler_params=room(24),
        cost_estimate=cost(10**9, 3 * 10**6, 10**6),
        name="first_system",
    )(
        info,
        dest,
        received,
        back,
        far,
        pltpu.with_memory_space_constraint(part, pltpu.HBM),
        pltpu.with_memory_space_constraint(spare, pltpu.HBM),
    )


def split(x):
    high = x.astype(BF16)
    return high, (x - high.astype(F32)).astype(BF16)


def split3(x):
    high, _ = split(x)
    rest = x - high.astype(F32)
    middle, low = split(rest)
    return high, middle, low


def product(a, b):
    (a_high, a_low), (b_high, b_low) = a, b
    return dot(
        jnp.concatenate([a_high, a_high, a_low], axis=1),
        jnp.concatenate([b_high, b_low, b_high], axis=0),
    )


def product_full(a, b):
    (a0, a1, a2), (b0, b1, b2) = split3(a), split3(b)
    return dot(
        jnp.concatenate([a0, a0, a1, a0, a1, a2], axis=1),
        jnp.concatenate([b0, b1, b0, b2, b1, b0], axis=0),
    )


def finish_kernel(
    info_ref, dest_ref, recv_ref, back_ref, far_ref, first_ref, first_ends_ref, part_ref, spare_ref,
    probs_ref, inverse_ref, keys_ref, total_ref, held_ref, sys_ref, parts_ref, out_ref, sems
):
    count = first_ref.shape[1]
    eye = iota((count, count), 0) == iota((count, count), 1)
    held_systems = [first_ref.at[0], sys_ref.at[0], sys_ref.at[1]]
    more = any_of((1, 2), info_ref)
    one = jnp.logical_not(more) & (info_ref[SLOT_FIT] >= 0)
    probs_copy = pltpu.make_async_copy(held_ref, probs_ref, sems.at[0])

    def copy(j):
        return pltpu.make_async_copy(out_ref.at[j], inverse_ref.at[j], sems.at[1 + j])

    def start(j, low, high):
        middle = 2.0 / (low + high)
        system = held_systems[j][...]
        out_ref[j] = middle * (jnp.where(eye, 2.0, 0.0) - middle * system)
        parts_ref[j, 0], parts_ref[j, 1] = split(system)
        ratio = (high - low) / (high + low)
        return 1.0 - ratio * ratio

    def step(slots, lows, last=False, full=False):
        nexts = []
        for j, lowest in zip(slots, lows):
            held = out_ref[j]
            middle = 2.0 / (lowest + 1.0)
            parts = split(held)
            if full:
                images = product_full(held_systems[j][...], held)
            else:
                images = product((parts_ref[j, 0], parts_ref[j, 1]), parts)
            rest = jnp.where(eye, 1.0, 0.0) - middle * images
            if last:
                moved = dot(parts[0], rest.astype(BF16))
            else:
                moved = product(parts, split(rest))
            out_ref[j] = middle * (held + moved)
            ratio = (1.0 - lowest) / (1.0 + lowest)
            nexts.append(1.0 - ratio * ratio)
        return tuple(nexts)

    def solve(slots, lows):
        stiff = functools.reduce(jnp.minimum, lows) < STIFF
        lows = lax.while_loop(
            lambda lows: functools.reduce(jnp.minimum, lows) < CLOSE,
            functools.partial(step, slots),
            lows,
        )

        @pl.when(stiff)
        def _():
            step(slots, lows, full=True)

        @pl.when(jnp.logical_not(stiff))
        def _():
            step(slots, lows, last=True)

        for j in slots:
            copy(j).start()

    first_ends = jnp.max(first_ends_ref[0, 0:1, :]), jnp.max(first_ends_ref[0, 1:2, :])

    @pl.when(more)
    def _():
        found = found_systems(
            (1, 2), info_ref, dest_ref, recv_ref, back_ref, far_ref, part_ref, spare_ref, keys_ref,
            total_ref
        )
        lows = [start(0, *first_ends)]
        for i, (system, probs, ends) in enumerate(found):
            held_ref[i] = probs
            sys_ref[i] = system
            lows.append(start(1 + i, *ends))
        probs_copy.start()
        solve((0, 1, 2), tuple(lows))
        probs_copy.wait()
        for j in range(SLOTS):
            copy(j).wait()

    @pl.when(one)
    def _():
        solve((0,), (start(0, *first_ends),))
        copy(0).wait()


def finish(info, dest, received, back, far, part, spare, first, first_ends):
    count = first.shape[1]
    in_hbm = pl.BlockSpec(memory_space=pltpu.HBM)
    return pl.pallas_call(
        finish_kernel,
        out_shape=(
            pltpu.HBM((SLOTS - 1, CMAX, count), BF16),
            pltpu.HBM((SLOTS, count, count), F32),
        ),
        in_specs=[SMEM] + [VMEM] * 6 + [in_hbm] * 2,
        out_specs=(in_hbm, in_hbm),
        scratch_shapes=[
            pltpu.VMEM((HD, (SLOTS - 1) * CMAX), BF16),
            pltpu.VMEM((HD, (SLOTS - 1) * CMAX), F32),
            pltpu.VMEM((SLOTS - 1, CMAX, count), BF16),
            pltpu.VMEM((SLOTS - 1, count, count), F32),
            pltpu.VMEM((SLOTS, 2, count, count), BF16),
            pltpu.VMEM((SLOTS, count, count), F32),
            pltpu.SemaphoreType.DMA((1 + SLOTS,)),
        ],
        compiler_params=room(32),
        cost_estimate=cost(8 * 10**9, 4 * 10**6, 10**6),
        name="finish_systems",
    )(
        info,
        dest,
        received,
        back,
        far,
        first,
        first_ends,
        pltpu.with_memory_space_constraint(part, pltpu.HBM),
        pltpu.with_memory_space_constraint(spare, pltpu.HBM),
    )


def values_kernel(
    info_ref, target_ref, inverse_ref, first_ref, other_ref, out_ref, inv, held, result, sems
):
    fits = [info_ref[SLOT_FIT + j] for j in range(SLOTS)]
    sources = [first_ref.at[0], other_ref.at[0], other_ref.at[1]]
    more = any_of((1, 2), info_ref)

    def copies(j):
        return (
            pltpu.make_async_copy(inverse_ref.at[j], inv.at[j], sems.at[0, j]),
            pltpu.make_async_copy(sources[j], held.at[j], sems.at[1, j]),
        )

    def copy_out(j):
        return pltpu.make_async_copy(result.at[j], out_ref.at[0, j], sems.at[2, j])

    def clear(j):
        result[j] = jnp.zeros(result.shape[1:], BF16)
        copy_out(j).start()

    def fill(slots):
        for j in slots:
            for copy in copies(j):
                copy.start()
        rows = target_ref[...]
        layers = layer_rows(rows, 0), layer_rows(rows, 1)
        for j in slots:
            for copy in copies(j):
                copy.wait()
        weights = []
        for j in slots:
            second = (fits[j] >= FITS_LAYER).astype(F32)
            target = jnp.where(second > 0.5, layers[1], layers[0]).astype(BF16)
            weights.append(
                dot(
                    jnp.concatenate(split3(inv[j]), axis=1),
                    jnp.concatenate([target] * 3, axis=0),
                )
            )
        for j, weight in zip(slots, weights):
            high, low = split(weight)
            probs = held[j]
            found = dot(
                jnp.concatenate([probs, probs], axis=1), jnp.concatenate([high, low], axis=0)
            )
            taken = (fits[j] >= 0).astype(F32)
            result[j] = jnp.where(taken > 0.5, found, 0.0).astype(BF16)
            copy_out(j).start()

    @pl.when(more)
    def _():
        fill((0, 1, 2))

    @pl.when(jnp.logical_not(more))
    def _():
        clear(1)
        clear(2)

        @pl.when(fits[0] >= 0)
        def _():
            fill((0,))

        @pl.when(fits[0] < 0)
        def _():
            clear(0)

    for j in range(SLOTS):
        copy_out(j).wait()


def fitted_values(info, inverse, first, other, target):
    anywhere = pl.BlockSpec(memory_space=pltpu.HBM)
    count = inverse.shape[1]
    return pl.pallas_call(
        values_kernel,
        out_shape=pltpu.HBM((1, SLOTS, CMAX, HD), BF16),
        in_specs=[SMEM, VMEM, anywhere, anywhere, anywhere],
        out_specs=pl.BlockSpec(memory_space=pltpu.HBM),
        scratch_shapes=[
            pltpu.VMEM((SLOTS, count, count), F32),
            pltpu.VMEM((SLOTS, CMAX, count), BF16),
            pltpu.VMEM((SLOTS, CMAX, HD), BF16),
            pltpu.SemaphoreType.DMA((3, SLOTS)),
        ],
        compiler_params=room(16),
        cost_estimate=cost(10**9, 4 * 10**6),
        name="fitted_values",
    )(
        info,
        target,
        pltpu.with_memory_space_constraint(inverse, pltpu.HBM),
        pltpu.with_memory_space_constraint(first, pltpu.HBM),
        pltpu.with_memory_space_constraint(other, pltpu.HBM),
    )


def exchange(blocks):
    return lax.all_to_all(blocks, SEQ, split_axis=0, concat_axis=0, tiled=True)


def gathered_keys(owners, indices, keys):
    layers, local, width = keys.shape
    shards = lax.axis_size(SEQ)
    me = lax.axis_index(SEQ)
    fits = indices.shape[0]
    fit_ids = jnp.arange(fits, dtype=jnp.int32)
    offset = indices - me * local
    inside = (offset >= 0) & (offset < local)
    source = (fit_ids // FITS_LAYER)[:, None] * local + jnp.clip(offset, 0, local - 1)
    picked = jnp.take(keys.reshape(layers * local, width), source, axis=0)
    found = jnp.where(inside[..., None], picked, jnp.zeros((), picked.dtype))
    ring = [(k, (k + 1) % shards) for k in range(shards)]

    def pass_on(_, carried):
        moving, whole = carried
        moving = lax.ppermute(moving, SEQ, ring)
        return moving, whole + moving

    _, everything = lax.fori_loop(0, shards - 1, pass_on, (found, found))
    mine = owners[0] == me
    earlier = jnp.sum(
        jnp.where(mine[None, :] & (fit_ids[:, None] > fit_ids[None, :]), 1, 0), axis=1
    )
    chosen = [
        everything[jnp.sum(jnp.where(mine & (earlier == slot), fit_ids, 0))]
        for slot in range(SLOTS)
    ]
    return jnp.swapaxes(jnp.stack(chosen), 1, 2)


def on_device(queries, keys, values, indices, sizes, owners):
    layers, _, local, width = keys.shape
    key_rows = keys.reshape(layers, local, width)
    value_rows = values.reshape(layers, local, width)
    positions = indices[0]
    shards = lax.axis_size(SEQ)
    regrouped = lax.all_to_all(queries, "head", split_axis=1, concat_axis=2, tiled=True)
    own_rows = regrouped.reshape(1, 16, width)
    packed, info = pack_keys(owners, sizes, positions, key_rows, shards)
    packed = lax.dynamic_update_slice(
        packed, jnp.broadcast_to(own_rows, (shards, 16, width)), (0, ROOM, 0)
    )
    received = exchange(packed)
    spare = lax.cond(
        info[OVER] > 0,
        lambda: gathered_keys(owners, positions, key_rows),
        lambda: jnp.zeros((SLOTS, width, CMAX), BF16),
    )
    dest, owned = plan(info, positions, spare, shards, local.bit_length() - 1)
    own_block = turned(received, dest)
    near, back, far = (
        lax.ppermute(own_block, "seq_1", [(k, (k + d) % PARTS) for k in range(PARTS)])
        for d in (1, PARTS - 1, PARTS // 2)
    )
    attended = attend(received, key_rows, value_rows)
    parts = exchange(attended)
    ordering = ordered(0, owned, dest, own_block, attended)
    ordering = ordered(1, owned, dest, near, ordering)
    late = dest, received, back, far, ordering, spare
    first_probs, first, first_ends = first_system(owned, *late)
    target = exchange(join(parts, first))
    other_probs, inverse = finish(owned, *late, first, first_ends)
    return fitted_values(owned, inverse, first_probs, other_probs, target)


def solution(mesh):
    apart = Mesh(mesh.devices.reshape(mesh.shape["head"], 8, 4), ("head", "seq_0", "seq_1"))
    placed = (
        P(None, None, HEAD_SEQ, None),
        P(None, "head", SEQ, None),
        P(None, "head", SEQ, None),
        P("head", None, None),
        P("head", None),
        P("head", None),
    )
    return jax.shard_map(
        on_device,
        mesh=apart,
        in_specs=placed,
        out_specs=P("head", SEQ, None, None),
        check_vma=False,
    )
```

```python
import functools

import jax
import jax.numpy as jnp
from jax import lax
from jax.experimental import pallas as pl
from jax.experimental.pallas import tpu as pltpu
from jax.sharding import Mesh
from jax.sharding import PartitionSpec as P

FITS = 8
FITS_LAYER = 4
SLOTS = 3
CMAX = 1024
HD = 128
LANES = 128
ROOM = 48
ROWS = ROOM + 16
PARTS = 4
CLOSE = 0.97
STIFF = 0.004
BOUND = 1.001
RIDGE = 0.3
DEALT = (0, 1, 3, 2)
OVER, ME, OWNERS, SIZES, INFO = 0, 1, 2, 10, 32
SLOT_FIT, SLOT_SIZE, USED = 1, 4, 8
SCALE = HD ** (-0.5)
SEQ = ("seq_0", "seq_1")
HEAD_SEQ = ("head", "seq_0", "seq_1")
F32 = jnp.float32
BF16 = jnp.bfloat16


def room(mib):
    return pltpu.CompilerParams(vmem_limit_bytes=mib << 20)


SMEM = pl.BlockSpec(memory_space=pltpu.SMEM)
VMEM = pl.BlockSpec(memory_space=pltpu.VMEM)


def cost(flops, moved, exps=0):
    return pl.CostEstimate(flops=flops, transcendentals=exps, bytes_accessed=moved)


def iota(shape, dim):
    return lax.broadcasted_iota(jnp.int32, shape, dim)


def fiota(shape, dim):
    return iota(shape, dim).astype(F32)


def dot(a, b, dims=((1,), (0,))):
    return lax.dot_general(a, b, (dims, ((), ())), preferred_element_type=F32)


def running(mask):
    rows, width = mask.shape
    blocks = width // LANES
    upper = (iota((LANES, LANES), 0) <= iota((LANES, LANES), 1)).astype(BF16)
    stacked = jnp.concatenate(
        [mask[:, b * LANES : (b + 1) * LANES] for b in range(blocks)], axis=0
    )
    inner = dot(stacked.astype(BF16), upper)
    carry = jnp.zeros((rows, 1), F32)
    parts = []
    for b in range(blocks):
        part = inner[b * rows : (b + 1) * rows]
        parts.append(part + carry)
        carry = carry + part[:, LANES - 1 : LANES]
    return jnp.concatenate(parts, axis=1), carry


def heaviest(owner_of):
    owners = [owner_of(f) for f in range(FITS)]
    number = [sum((a == b).astype(jnp.int32) for b in owners) for a in owners]
    places = []
    for f in range(FITS):
        best, place = jnp.int32(0), jnp.int32(0)
        for g in range(FITS):
            better = (owners[g] // PARTS == owners[f] // PARTS) & (number[g] > best)
            best = jnp.where(better, number[g], best)
            place = jnp.where(better, owners[g] & (PARTS - 1), place)
        places.append(place)
    return places


def send_kernel(
    shards, own_hbm, size_hbm, idx_ref, keys_ref, send_ref, info_ref, own_ref, size_ref, sems
):
    copies = [
        pltpu.make_async_copy(own_hbm, own_ref, sems.at[0]),
        pltpu.make_async_copy(size_hbm, size_ref, sems.at[1]),
    ]
    for copy in copies:
        copy.start()
    send_ref[...] = jnp.zeros(send_ref.shape, BF16)
    for copy in copies:
        copy.wait()
    me = lax.axis_index(SEQ).astype(jnp.int32)
    local = keys_ref.shape[1]
    shift = local.bit_length() - 1
    fits, width = idx_ref.shape
    idx = idx_ref[...]
    row = iota((fits, width), 0)
    lane = iota((fits, width), 1)
    size = jnp.zeros((fits, width), jnp.int32)
    own = jnp.zeros((fits, LANES), jnp.int32)
    row1 = iota((fits, LANES), 0)
    lane1 = iota((fits, LANES), 1)
    for f in range(fits):
        size = jnp.where(row == f, size_ref[0, f], size)
        own = jnp.where(row1 == f, own_ref[0, f] // PARTS, own)
    shard = jnp.where(lane < size, lax.shift_right_logical(idx, shift), -1)
    counts = jnp.zeros((fits, LANES), F32)
    for s in range(shards):
        count = jnp.sum(jnp.where(shard == s, 1.0, 0.0), axis=1, keepdims=True)
        counts = jnp.where(lane1 == s, count, counts)
    total = jnp.zeros((fits, LANES), F32)
    before = jnp.zeros((fits, LANES), F32)
    for f in range(fits):
        shared = jnp.where(own == own_ref[0, f] // PARTS, counts[f : f + 1, :], 0.0)
        total = total + shared
        before = before + jnp.where(row1 > f, shared, 0.0)
    info_ref[OVER] = (jnp.max(total) > PARTS * ROOM).astype(jnp.int32)
    info_ref[ME] = me
    for f in range(fits):
        info_ref[OWNERS + f] = own_ref[0, f]
        info_ref[SIZES + f] = size_ref[0, f]
    first = jnp.sum(jnp.where(lane1 == me, before, 0.0), axis=1, keepdims=True)
    mine = shard == me
    held = jnp.where(mine, 1.0, 0.0)
    place, _ = running(held)
    place = jnp.where(mine, place - 1.0 + first, -1.0)
    spot = jnp.where(mine, idx - me * local + 1, 0).astype(F32)
    slot = fiota((PARTS * ROOM, width), 0)
    at = fiota((PARTS * ROOM, local), 1)
    middle = heaviest(lambda f: own_ref[0, f])
    for f in range(fits):
        here = place[f : f + 1, :] == slot
        pos = jnp.sum(jnp.where(here, spot[f : f + 1, :], 0.0), axis=1, keepdims=True) - 1.0
        pick = jnp.where(pos == at, 1.0, 0.0).astype(BF16)
        rows = dot(pick, keys_ref[f // FITS_LAYER])
        rows = rows.astype(BF16)
        to = own_ref[0, f] // PARTS * PARTS
        for part, step in enumerate(DEALT):
            place_along = (middle[f] + step) & (PARTS - 1)
            send_ref[to + place_along, 0:ROOM, :] += rows[part * ROOM : (part + 1) * ROOM]


def pack_keys(owners, sizes, indices, keys, shards):
    return pl.pallas_call(
        lambda *refs: send_kernel(shards, *refs),
        out_shape=(
            jax.ShapeDtypeStruct((shards, ROWS, LANES), BF16),
            jax.ShapeDtypeStruct((INFO,), jnp.int32),
        ),
        in_specs=[pl.BlockSpec(memory_space=pltpu.HBM)] * 2 + [VMEM, VMEM],
        out_specs=(VMEM, SMEM),
        scratch_shapes=[
            pltpu.SMEM((1, FITS), jnp.int32),
            pltpu.SMEM((1, FITS), jnp.int32),
            pltpu.SemaphoreType.DMA((2,)),
        ],
        compiler_params=room(24),
        cost_estimate=cost(10**9, 3 * 10**6),
        name="pack_keys",
    )(
        pltpu.with_memory_space_constraint(owners, pltpu.HBM),
        pltpu.with_memory_space_constraint(sizes, pltpu.HBM),
        indices,
        keys,
    )


def slots_of(me, info_ref):
    found = [jnp.int32(-1)] * SLOTS
    seen = jnp.int32(0)
    for f in range(FITS):
        match = info_ref[OWNERS + f] == me
        for j in range(SLOTS):
            found[j] = jnp.where(match & (seen == j), f, found[j])
        seen = seen + match.astype(jnp.int32)
    return found


def layer_rows(rows, layer):
    wide = rows.astype(F32)[:, 8 * layer : 8 * layer + 8, :]
    return wide.reshape(-1, wide.shape[-1])


def attend_kernel(recv_ref, keys_ref, values_ref, out_ref):
    shards = recv_ref.shape[0]
    outs = []
    stat = jnp.zeros((shards * 8, LANES), F32)
    lane = iota(stat.shape, 1)
    for layer in range(2):
        query = layer_rows(recv_ref[...], layer).astype(BF16)
        scores = dot(query, keys_ref[layer], ((1,), (1,))) * SCALE
        peak = jnp.max(scores, axis=1, keepdims=True)
        weights = jnp.exp(scores - peak)
        total = jnp.sum(weights, axis=1, keepdims=True)
        numer = dot(weights.astype(BF16), values_ref[layer])
        outs.append((numer / total).reshape(shards, 8, HD))
        level = peak + jnp.log(total)
        high = level.astype(BF16).astype(F32)
        middle = (level - high).astype(BF16).astype(F32)
        for k, piece in enumerate((high, middle, level - high - middle)):
            stat = jnp.where(lane == 64 * layer + k, piece, stat)
    out_ref[:, 0:16, :] = jnp.concatenate(outs, axis=1).astype(BF16)
    out_ref[:, 16:24, :] = stat.reshape(shards, 8, LANES).astype(BF16)


def attend(received, keys, values):
    shards = received.shape[0]
    return pl.pallas_call(
        attend_kernel,
        out_shape=jax.ShapeDtypeStruct((shards, 24, LANES), BF16),
        grid=(1,),
        in_specs=[
            pl.BlockSpec((shards, 16, LANES), lambda i: (0, ROOM // 16, 0)),
            pl.BlockSpec(keys.shape, lambda i: (0, 0, 0)),
            pl.BlockSpec(values.shape, lambda i: (0, 0, 0)),
        ],
        out_specs=pl.BlockSpec((shards, 24, LANES), lambda i: (0, 0, 0)),
        compiler_params=room(24),
        cost_estimate=cost(5 * 10**8, 3 * 10**6, 10**6),
        name="attend",
    )(received, keys, values)


def join_kernel(parts_ref, after_ref, out_ref):
    parts = parts_ref[...].astype(F32)
    stat = parts[:, 16:24, :]
    first = iota(stat.shape, 2) < 64
    level = jnp.concatenate(
        [
            jnp.sum(jnp.where(first, stat, 0.0), axis=2, keepdims=True),
            jnp.sum(jnp.where(first, 0.0, stat), axis=2, keepdims=True),
        ],
        axis=1,
    )
    weights = jnp.exp(level - jnp.max(level, axis=0, keepdims=True))
    numer = jnp.sum(weights * parts[:, 0:16, :], axis=0, keepdims=True)
    target = numer / jnp.sum(weights, axis=0, keepdims=True)
    out_ref[...] = jnp.broadcast_to(target, out_ref.shape).astype(BF16)


def join(parts, after):
    shards = parts.shape[0]
    return pl.pallas_call(
        join_kernel,
        out_shape=jax.ShapeDtypeStruct((shards, 16, LANES), BF16),
        in_specs=[VMEM, pl.BlockSpec(memory_space=pl.ANY)],
        out_specs=VMEM,
        compiler_params=room(8),
        cost_estimate=cost(10**6, 4 * 10**5, 10**3),
        name="join_parts",
    )(parts, after)


def turn_kernel(recv_ref, after_ref, out_ref):
    rows = recv_ref[:, 0:ROOM, :]
    out_ref[...] = rows.reshape(-1, HD).astype(F32).T.astype(BF16)


def turned(received, after):
    return pl.pallas_call(
        turn_kernel,
        out_shape=jax.ShapeDtypeStruct((HD, received.shape[0] * ROOM), BF16),
        in_specs=[VMEM, pl.BlockSpec(memory_space=pl.ANY)],
        out_specs=VMEM,
        compiler_params=room(8),
        cost_estimate=cost(10**6, 10**6),
        name="turn_keys",
    )(received, after)


def plan_kernel(shift, shards, info_ref, idx_ref, after_ref, dest_ref, out_ref):
    width = idx_ref.shape[1]
    me = info_ref[ME]
    fits = slots_of(me, info_ref)
    lane = iota((1, width), 1)
    source = iota((shards, width), 0)

    def shards_of(fit, size):
        place = lax.shift_right_logical(idx_ref[pl.ds(fit, 1), :], shift)
        return jnp.where(lane < size, place, -1)

    middle = heaviest(lambda f: info_ref[OWNERS + f])
    counts = []
    for f in range(FITS):
        shard = shards_of(f, info_ref[SIZES + f])
        counts.append(jnp.sum(jnp.where(shard == source, 1.0, 0.0), axis=1, keepdims=True))
    dest_ref[...] = jnp.full(dest_ref.shape, -1, jnp.int32)
    out_ref[OVER] = info_ref[OVER]
    for j in range(SLOTS):
        fit = jnp.maximum(fits[j], 0)
        size = info_ref[SIZES + fit]
        out_ref[SLOT_FIT + j] = fits[j]
        out_ref[SLOT_SIZE + j] = size
        shard = shards_of(fit, jnp.where(fits[j] >= 0, size, 0))
        first = jnp.zeros((shards, 1), F32)
        for f in range(FITS):
            ahead = (f < fit) & (info_ref[OWNERS + f] // PARTS == me // PARTS)
            first = first + counts[f] * ahead.astype(F32)
        held = jnp.where(shard == source, 1.0, 0.0)
        place, _ = running(held)
        rank = jnp.sum(held * (place - 1.0 + first), axis=0, keepdims=True).astype(jnp.int32)
        part = sum((rank >= k * ROOM).astype(jnp.int32) for k in range(1, PARTS))
        center = sum(jnp.where(fit == f, middle[f], 0) for f in range(FITS))
        step = jnp.full(part.shape, DEALT[0], jnp.int32)
        for k in range(1, PARTS):
            step = jnp.where(part == k, DEALT[k], step)
        turn = (me - center - step) & (PARTS - 1)
        dest = shard * ROOM + rank - part * ROOM + turn * (shards * ROOM)
        dest_ref[j : j + 1, :] = jnp.where(shard >= 0, dest, -1)
        for b in range(PARTS):
            here = jnp.where((shard >= 0) & (turn == b), 1, 0)
            out_ref[USED + j * PARTS + b] = jnp.max(here)


def plan(info, indices, after, shards, shift):
    return pl.pallas_call(
        lambda *refs: plan_kernel(shift, shards, *refs),
        out_shape=(
            jax.ShapeDtypeStruct(indices.shape, jnp.int32),
            jax.ShapeDtypeStruct((INFO,), jnp.int32),
        ),
        in_specs=[SMEM, VMEM, pl.BlockSpec(memory_space=pl.ANY)],
        out_specs=(VMEM, SMEM),
        compiler_params=room(8),
        cost_estimate=cost(10**10, 10**6),
        name="plan",
    )(info, indices, after)


def any_of(slots, info_ref):
    return functools.reduce(jnp.maximum, [info_ref[SLOT_FIT + j] for j in slots]) >= 0


def add_found(slots, turns, blocks, info_ref, dest_ref, total_ref):
    span = 256
    width = dest_ref.shape[1]
    columns = slice(slots[0] * width, (slots[-1] + 1) * width)
    dest = jnp.concatenate([dest_ref[j : j + 1, :] for j in slots], axis=1)
    block = lax.shift_right_arithmetic(dest, 8)
    offset = dest & (span - 1)
    for b, block_ref in zip(turns, blocks):
        used = sum(info_ref[USED + j * PARTS + b] for j in slots)

        @pl.when(used > 0)
        def _():
            pick = jnp.where(offset == iota((span, offset.shape[1]), 0), 1.0, 0.0).astype(BF16)
            pieces = block_ref.shape[1] // span
            stacked = jnp.concatenate(
                [block_ref[:, n * span : (n + 1) * span] for n in range(pieces)], axis=0
            )
            found = dot(stacked, pick)
            total = total_ref[:, columns]
            for n in range(pieces):
                total = jnp.where(block == b * pieces + n, found[n * HD : (n + 1) * HD], total)
            total_ref[:, columns] = total


def order_kernel(turn, info_ref, dest_ref, block_ref, *refs):
    out_ref, total_ref = refs[-2:]
    if turn == 0:
        total_ref[...] = jnp.zeros(total_ref.shape, F32)
    else:
        total_ref[...] = refs[0][...].astype(F32)
    for j in range(SLOTS):
        add_found((j,), (turn,), (block_ref,), info_ref, dest_ref, total_ref)
    out_ref[...] = total_ref[...].astype(BF16)


def ordered(turn, info, dest, block, before):
    anywhere = pl.BlockSpec(memory_space=pl.ANY)
    return pl.pallas_call(
        lambda *refs: order_kernel(turn, *refs),
        out_shape=jax.ShapeDtypeStruct((HD, SLOTS * CMAX), BF16),
        in_specs=[SMEM, VMEM, VMEM, VMEM if turn else anywhere],
        out_specs=VMEM,
        scratch_shapes=[pltpu.VMEM((HD, SLOTS * CMAX), F32)],
        compiler_params=room(16),
        cost_estimate=cost(2 * 10**9, 3 * 10**6),
        name="order_%d" % turn,
    )(info, dest, block, before)


def build_systems(slots, info_ref, recv_ref, keys_ref):
    count = recv_ref.shape[0] * 8
    width = CMAX
    eye = iota((count, count), 0) == iota((count, count), 1)
    lane = iota((1, width), 1)
    results = []
    rows = recv_ref[:, ROOM:ROWS, :]
    layers = layer_rows(rows, 0), layer_rows(rows, 1)
    for j in slots:
        live = info_ref[SLOT_FIT + j] >= 0
        size = info_ref[SLOT_SIZE + j]
        second = (info_ref[SLOT_FIT + j] >= FITS_LAYER).astype(F32)
        query = jnp.where(second > 0.5, layers[1], layers[0]).astype(BF16)
        scores = dot(query, keys_ref[:, j * width : (j + 1) * width]) * SCALE
        scores = jnp.where(lane < size, scores, -jnp.inf)
        expo = jnp.exp(scores - jnp.max(scores, axis=1, keepdims=True))
        probs = (expo / jnp.sum(expo, axis=1, keepdims=True)).astype(BF16)
        turned_probs = probs.astype(F32).T.astype(BF16)
        gram = dot(probs, turned_probs)
        trace = jnp.sum(jnp.where(eye, gram, 0.0))
        ridge = RIDGE * trace / size.astype(F32)
        sums = jnp.sum(gram, axis=0, keepdims=True)
        ratios = jnp.sum(gram * sums, axis=1, keepdims=True) / jnp.sum(gram, axis=1, keepdims=True)
        top = jnp.minimum(BOUND * jnp.max(ratios), trace) + ridge
        taken = live.astype(F32)
        system = jnp.where(taken > 0.5, gram, 0.0) + jnp.where(
            eye, jnp.where(live, ridge, 1.0), 0.0
        )
        ends = jnp.where(live, ridge, 1.0), jnp.where(live, top, 1.0)
        results.append((system, turned_probs, ends))
    return results


def system_kernel(
    info_ref, dest_ref, recv_ref, back_ref, far_ref, part_ref, spare_ref, probs_ref, sys_ref, ends_ref,
    keys_ref, total_ref, held_ref, sems
):
    count = sys_ref.shape[1]
    width = dest_ref.shape[1]
    eye = iota((count, count), 0) == iota((count, count), 1)
    turns = PARTS - 1, PARTS // 2
    late = sum(info_ref[USED + j * PARTS + turn] for j in range(SLOTS) for turn in turns)
    keys_ref[...] = part_ref[...]

    @pl.when((info_ref[OVER] == 0) & (late > 0))
    def _():
        total_ref[...] = part_ref[...].astype(F32)
        for j in range(SLOTS):
            add_found((j,), turns, (back_ref, far_ref), info_ref, dest_ref, total_ref)
        keys_ref[...] = total_ref[...].astype(BF16)

    @pl.when(info_ref[OVER] > 0)
    def _():
        for j in range(SLOTS):
            pltpu.sync_copy(spare_ref.at[j], keys_ref.at[:, pl.ds(j * width, width)])

    def copy(j):
        return pltpu.make_async_copy(held_ref.at[j], probs_ref.at[j], sems.at[j])

    def fill(slots):
        live = any_of(slots, info_ref)

        @pl.when(live)
        def _():
            found = build_systems(slots, info_ref, recv_ref, keys_ref)
            for j, (system, probs, ends) in zip(slots, found):
                held_ref[j] = probs
                copy(j).start()
                sys_ref[j] = system
                ends_ref[j] = jnp.where(iota((8, LANES), 0) == 0, ends[0], ends[1])

        @pl.when(jnp.logical_not(live))
        def _():
            for j in slots:
                sys_ref[j] = jnp.where(eye, 1.0, 0.0)
                ends_ref[j] = jnp.full((8, LANES), 1.0, F32)

    groups = (0,), (1, 2)
    for slots in groups:
        fill(slots)
    for slots in groups:

        @pl.when(any_of(slots, info_ref))
        def _():
            for j in slots:
                copy(j).wait()


def systems(info, dest, received, back, far, part, spare):
    count = received.shape[0] * 8
    return pl.pallas_call(
        system_kernel,
        out_shape=(
            pltpu.HBM((SLOTS, CMAX, count), BF16),
            jax.ShapeDtypeStruct((SLOTS, count, count), F32),
            jax.ShapeDtypeStruct((SLOTS, 8, LANES), F32),
        ),
        in_specs=[SMEM] + [VMEM] * 5 + [pl.BlockSpec(memory_space=pltpu.HBM)],
        out_specs=(pl.BlockSpec(memory_space=pltpu.HBM), VMEM, VMEM),
        scratch_shapes=[
            pltpu.VMEM((HD, SLOTS * CMAX), BF16),
            pltpu.VMEM((HD, SLOTS * CMAX), F32),
            pltpu.VMEM((SLOTS, CMAX, count), BF16),
            pltpu.SemaphoreType.DMA((SLOTS,)),
        ],
        compiler_params=room(32),
        cost_estimate=cost(3 * 10**9, 3 * 10**6, 10**6),
        name="systems",
    )(
        info,
        dest,
        received,
        back,
        far,
        part,
        pltpu.with_memory_space_constraint(spare, pltpu.HBM),
    )


def split(x):
    high = x.astype(BF16)
    return high, (x - high.astype(F32)).astype(BF16)


def split3(x):
    high, _ = split(x)
    rest = x - high.astype(F32)
    middle, low = split(rest)
    return high, middle, low


def product(a, b):
    (a_high, a_low), (b_high, b_low) = a, b
    return dot(
        jnp.concatenate([a_high, a_high, a_low], axis=1),
        jnp.concatenate([b_high, b_low, b_high], axis=0),
    )


def product_full(a, b):
    (a0, a1, a2), (b0, b1, b2) = split3(a), split3(b)
    return dot(
        jnp.concatenate([a0, a0, a1, a0, a1, a2], axis=1),
        jnp.concatenate([b0, b1, b0, b2, b1, b0], axis=0),
    )


def invert_kernel(info_ref, sys_ref, ends_ref, inverse_ref, parts_ref, out_ref, sems):
    count = sys_ref.shape[1]
    eye = iota((count, count), 0) == iota((count, count), 1)
    more = any_of((1, 2), info_ref)
    one = jnp.logical_not(more) & (info_ref[SLOT_FIT] >= 0)

    def copy(j):
        return pltpu.make_async_copy(out_ref.at[j], inverse_ref.at[j], sems.at[j])

    def start(slots):
        lows = []
        for j in slots:
            low = jnp.max(ends_ref[j, 0:1, :])
            high = jnp.max(ends_ref[j, 1:2, :])
            middle = 2.0 / (low + high)
            system = sys_ref[j]
            out_ref[j] = middle * (jnp.where(eye, 2.0, 0.0) - middle * system)
            parts_ref[j, 0], parts_ref[j, 1] = split(system)
            ratio = (high - low) / (high + low)
            lows.append(1.0 - ratio * ratio)
        return tuple(lows)

    def step(slots, lows, last=False, full=False):
        nexts = []
        for j, lowest in zip(slots, lows):
            held = out_ref[j]
            middle = 2.0 / (lowest + 1.0)
            parts = split(held)
            if full:
                images = product_full(sys_ref[j], held)
            else:
                images = product((parts_ref[j, 0], parts_ref[j, 1]), parts)
            rest = jnp.where(eye, 1.0, 0.0) - middle * images
            if last:
                moved = dot(parts[0], rest.astype(BF16))
            else:
                moved = product(parts, split(rest))
            out_ref[j] = middle * (held + moved)
            ratio = (1.0 - lowest) / (1.0 + lowest)
            nexts.append(1.0 - ratio * ratio)
        return tuple(nexts)

    def solve(slots):
        lows = start(slots)
        stiff = functools.reduce(jnp.minimum, lows) < STIFF
        lows = lax.while_loop(
            lambda lows: functools.reduce(jnp.minimum, lows) < CLOSE,
            functools.partial(step, slots),
            lows,
        )

        @pl.when(stiff)
        def _():
            step(slots, lows, full=True)

        @pl.when(jnp.logical_not(stiff))
        def _():
            step(slots, lows, last=True)

        for j in slots:
            copy(j).start()
        for j in slots:
            copy(j).wait()

    @pl.when(more)
    def _():
        solve((0, 1, 2))

    @pl.when(one)
    def _():
        solve((0,))


def invert(info, system, ends):
    return pl.pallas_call(
        invert_kernel,
        out_shape=pltpu.HBM(system.shape, F32),
        in_specs=[SMEM, VMEM, VMEM],
        out_specs=pl.BlockSpec(memory_space=pltpu.HBM),
        scratch_shapes=[
            pltpu.VMEM((SLOTS, 2, *system.shape[1:]), BF16),
            pltpu.VMEM(system.shape, F32),
            pltpu.SemaphoreType.DMA((SLOTS,)),
        ],
        compiler_params=room(16),
        cost_estimate=cost(5 * 10**9, 2 * 10**6),
        name="invert",
    )(info, system, ends)


def values_kernel(
    info_ref, target_ref, inverse_ref, probs_ref, out_ref, inv, held, result, sems
):
    fits = [info_ref[SLOT_FIT + j] for j in range(SLOTS)]
    more = any_of((1, 2), info_ref)

    def copies(j):
        return (
            pltpu.make_async_copy(inverse_ref.at[j], inv.at[j], sems.at[0, j]),
            pltpu.make_async_copy(probs_ref.at[j], held.at[j], sems.at[1, j]),
        )

    def copy_out(j):
        return pltpu.make_async_copy(result.at[j], out_ref.at[0, j], sems.at[2, j])

    def clear(j):
        result[j] = jnp.zeros(result.shape[1:], BF16)
        copy_out(j).start()

    def fill(slots):
        for j in slots:
            for copy in copies(j):
                copy.start()
        rows = target_ref[...]
        layers = layer_rows(rows, 0), layer_rows(rows, 1)
        for j in slots:
            for copy in copies(j):
                copy.wait()
        weights = []
        for j in slots:
            second = (fits[j] >= FITS_LAYER).astype(F32)
            target = jnp.where(second > 0.5, layers[1], layers[0]).astype(BF16)
            weights.append(
                dot(
                    jnp.concatenate(split3(inv[j]), axis=1),
                    jnp.concatenate([target] * 3, axis=0),
                )
            )
        for j, weight in zip(slots, weights):
            high, low = split(weight)
            probs = held[j]
            found = dot(
                jnp.concatenate([probs, probs], axis=1), jnp.concatenate([high, low], axis=0)
            )
            taken = (fits[j] >= 0).astype(F32)
            result[j] = jnp.where(taken > 0.5, found, 0.0).astype(BF16)
            copy_out(j).start()

    @pl.when(more)
    def _():
        fill((0, 1, 2))

    @pl.when(jnp.logical_not(more))
    def _():
        clear(1)
        clear(2)

        @pl.when(fits[0] >= 0)
        def _():
            fill((0,))

        @pl.when(fits[0] < 0)
        def _():
            clear(0)

    for j in range(SLOTS):
        copy_out(j).wait()


def fitted_values(info, inverse, probs, target):
    anywhere = pl.BlockSpec(memory_space=pltpu.HBM)
    count = inverse.shape[1]
    return pl.pallas_call(
        values_kernel,
        out_shape=pltpu.HBM((1, SLOTS, CMAX, HD), BF16),
        in_specs=[SMEM, VMEM, anywhere, anywhere],
        out_specs=pl.BlockSpec(memory_space=pltpu.HBM),
        scratch_shapes=[
            pltpu.VMEM((SLOTS, count, count), F32),
            pltpu.VMEM((SLOTS, CMAX, count), BF16),
            pltpu.VMEM((SLOTS, CMAX, HD), BF16),
            pltpu.SemaphoreType.DMA((3, SLOTS)),
        ],
        compiler_params=room(16),
        cost_estimate=cost(10**9, 4 * 10**6),
        name="fitted_values",
    )(
        info,
        target,
        pltpu.with_memory_space_constraint(inverse, pltpu.HBM),
        pltpu.with_memory_space_constraint(probs, pltpu.HBM),
    )


def exchange(blocks):
    return lax.all_to_all(blocks, SEQ, split_axis=0, concat_axis=0, tiled=True)


def gathered_keys(owners, indices, keys):
    layers, local, width = keys.shape
    shards = lax.axis_size(SEQ)
    me = lax.axis_index(SEQ)
    fits = indices.shape[0]
    fit_ids = jnp.arange(fits, dtype=jnp.int32)
    offset = indices - me * local
    inside = (offset >= 0) & (offset < local)
    source = (fit_ids // FITS_LAYER)[:, None] * local + jnp.clip(offset, 0, local - 1)
    picked = jnp.take(keys.reshape(layers * local, width), source, axis=0)
    found = jnp.where(inside[..., None], picked, jnp.zeros((), picked.dtype))
    ring = [(k, (k + 1) % shards) for k in range(shards)]

    def pass_on(_, carried):
        moving, whole = carried
        moving = lax.ppermute(moving, SEQ, ring)
        return moving, whole + moving

    _, everything = lax.fori_loop(0, shards - 1, pass_on, (found, found))
    mine = owners[0] == me
    earlier = jnp.sum(
        jnp.where(mine[None, :] & (fit_ids[:, None] > fit_ids[None, :]), 1, 0), axis=1
    )
    chosen = [
        everything[jnp.sum(jnp.where(mine & (earlier == slot), fit_ids, 0))]
        for slot in range(SLOTS)
    ]
    return jnp.swapaxes(jnp.stack(chosen), 1, 2)


def on_device(queries, keys, values, indices, sizes, owners):
    layers, _, local, width = keys.shape
    key_rows = keys.reshape(layers, local, width)
    value_rows = values.reshape(layers, local, width)
    positions = indices[0]
    shards = lax.axis_size(SEQ)
    regrouped = lax.all_to_all(queries, "head", split_axis=1, concat_axis=2, tiled=True)
    own_rows = regrouped.reshape(1, 16, width)
    packed, info = pack_keys(owners, sizes, positions, key_rows, shards)
    packed = lax.dynamic_update_slice(
        packed, jnp.broadcast_to(own_rows, (shards, 16, width)), (0, ROOM, 0)
    )
    received = exchange(packed)
    spare = lax.cond(
        info[OVER] > 0,
        lambda: gathered_keys(owners, positions, key_rows),
        lambda: jnp.zeros((SLOTS, width, CMAX), BF16),
    )
    dest, owned = plan(info, positions, spare, shards, local.bit_length() - 1)
    own_block = turned(received, dest)
    near, back, far = (
        lax.ppermute(own_block, "seq_1", [(k, (k + d) % PARTS) for k in range(PARTS)])
        for d in (1, PARTS - 1, PARTS // 2)
    )
    attended = attend(received, key_rows, value_rows)
    parts = exchange(attended)
    ordering = ordered(0, owned, dest, own_block, attended)
    ordering = ordered(1, owned, dest, near, ordering)
    probs, system, ends = systems(owned, dest, received, back, far, ordering, spare)
    target = exchange(join(parts, system))
    inverse = invert(owned, system, ends)
    return fitted_values(owned, inverse, probs, target)


def solution(mesh):
    apart = Mesh(mesh.devices.reshape(mesh.shape["head"], 8, 4), ("head", "seq_0", "seq_1"))
    placed = (
        P(None, None, HEAD_SEQ, None),
        P(None, "head", SEQ, None),
        P(None, "head", SEQ, None),
        P("head", None, None),
        P("head", None),
        P("head", None),
    )
    return jax.shard_map(
        on_device,
        mesh=apart,
        in_specs=placed,
        out_specs=P("head", SEQ, None, None),
        check_vma=False,
    )
```

```python
import functools

import jax
import jax.numpy as jnp
from jax import lax
from jax.experimental import pallas as pl
from jax.experimental.pallas import tpu as pltpu
from jax.sharding import Mesh
from jax.sharding import PartitionSpec as P

FITS = 8
FITS_LAYER = 4
SLOTS = 3
CMAX = 1024
HD = 128
LANES = 128
ROOM = 48
ROWS = ROOM + 16
PARTS = 4
CLOSE = 0.97
STIFF = 0.004
BOUND = 1.001
RIDGE = 0.3
DEALT = (0, 1, 3, 2)
OVER, ME, OWNERS, SIZES, INFO = 0, 1, 2, 10, 32
SLOT_FIT, SLOT_SIZE, USED = 1, 4, 8
SCALE = HD ** (-0.5)
SEQ = ("seq_0", "seq_1")
HEAD_SEQ = ("head", "seq_0", "seq_1")
F32 = jnp.float32
BF16 = jnp.bfloat16


def room(mib):
    return pltpu.CompilerParams(vmem_limit_bytes=mib << 20)


SMEM = pl.BlockSpec(memory_space=pltpu.SMEM)
VMEM = pl.BlockSpec(memory_space=pltpu.VMEM)


def cost(flops, moved, exps=0):
    return pl.CostEstimate(flops=flops, transcendentals=exps, bytes_accessed=moved)


def iota(shape, dim):
    return lax.broadcasted_iota(jnp.int32, shape, dim)


def fiota(shape, dim):
    return iota(shape, dim).astype(F32)


def dot(a, b, dims=((1,), (0,))):
    return lax.dot_general(a, b, (dims, ((), ())), preferred_element_type=F32)


def running(mask):
    rows, width = mask.shape
    blocks = width // LANES
    upper = (iota((LANES, LANES), 0) <= iota((LANES, LANES), 1)).astype(BF16)
    stacked = jnp.concatenate(
        [mask[:, b * LANES : (b + 1) * LANES] for b in range(blocks)], axis=0
    )
    inner = dot(stacked.astype(BF16), upper)
    carry = jnp.zeros((rows, 1), F32)
    parts = []
    for b in range(blocks):
        part = inner[b * rows : (b + 1) * rows]
        parts.append(part + carry)
        carry = carry + part[:, LANES - 1 : LANES]
    return jnp.concatenate(parts, axis=1), carry


def heaviest(owner_of):
    owners = [owner_of(f) for f in range(FITS)]
    number = [sum((a == b).astype(jnp.int32) for b in owners) for a in owners]
    places = []
    for f in range(FITS):
        best, place = jnp.int32(0), jnp.int32(0)
        for g in range(FITS):
            better = (owners[g] // PARTS == owners[f] // PARTS) & (number[g] > best)
            best = jnp.where(better, number[g], best)
            place = jnp.where(better, owners[g] & (PARTS - 1), place)
        places.append(place)
    return places


def send_kernel(
    shards, own_hbm, size_hbm, idx_ref, keys_ref, send_ref, info_ref, own_ref, size_ref, sems
):
    copies = [
        pltpu.make_async_copy(own_hbm, own_ref, sems.at[0]),
        pltpu.make_async_copy(size_hbm, size_ref, sems.at[1]),
    ]
    for copy in copies:
        copy.start()
    send_ref[...] = jnp.zeros(send_ref.shape, BF16)
    for copy in copies:
        copy.wait()
    me = lax.axis_index(SEQ).astype(jnp.int32)
    local = keys_ref.shape[1]
    shift = local.bit_length() - 1
    fits, width = idx_ref.shape
    idx = idx_ref[...]
    row = iota((fits, width), 0)
    lane = iota((fits, width), 1)
    size = jnp.zeros((fits, width), jnp.int32)
    own = jnp.zeros((fits, LANES), jnp.int32)
    row1 = iota((fits, LANES), 0)
    lane1 = iota((fits, LANES), 1)
    for f in range(fits):
        size = jnp.where(row == f, size_ref[0, f], size)
        own = jnp.where(row1 == f, own_ref[0, f] // PARTS, own)
    shard = jnp.where(lane < size, lax.shift_right_logical(idx, shift), -1)
    counts = jnp.zeros((fits, LANES), F32)
    for s in range(shards):
        count = jnp.sum(jnp.where(shard == s, 1.0, 0.0), axis=1, keepdims=True)
        counts = jnp.where(lane1 == s, count, counts)
    total = jnp.zeros((fits, LANES), F32)
    before = jnp.zeros((fits, LANES), F32)
    for f in range(fits):
        shared = jnp.where(own == own_ref[0, f] // PARTS, counts[f : f + 1, :], 0.0)
        total = total + shared
        before = before + jnp.where(row1 > f, shared, 0.0)
    info_ref[OVER] = (jnp.max(total) > PARTS * ROOM).astype(jnp.int32)
    info_ref[ME] = me
    for f in range(fits):
        info_ref[OWNERS + f] = own_ref[0, f]
        info_ref[SIZES + f] = size_ref[0, f]
    first = jnp.sum(jnp.where(lane1 == me, before, 0.0), axis=1, keepdims=True)
    mine = shard == me
    held = jnp.where(mine, 1.0, 0.0)
    place, _ = running(held)
    place = jnp.where(mine, place - 1.0 + first, -1.0)
    spot = jnp.where(mine, idx - me * local + 1, 0).astype(F32)
    slot = fiota((PARTS * ROOM, width), 0)
    at = fiota((PARTS * ROOM, local), 1)
    middle = heaviest(lambda f: own_ref[0, f])
    taken = PARTS * ROOM
    for begin in range(0, fits, FITS_LAYER):
        picks = []
        for f in range(begin, begin + FITS_LAYER):
            here = place[f : f + 1, :] == slot
            pos = jnp.sum(jnp.where(here, spot[f : f + 1, :], 0.0), axis=1, keepdims=True) - 1.0
            picks.append(jnp.where(pos == at, 1.0, 0.0).astype(BF16))
        rows = dot(jnp.concatenate(picks, axis=0), keys_ref[begin // FITS_LAYER]).astype(BF16)
        for i, f in enumerate(range(begin, begin + FITS_LAYER)):
            to = own_ref[0, f] // PARTS * PARTS
            for part, step in enumerate(DEALT):
                place_along = (middle[f] + step) & (PARTS - 1)
                first = i * taken + part * ROOM
                send_ref[to + place_along, 0:ROOM, :] += rows[first : first + ROOM]


def pack_keys(owners, sizes, indices, keys, shards):
    return pl.pallas_call(
        lambda *refs: send_kernel(shards, *refs),
        out_shape=(
            jax.ShapeDtypeStruct((shards, ROWS, LANES), BF16),
            jax.ShapeDtypeStruct((INFO,), jnp.int32),
        ),
        in_specs=[pl.BlockSpec(memory_space=pltpu.HBM)] * 2 + [VMEM, VMEM],
        out_specs=(VMEM, SMEM),
        scratch_shapes=[
            pltpu.SMEM((1, FITS), jnp.int32),
            pltpu.SMEM((1, FITS), jnp.int32),
            pltpu.SemaphoreType.DMA((2,)),
        ],
        compiler_params=room(24),
        cost_estimate=cost(10**9, 3 * 10**6),
        name="pack_keys",
    )(
        pltpu.with_memory_space_constraint(owners, pltpu.HBM),
        pltpu.with_memory_space_constraint(sizes, pltpu.HBM),
        indices,
        keys,
    )


def slots_of(me, info_ref):
    found = [jnp.int32(-1)] * SLOTS
    seen = jnp.int32(0)
    for f in range(FITS):
        match = info_ref[OWNERS + f] == me
        for j in range(SLOTS):
            found[j] = jnp.where(match & (seen == j), f, found[j])
        seen = seen + match.astype(jnp.int32)
    return found


def layer_rows(rows, layer):
    wide = rows.astype(F32)[:, 8 * layer : 8 * layer + 8, :]
    return wide.reshape(-1, wide.shape[-1])


def attend_kernel(recv_ref, keys_ref, values_ref, out_ref):
    shards = recv_ref.shape[0]
    outs = []
    stat = jnp.zeros((shards * 8, LANES), F32)
    lane = iota(stat.shape, 1)
    for layer in range(2):
        query = layer_rows(recv_ref[...], layer).astype(BF16)
        scores = dot(query, keys_ref[layer], ((1,), (1,))) * SCALE
        peak = jnp.max(scores, axis=1, keepdims=True)
        weights = jnp.exp(scores - peak)
        total = jnp.sum(weights, axis=1, keepdims=True)
        numer = dot(weights.astype(BF16), values_ref[layer])
        outs.append((numer / total).reshape(shards, 8, HD))
        level = peak + jnp.log(total)
        high = level.astype(BF16).astype(F32)
        middle = (level - high).astype(BF16).astype(F32)
        for k, piece in enumerate((high, middle, level - high - middle)):
            stat = jnp.where(lane == 64 * layer + k, piece, stat)
    out_ref[:, 0:16, :] = jnp.concatenate(outs, axis=1).astype(BF16)
    out_ref[:, 16:24, :] = stat.reshape(shards, 8, LANES).astype(BF16)


def attend(received, keys, values):
    shards = received.shape[0]
    return pl.pallas_call(
        attend_kernel,
        out_shape=jax.ShapeDtypeStruct((shards, 24, LANES), BF16),
        grid=(1,),
        in_specs=[
            pl.BlockSpec((shards, 16, LANES), lambda i: (0, ROOM // 16, 0)),
            pl.BlockSpec(keys.shape, lambda i: (0, 0, 0)),
            pl.BlockSpec(values.shape, lambda i: (0, 0, 0)),
        ],
        out_specs=pl.BlockSpec((shards, 24, LANES), lambda i: (0, 0, 0)),
        compiler_params=room(24),
        cost_estimate=cost(5 * 10**8, 3 * 10**6, 10**6),
        name="attend",
    )(received, keys, values)


def join_kernel(parts_ref, after_ref, out_ref):
    parts = parts_ref[...].astype(F32)
    stat = parts[:, 16:24, :]
    first = iota(stat.shape, 2) < 64
    level = jnp.concatenate(
        [
            jnp.sum(jnp.where(first, stat, 0.0), axis=2, keepdims=True),
            jnp.sum(jnp.where(first, 0.0, stat), axis=2, keepdims=True),
        ],
        axis=1,
    )
    weights = jnp.exp(level - jnp.max(level, axis=0, keepdims=True))
    numer = jnp.sum(weights * parts[:, 0:16, :], axis=0, keepdims=True)
    target = numer / jnp.sum(weights, axis=0, keepdims=True)
    out_ref[...] = jnp.broadcast_to(target, out_ref.shape).astype(BF16)


def join(parts, after):
    shards = parts.shape[0]
    return pl.pallas_call(
        join_kernel,
        out_shape=jax.ShapeDtypeStruct((shards, 16, LANES), BF16),
        in_specs=[VMEM, pl.BlockSpec(memory_space=pl.ANY)],
        out_specs=VMEM,
        compiler_params=room(8),
        cost_estimate=cost(10**6, 4 * 10**5, 10**3),
        name="join_parts",
    )(parts, after)


def turn_kernel(recv_ref, after_ref, out_ref):
    rows = recv_ref[:, 0:ROOM, :]
    out_ref[...] = rows.reshape(-1, HD).astype(F32).T.astype(BF16)


def turned(received, after):
    return pl.pallas_call(
        turn_kernel,
        out_shape=jax.ShapeDtypeStruct((HD, received.shape[0] * ROOM), BF16),
        in_specs=[VMEM, pl.BlockSpec(memory_space=pl.ANY)],
        out_specs=VMEM,
        compiler_params=room(8),
        cost_estimate=cost(10**6, 10**6),
        name="turn_keys",
    )(received, after)


def plan_kernel(shift, shards, info_ref, idx_ref, after_ref, dest_ref, out_ref):
    width = idx_ref.shape[1]
    me = info_ref[ME]
    fits = slots_of(me, info_ref)
    lane = iota((1, width), 1)
    source = iota((shards, width), 0)

    def shards_of(fit, size):
        place = lax.shift_right_logical(idx_ref[pl.ds(fit, 1), :], shift)
        return jnp.where(lane < size, place, -1)

    middle = heaviest(lambda f: info_ref[OWNERS + f])
    counts = []
    for f in range(FITS):
        shard = shards_of(f, info_ref[SIZES + f])
        counts.append(jnp.sum(jnp.where(shard == source, 1.0, 0.0), axis=1, keepdims=True))
    dest_ref[...] = jnp.full(dest_ref.shape, -1, jnp.int32)
    out_ref[OVER] = info_ref[OVER]
    for j in range(SLOTS):
        fit = jnp.maximum(fits[j], 0)
        size = info_ref[SIZES + fit]
        out_ref[SLOT_FIT + j] = fits[j]
        out_ref[SLOT_SIZE + j] = size
        shard = shards_of(fit, jnp.where(fits[j] >= 0, size, 0))
        first = jnp.zeros((shards, 1), F32)
        for f in range(FITS):
            ahead = (f < fit) & (info_ref[OWNERS + f] // PARTS == me // PARTS)
            first = first + counts[f] * ahead.astype(F32)
        held = jnp.where(shard == source, 1.0, 0.0)
        place, _ = running(held)
        rank = jnp.sum(held * (place - 1.0 + first), axis=0, keepdims=True).astype(jnp.int32)
        part = sum((rank >= k * ROOM).astype(jnp.int32) for k in range(1, PARTS))
        center = sum(jnp.where(fit == f, middle[f], 0) for f in range(FITS))
        step = jnp.full(part.shape, DEALT[0], jnp.int32)
        for k in range(1, PARTS):
            step = jnp.where(part == k, DEALT[k], step)
        turn = (me - center - step) & (PARTS - 1)
        dest = shard * ROOM + rank - part * ROOM + turn * (shards * ROOM)
        dest_ref[j : j + 1, :] = jnp.where(shard >= 0, dest, -1)
        for b in range(PARTS):
            here = jnp.where((shard >= 0) & (turn == b), 1, 0)
            out_ref[USED + j * PARTS + b] = jnp.max(here)


def plan(info, indices, after, shards, shift):
    return pl.pallas_call(
        lambda *refs: plan_kernel(shift, shards, *refs),
        out_shape=(
            jax.ShapeDtypeStruct(indices.shape, jnp.int32),
            jax.ShapeDtypeStruct((INFO,), jnp.int32),
        ),
        in_specs=[SMEM, VMEM, pl.BlockSpec(memory_space=pl.ANY)],
        out_specs=(VMEM, SMEM),
        compiler_params=room(8),
        cost_estimate=cost(10**10, 10**6),
        name="plan",
    )(info, indices, after)


def any_of(slots, info_ref):
    return functools.reduce(jnp.maximum, [info_ref[SLOT_FIT + j] for j in slots]) >= 0


def add_found(slots, turns, blocks, info_ref, dest_ref, total_ref):
    span = 256
    width = dest_ref.shape[1]
    columns = slice(slots[0] * width, (slots[-1] + 1) * width)
    dest = jnp.concatenate([dest_ref[j : j + 1, :] for j in slots], axis=1)
    block = lax.shift_right_arithmetic(dest, 8)
    offset = dest & (span - 1)
    for b, block_ref in zip(turns, blocks):
        used = sum(info_ref[USED + j * PARTS + b] for j in slots)

        @pl.when(used > 0)
        def _():
            pick = jnp.where(offset == iota((span, offset.shape[1]), 0), 1.0, 0.0).astype(BF16)
            pieces = block_ref.shape[1] // span
            stacked = jnp.concatenate(
                [block_ref[:, n * span : (n + 1) * span] for n in range(pieces)], axis=0
            )
            found = dot(stacked, pick)
            total = total_ref[:, columns]
            for n in range(pieces):
                total = jnp.where(block == b * pieces + n, found[n * HD : (n + 1) * HD], total)
            total_ref[:, columns] = total


def order_kernel(turn, info_ref, dest_ref, block_ref, *refs):
    out_ref, total_ref = refs[-2:]
    if turn == 0:
        total_ref[...] = jnp.zeros(total_ref.shape, F32)
    else:
        total_ref[...] = refs[0][...].astype(F32)
    for j in range(SLOTS):
        add_found((j,), (turn,), (block_ref,), info_ref, dest_ref, total_ref)
    out_ref[...] = total_ref[...].astype(BF16)


def ordered(turn, info, dest, block, before):
    anywhere = pl.BlockSpec(memory_space=pl.ANY)
    return pl.pallas_call(
        lambda *refs: order_kernel(turn, *refs),
        out_shape=jax.ShapeDtypeStruct((HD, SLOTS * CMAX), BF16),
        in_specs=[SMEM, VMEM, VMEM, VMEM if turn else anywhere],
        out_specs=VMEM,
        scratch_shapes=[pltpu.VMEM((HD, SLOTS * CMAX), F32)],
        compiler_params=room(16),
        cost_estimate=cost(2 * 10**9, 3 * 10**6),
        name="order_%d" % turn,
    )(info, dest, block, before)


def build_systems(slots, info_ref, recv_ref, keys_ref):
    count = recv_ref.shape[0] * 8
    width = CMAX
    eye = iota((count, count), 0) == iota((count, count), 1)
    lane = iota((1, width), 1)
    results = []
    rows = recv_ref[:, ROOM:ROWS, :]
    layers = layer_rows(rows, 0), layer_rows(rows, 1)
    for j in slots:
        live = info_ref[SLOT_FIT + j] >= 0
        size = info_ref[SLOT_SIZE + j]
        second = (info_ref[SLOT_FIT + j] >= FITS_LAYER).astype(F32)
        query = jnp.where(second > 0.5, layers[1], layers[0]).astype(BF16)
        scores = dot(query, keys_ref[:, j * width : (j + 1) * width]) * SCALE
        scores = jnp.where(lane < size, scores, -jnp.inf)
        expo = jnp.exp(scores - jnp.max(scores, axis=1, keepdims=True))
        probs = (expo / jnp.sum(expo, axis=1, keepdims=True)).astype(BF16)
        turned_probs = probs.astype(F32).T.astype(BF16)
        gram = dot(probs, turned_probs)
        trace = jnp.sum(jnp.where(eye, gram, 0.0))
        ridge = RIDGE * trace / size.astype(F32)
        sums = jnp.sum(gram, axis=0, keepdims=True)
        ratios = jnp.sum(gram * sums, axis=1, keepdims=True) / jnp.sum(gram, axis=1, keepdims=True)
        top = jnp.minimum(BOUND * jnp.max(ratios), trace) + ridge
        taken = live.astype(F32)
        system = jnp.where(taken > 0.5, gram, 0.0) + jnp.where(
            eye, jnp.where(live, ridge, 1.0), 0.0
        )
        ends = jnp.where(live, ridge, 1.0), jnp.where(live, top, 1.0)
        results.append((system, turned_probs, ends))
    return results


def system_kernel(
    info_ref, dest_ref, recv_ref, back_ref, far_ref, part_ref, spare_ref, probs_ref, sys_ref, ends_ref,
    keys_ref, total_ref, held_ref, sems
):
    count = sys_ref.shape[1]
    width = dest_ref.shape[1]
    eye = iota((count, count), 0) == iota((count, count), 1)
    turns = PARTS - 1, PARTS // 2
    late = sum(info_ref[USED + j * PARTS + turn] for j in range(SLOTS) for turn in turns)
    keys_ref[...] = part_ref[...]

    @pl.when((info_ref[OVER] == 0) & (late > 0))
    def _():
        total_ref[...] = part_ref[...].astype(F32)
        for j in range(SLOTS):
            add_found((j,), turns, (back_ref, far_ref), info_ref, dest_ref, total_ref)
        keys_ref[...] = total_ref[...].astype(BF16)

    @pl.when(info_ref[OVER] > 0)
    def _():
        for j in range(SLOTS):
            pltpu.sync_copy(spare_ref.at[j], keys_ref.at[:, pl.ds(j * width, width)])

    def copy(j):
        return pltpu.make_async_copy(held_ref.at[j], probs_ref.at[j], sems.at[j])

    def fill(slots):
        live = any_of(slots, info_ref)

        @pl.when(live)
        def _():
            found = build_systems(slots, info_ref, recv_ref, keys_ref)
            for j, (system, probs, ends) in zip(slots, found):
                held_ref[j] = probs
                copy(j).start()
                sys_ref[j] = system
                ends_ref[j] = jnp.where(iota((8, LANES), 0) == 0, ends[0], ends[1])

        @pl.when(jnp.logical_not(live))
        def _():
            for j in slots:
                sys_ref[j] = jnp.where(eye, 1.0, 0.0)
                ends_ref[j] = jnp.full((8, LANES), 1.0, F32)

    groups = (0,), (1, 2)
    for slots in groups:
        fill(slots)
    for slots in groups:

        @pl.when(any_of(slots, info_ref))
        def _():
            for j in slots:
                copy(j).wait()


def systems(info, dest, received, back, far, part, spare):
    count = received.shape[0] * 8
    return pl.pallas_call(
        system_kernel,
        out_shape=(
            pltpu.HBM((SLOTS, CMAX, count), BF16),
            jax.ShapeDtypeStruct((SLOTS, count, count), F32),
            jax.ShapeDtypeStruct((SLOTS, 8, LANES), F32),
        ),
        in_specs=[SMEM] + [VMEM] * 5 + [pl.BlockSpec(memory_space=pltpu.HBM)],
        out_specs=(pl.BlockSpec(memory_space=pltpu.HBM), VMEM, VMEM),
        scratch_shapes=[
            pltpu.VMEM((HD, SLOTS * CMAX), BF16),
            pltpu.VMEM((HD, SLOTS * CMAX), F32),
            pltpu.VMEM((SLOTS, CMAX, count), BF16),
            pltpu.SemaphoreType.DMA((SLOTS,)),
        ],
        compiler_params=room(32),
        cost_estimate=cost(3 * 10**9, 3 * 10**6, 10**6),
        name="systems",
    )(
        info,
        dest,
        received,
        back,
        far,
        part,
        pltpu.with_memory_space_constraint(spare, pltpu.HBM),
    )


def split(x):
    high = x.astype(BF16)
    return high, (x - high.astype(F32)).astype(BF16)


def split3(x):
    high, _ = split(x)
    rest = x - high.astype(F32)
    middle, low = split(rest)
    return high, middle, low


def product(a, b):
    (a_high, a_low), (b_high, b_low) = a, b
    return dot(
        jnp.concatenate([a_high, a_high, a_low], axis=1),
        jnp.concatenate([b_high, b_low, b_high], axis=0),
    )


def product_full(a, b):
    (a0, a1, a2), (b0, b1, b2) = split3(a), split3(b)
    return dot(
        jnp.concatenate([a0, a0, a1, a0, a1, a2], axis=1),
        jnp.concatenate([b0, b1, b0, b2, b1, b0], axis=0),
    )


def invert_kernel(info_ref, sys_ref, ends_ref, inverse_ref, parts_ref, out_ref, sems):
    count = sys_ref.shape[1]
    eye = iota((count, count), 0) == iota((count, count), 1)
    more = any_of((1, 2), info_ref)
    one = jnp.logical_not(more) & (info_ref[SLOT_FIT] >= 0)

    def copy(j):
        return pltpu.make_async_copy(out_ref.at[j], inverse_ref.at[j], sems.at[j])

    def start(slots):
        lows = []
        for j in slots:
            low = jnp.max(ends_ref[j, 0:1, :])
            high = jnp.max(ends_ref[j, 1:2, :])
            middle = 2.0 / (low + high)
            system = sys_ref[j]
            out_ref[j] = middle * (jnp.where(eye, 2.0, 0.0) - middle * system)
            parts_ref[j, 0], parts_ref[j, 1] = split(system)
            ratio = (high - low) / (high + low)
            lows.append(1.0 - ratio * ratio)
        return tuple(lows)

    def step(slots, lows, last=False, full=False):
        nexts = []
        for j, lowest in zip(slots, lows):
            held = out_ref[j]
            middle = 2.0 / (lowest + 1.0)
            parts = split(held)
            if full:
                images = product_full(sys_ref[j], held)
            else:
                images = product((parts_ref[j, 0], parts_ref[j, 1]), parts)
            rest = jnp.where(eye, 1.0, 0.0) - middle * images
            if last:
                moved = dot(parts[0], rest.astype(BF16))
            else:
                moved = product(parts, split(rest))
            out_ref[j] = middle * (held + moved)
            ratio = (1.0 - lowest) / (1.0 + lowest)
            nexts.append(1.0 - ratio * ratio)
        return tuple(nexts)

    def solve(slots):
        lows = start(slots)
        stiff = functools.reduce(jnp.minimum, lows) < STIFF
        lows = lax.while_loop(
            lambda lows: functools.reduce(jnp.minimum, lows) < CLOSE,
            functools.partial(step, slots),
            lows,
        )

        @pl.when(stiff)
        def _():
            step(slots, lows, full=True)

        @pl.when(jnp.logical_not(stiff))
        def _():
            step(slots, lows, last=True)

        for j in slots:
            copy(j).start()
        for j in slots:
            copy(j).wait()

    @pl.when(more)
    def _():
        solve((0, 1, 2))

    @pl.when(one)
    def _():
        solve((0,))


def invert(info, system, ends):
    return pl.pallas_call(
        invert_kernel,
        out_shape=pltpu.HBM(system.shape, F32),
        in_specs=[SMEM, VMEM, VMEM],
        out_specs=pl.BlockSpec(memory_space=pltpu.HBM),
        scratch_shapes=[
            pltpu.VMEM((SLOTS, 2, *system.shape[1:]), BF16),
            pltpu.VMEM(system.shape, F32),
            pltpu.SemaphoreType.DMA((SLOTS,)),
        ],
        compiler_params=room(16),
        cost_estimate=cost(5 * 10**9, 2 * 10**6),
        name="invert",
    )(info, system, ends)


def values_kernel(
    info_ref, target_ref, inverse_ref, probs_ref, out_ref, inv, held, result, sems
):
    fits = [info_ref[SLOT_FIT + j] for j in range(SLOTS)]
    more = any_of((1, 2), info_ref)

    def copies(j):
        return (
            pltpu.make_async_copy(inverse_ref.at[j], inv.at[j], sems.at[0, j]),
            pltpu.make_async_copy(probs_ref.at[j], held.at[j], sems.at[1, j]),
        )

    def copy_out(j):
        return pltpu.make_async_copy(result.at[j], out_ref.at[0, j], sems.at[2, j])

    def clear(j):
        result[j] = jnp.zeros(result.shape[1:], BF16)
        copy_out(j).start()

    def fill(slots):
        for j in slots:
            for copy in copies(j):
                copy.start()
        rows = target_ref[...]
        layers = layer_rows(rows, 0), layer_rows(rows, 1)
        for j in slots:
            for copy in copies(j):
                copy.wait()
        weights = []
        for j in slots:
            second = (fits[j] >= FITS_LAYER).astype(F32)
            target = jnp.where(second > 0.5, layers[1], layers[0]).astype(BF16)
            weights.append(
                dot(
                    jnp.concatenate(split3(inv[j]), axis=1),
                    jnp.concatenate([target] * 3, axis=0),
                )
            )
        for j, weight in zip(slots, weights):
            high, low = split(weight)
            probs = held[j]
            found = dot(
                jnp.concatenate([probs, probs], axis=1), jnp.concatenate([high, low], axis=0)
            )
            taken = (fits[j] >= 0).astype(F32)
            result[j] = jnp.where(taken > 0.5, found, 0.0).astype(BF16)
            copy_out(j).start()

    @pl.when(more)
    def _():
        fill((0, 1, 2))

    @pl.when(jnp.logical_not(more))
    def _():
        clear(1)
        clear(2)

        @pl.when(fits[0] >= 0)
        def _():
            fill((0,))

        @pl.when(fits[0] < 0)
        def _():
            clear(0)

    for j in range(SLOTS):
        copy_out(j).wait()


def fitted_values(info, inverse, probs, target):
    anywhere = pl.BlockSpec(memory_space=pltpu.HBM)
    count = inverse.shape[1]
    return pl.pallas_call(
        values_kernel,
        out_shape=pltpu.HBM((1, SLOTS, CMAX, HD), BF16),
        in_specs=[SMEM, VMEM, anywhere, anywhere],
        out_specs=pl.BlockSpec(memory_space=pltpu.HBM),
        scratch_shapes=[
            pltpu.VMEM((SLOTS, count, count), F32),
            pltpu.VMEM((SLOTS, CMAX, count), BF16),
            pltpu.VMEM((SLOTS, CMAX, HD), BF16),
            pltpu.SemaphoreType.DMA((3, SLOTS)),
        ],
        compiler_params=room(16),
        cost_estimate=cost(10**9, 4 * 10**6),
        name="fitted_values",
    )(
        info,
        target,
        pltpu.with_memory_space_constraint(inverse, pltpu.HBM),
        pltpu.with_memory_space_constraint(probs, pltpu.HBM),
    )


def exchange(blocks):
    return lax.all_to_all(blocks, SEQ, split_axis=0, concat_axis=0, tiled=True)


def gathered_keys(owners, indices, keys):
    layers, local, width = keys.shape
    shards = lax.axis_size(SEQ)
    me = lax.axis_index(SEQ)
    fits = indices.shape[0]
    fit_ids = jnp.arange(fits, dtype=jnp.int32)
    offset = indices - me * local
    inside = (offset >= 0) & (offset < local)
    source = (fit_ids // FITS_LAYER)[:, None] * local + jnp.clip(offset, 0, local - 1)
    picked = jnp.take(keys.reshape(layers * local, width), source, axis=0)
    found = jnp.where(inside[..., None], picked, jnp.zeros((), picked.dtype))
    ring = [(k, (k + 1) % shards) for k in range(shards)]

    def pass_on(_, carried):
        moving, whole = carried
        moving = lax.ppermute(moving, SEQ, ring)
        return moving, whole + moving

    _, everything = lax.fori_loop(0, shards - 1, pass_on, (found, found))
    mine = owners[0] == me
    earlier = jnp.sum(
        jnp.where(mine[None, :] & (fit_ids[:, None] > fit_ids[None, :]), 1, 0), axis=1
    )
    chosen = [
        everything[jnp.sum(jnp.where(mine & (earlier == slot), fit_ids, 0))]
        for slot in range(SLOTS)
    ]
    return jnp.swapaxes(jnp.stack(chosen), 1, 2)


def on_device(queries, keys, values, indices, sizes, owners):
    layers, _, local, width = keys.shape
    key_rows = keys.reshape(layers, local, width)
    value_rows = values.reshape(layers, local, width)
    positions = indices[0]
    shards = lax.axis_size(SEQ)
    regrouped = lax.all_to_all(queries, "head", split_axis=1, concat_axis=2, tiled=True)
    own_rows = regrouped.reshape(1, 16, width)
    packed, info = pack_keys(owners, sizes, positions, key_rows, shards)
    packed = lax.dynamic_update_slice(
        packed, jnp.broadcast_to(own_rows, (shards, 16, width)), (0, ROOM, 0)
    )
    received = exchange(packed)
    spare = lax.cond(
        info[OVER] > 0,
        lambda: gathered_keys(owners, positions, key_rows),
        lambda: jnp.zeros((SLOTS, width, CMAX), BF16),
    )
    dest, owned = plan(info, positions, spare, shards, local.bit_length() - 1)
    own_block = turned(received, dest)
    near, back, far = (
        lax.ppermute(own_block, "seq_1", [(k, (k + d) % PARTS) for k in range(PARTS)])
        for d in (1, PARTS - 1, PARTS // 2)
    )
    attended = attend(received, key_rows, value_rows)
    parts = exchange(attended)
    ordering = ordered(0, owned, dest, own_block, attended)
    ordering = ordered(1, owned, dest, near, ordering)
    probs, system, ends = systems(owned, dest, received, back, far, ordering, spare)
    target = exchange(join(parts, system))
    inverse = invert(owned, system, ends)
    return fitted_values(owned, inverse, probs, target)


def solution(mesh):
    apart = Mesh(mesh.devices.reshape(mesh.shape["head"], 8, 4), ("head", "seq_0", "seq_1"))
    placed = (
        P(None, None, HEAD_SEQ, None),
        P(None, "head", SEQ, None),
        P(None, "head", SEQ, None),
        P("head", None, None),
        P("head", None),
        P("head", None),
    )
    return jax.shard_map(
        on_device,
        mesh=apart,
        in_specs=placed,
        out_specs=P("head", SEQ, None, None),
        check_vma=False,
    )
```
